32 devices in a mesh: fsdp: 4 (over y, core), tensor: 8 (over z, x).
Axes of the slice: x: 2, y: 2, z: 4, core: 2. Of those that a mesh axis runs over, the one named last changes fastest.
Arguments:
- layer_input: bfloat16 [8, 1024, 1024], P('fsdp', 'tensor'), may hold values from -7 to 7
- cotangent: bfloat16 [8, 1024, 1024], P('fsdp', 'tensor'), may hold values from -6 to 6
- attn_weight: float32 [1024, 3072], P('fsdp', 'tensor'), may hold values from -0.1875 to 0.1875
- attn_bias: float32 [16, 192], P('tensor', 'fsdp'), may hold values from -3 to 3
- out_weight: float32 [1024, 1024], P('tensor', 'fsdp'), may hold values from -3 to 3
- up_weight: float32 [1024, 4096], P('fsdp', 'tensor'), may hold values from -0.1875 to 0.1875
- up_bias: float32 [4096], P(('tensor', 'fsdp')), may hold values from -3 to 3
- down_weight: float32 [4096, 1024], P('tensor', 'fsdp'), may hold values from -0.09375 to 0.09375
- norm_gains: float32 [2, 1024], P(None, 'fsdp'), may hold values from 0.25 to 1.75
- norm_shifts: float32 [4, 1024], P(None, 'fsdp'), may hold values from -2 to 2
- attn_weight_moments: float32 [2, 1024, 3072], P(None, 'fsdp', 'tensor'), may hold values from -18.101934 to 18.101934, as said below
- attn_bias_moments: float32 [2, 16, 192], P(None, 'tensor', 'fsdp'), may hold values from -18.101934 to 18.101934, as said below
- out_weight_moments: float32 [2, 1024, 1024], P(None, 'tensor', 'fsdp'), may hold values from -18.101934 to 18.101934, as said below
- up_weight_moments: float32 [2, 1024, 4096], P(None, 'fsdp', 'tensor'), may hold values from -18.101934 to 18.101934, as said below
- up_bias_moments: float32 [2, 4096], P(None, ('tensor', 'fsdp')), may hold values from -18.101934 to 18.101934, as said below
- down_weight_moments: float32 [2, 4096, 1024], P(None, 'tensor', 'fsdp'), may hold values from -18.101934 to 18.101934, as said below
- norm_gains_moments: float32 [2, 2, 1024], P(None, None, 'fsdp'), may hold values from -18.101934 to 18.101934, as said below
- norm_shifts_moments: float32 [2, 4, 1024], P(None, None, 'fsdp'), may hold values from -18.101934 to 18.101934, as said below
Outputs:
- layer_output: bfloat16 [8, 1024, 1024], P('fsdp', 'tensor')
- input_grad: float32 [8, 1024, 1024], P('fsdp', 'tensor')
- grad_attn_weight: float32 [1024, 3072], P('fsdp', 'tensor')
- grad_attn_bias: float32 [16, 192], P('tensor', 'fsdp')
- grad_out_weight: float32 [1024, 1024], P('tensor', 'fsdp')
- grad_up_weight: float32 [1024, 4096], P('fsdp', 'tensor')
- grad_up_bias: float32 [4096], P(('tensor', 'fsdp'))
- grad_down_weight: float32 [4096, 1024], P('tensor', 'fsdp')
- grad_norm_gains: float32 [2, 1024], P(None, 'fsdp')
- grad_norm_shifts: float32 [4, 1024], P(None, 'fsdp')
- new_attn_weight: float32 [1024, 3072], P('fsdp', 'tensor')
- new_attn_bias: float32 [16, 192], P('tensor', 'fsdp')
- new_out_weight: float32 [1024, 1024], P('tensor', 'fsdp')
- new_up_weight: float32 [1024, 4096], P('fsdp', 'tensor')
- new_up_bias: float32 [4096], P(('tensor', 'fsdp'))
- new_down_weight: float32 [4096, 1024], P('tensor', 'fsdp')
- new_norm_gains: float32 [2, 1024], P(None, 'fsdp')
- new_norm_shifts: float32 [4, 1024], P(None, 'fsdp')
- new_attn_weight_moments: float32 [2, 1024, 3072], P(None, 'fsdp', 'tensor')
- new_attn_bias_moments: float32 [2, 16, 192], P(None, 'tensor', 'fsdp')
- new_out_weight_moments: float32 [2, 1024, 1024], P(None, 'tensor', 'fsdp')
- new_up_weight_moments: float32 [2, 1024, 4096], P(None, 'fsdp', 'tensor')
- new_up_bias_moments: float32 [2, 4096], P(None, ('tensor', 'fsdp'))
- new_down_weight_moments: float32 [2, 4096, 1024], P(None, 'tensor', 'fsdp')
- new_norm_gains_moments: float32 [2, 2, 1024], P(None, None, 'fsdp')
- new_norm_shifts_moments: float32 [2, 4, 1024], P(None, None, 'fsdp')
The draws below stay inside these ranges and needn't reach their ends.
Inputs may be any that keep to these rules, and one draw needn't show every extreme that they name: `attn_weight_moments`: index 0 of the first dimension holds first moments, index 1 positive second moments. `attn_bias_moments`: index 0 of the first dimension holds first moments, index 1 positive second moments. `out_weight_moments`: index 0 of the first dimension holds first moments, index 1 positive second moments. `up_weight_moments`: index 0 of the first dimension holds first moments, index 1 positive second moments. `up_bias_moments`: index 0 of the first dimension holds first moments, index 1 positive second moments. `down_weight_moments`: index 0 of the first dimension holds first moments, index 1 positive second moments. `norm_gains_moments`: index 0 of the first dimension holds first moments, index 1 positive second moments. `norm_shifts_moments`: index 0 of the first dimension holds first moments, index 1 positive second moments.
All inputs are finite; a program needn't handle non-finite values.
Results may differ from the reference program's by a relative error of at most 0.012.
The reference program's roundings to bfloat16 on the way count: a program that leaves them out, or rounds other values in their place, can miss the bound.
Values may be sent and summed in bfloat16 or wider, within the bound.
No kernel may reach another device: no remote copies, remote signals or barrier semaphores. Data moves between devices by JAX's collectives and lax.ppermute only.
A program may use at most 128 MiB of HBM per device.

```python
import jax
import jax.numpy as jnp
from jax import lax

D = 1024
HEADS = 16
HEAD_DIM = 64
FF = 4096
SEQ = 1024
SEQS = 8
TOKENS = 8192


def draw_layer_input(key, part):
    first_key = jax.random.fold_in(key, 0)
    return jnp.clip(jax.random.normal(first_key, (SEQS, SEQ, D), jnp.float32), -6.0, 6.0).astype(jnp.bfloat16)


def moment_pair(key, shape, label):
    first_key, second_key = jax.random.split(jax.random.fold_in(key, label))
    mean_part = 0.05 * TOKENS ** 0.5 * jnp.clip(jax.random.normal(first_key, shape, jnp.float32), -4.0, 4.0)
    square_part = 2e-05 * TOKENS * jnp.exp(jax.random.uniform(second_key, shape, jnp.float32, 0.0, 3.2188))
    return jnp.stack([mean_part, square_part])


def draw_attn_weight_moments(key, part):
    return moment_pair(key, (D, 3 * D), 101)


def draw_attn_bias_moments(key, part):
    return moment_pair(key, (HEADS, 3 * HEAD_DIM), 202)


def draw_out_weight_moments(key, part):
    return moment_pair(key, (D, D), 303)


def draw_up_weight_moments(key, part):
    return moment_pair(key, (D, FF), 404)


def draw_up_bias_moments(key, part):
    return moment_pair(key, (FF,), 505)


def draw_down_weight_moments(key, part):
    return moment_pair(key, (FF, D), 606)


def draw_norm_gains_moments(key, part):
    return moment_pair(key, (2, D), 707)


def draw_norm_shifts_moments(key, part):
    return moment_pair(key, (4, D), 808)


def level_of(key, dims, cuts, least, top_value):
    gain, own = 1.0, jax.random.fold_in(key, 6)
    for dim, parts in cuts:
        heights = jnp.exp(jax.random.uniform(jax.random.fold_in(own, dim), (parts,), jnp.float32, least / len(cuts), top_value / len(cuts)))
        gain = gain * jnp.repeat(heights, dims[dim] // parts).reshape([-1 if axis == dim else 1 for axis in range(len(dims))])
    return gain


def noise(rng, dims, deviation, most, pieces=(), kind=jnp.bfloat16):
    drawn = deviation * jax.random.normal(rng, dims, jnp.float32)
    if pieces:
        drawn = drawn * level_of(rng, dims, pieces, -0.22, 0.18)
    return jnp.clip(drawn, -most, most).astype(kind)


def setup_inputs(seed: int = 0) -> dict:
    key_list = jax.random.split(jax.random.key(seed), 19)
    layer_input = draw_layer_input(jax.random.fold_in(key_list[18], 71), 0)
    cotangent = noise(key_list[1], (SEQS, SEQ, D), 1.0, 6.0, ((0, 4), (1, 8)))
    attn_weight = noise(key_list[2], (D, 3 * D), D ** -0.5, 0.1875, ((0, 4), (1, 8)), jnp.float32)
    attn_bias = noise(key_list[3], (HEADS, 3 * HEAD_DIM), 0.5, 3.0, ((0, 8), (1, 4)), jnp.float32)
    out_weight = noise(key_list[4], (D, D), 4 ** -0.5, 3.0, ((0, 8), (1, 4)), jnp.float32)
    up_weight = noise(key_list[5], (D, FF), D ** -0.5, 0.1875, ((0, 4), (1, 8)), jnp.float32)
    up_bias = noise(key_list[6], (FF,), 0.5, 3.0, ((0, 32),), jnp.float32)
    down_weight = noise(key_list[7], (FF, D), FF ** -0.5, 0.09375, ((0, 8), (1, 4)), jnp.float32)
    norm_gains = jnp.clip(1.0 + 0.15 * jax.random.normal(key_list[8], (2, D), jnp.float32), 0.25, 1.75)
    norm_shifts = noise(key_list[9], (4, D), 0.3, 2.0, ((1, 4),), jnp.float32)
    attn_weight_moments = draw_attn_weight_moments(jax.random.fold_in(key_list[18], 71), 0)
    attn_bias_moments = draw_attn_bias_moments(jax.random.fold_in(key_list[18], 71), 0)
    out_weight_moments = draw_out_weight_moments(jax.random.fold_in(key_list[18], 71), 0)
    up_weight_moments = draw_up_weight_moments(jax.random.fold_in(key_list[18], 71), 0)
    up_bias_moments = draw_up_bias_moments(jax.random.fold_in(key_list[18], 71), 0)
    down_weight_moments = draw_down_weight_moments(jax.random.fold_in(key_list[18], 71), 0)
    norm_gains_moments = draw_norm_gains_moments(jax.random.fold_in(key_list[18], 71), 0)
    norm_shifts_moments = draw_norm_shifts_moments(jax.random.fold_in(key_list[18], 71), 0)
    return dict(layer_input=layer_input, cotangent=cotangent, attn_weight=attn_weight, attn_bias=attn_bias, out_weight=out_weight, up_weight=up_weight, up_bias=up_bias, down_weight=down_weight, norm_gains=norm_gains, norm_shifts=norm_shifts, attn_weight_moments=attn_weight_moments, attn_bias_moments=attn_bias_moments, out_weight_moments=out_weight_moments, up_weight_moments=up_weight_moments, up_bias_moments=up_bias_moments, down_weight_moments=down_weight_moments, norm_gains_moments=norm_gains_moments, norm_shifts_moments=norm_shifts_moments)


norm_eps = 1e-05
beta_one = 0.9
beta_two = 0.999
adam_eps = 1e-08
adam_step = 4.0
matrix_rate = 0.01
output_rate = 0.1
vector_rate = 0.1
decay_rate = 0.1
inv_root_two = 0.7071067811865476
inv_root_tau = 0.3989422804014327

def layer_norm(resid, gain_row, shift_row):
    center = resid - lax.optimization_barrier(jnp.mean(resid, axis=-1, keepdims=True))
    spread = lax.rsqrt(lax.optimization_barrier(jnp.mean(center * center, axis=-1, keepdims=True)) + norm_eps)
    normed = center * spread
    return (normed * gain_row + shift_row, normed, spread)

def norm_back(grad_out, gain_row, normed, spread):
    scaled = grad_out * gain_row
    return spread * (scaled - lax.optimization_barrier(jnp.mean(scaled, axis=-1, keepdims=True)) - normed * lax.optimization_barrier(jnp.mean(scaled * normed, axis=-1, keepdims=True)))

def gelu_value(inner):
    return inner * 0.5 * (1.0 + jax.scipy.special.erf(inner * inv_root_two))

def gelu_slope(inner):
    return 0.5 * (1.0 + jax.scipy.special.erf(inner * inv_root_two)) + inner * jnp.exp(-0.5 * inner * inner) * inv_root_tau

def split_heads(qkv, heads, head_width):
    seq_length = qkv.shape[0]
    triple = jnp.transpose(qkv.reshape(seq_length, heads, 3, head_width), (2, 1, 0, 3))
    return (triple[0], triple[1], triple[2])

def merge_heads(mixed):
    heads, seq_length, head_width = mixed.shape
    return jnp.transpose(mixed, (1, 0, 2)).reshape(seq_length, heads * head_width)

def attention_forward(queries, key_rows, values):
    heads, seq_length, head_width = queries.shape
    block_rows = min(512, seq_length)
    block_count = seq_length // block_rows
    score_scale = head_width ** (-0.5)
    key_wide = key_rows.astype(jnp.float32)
    value_wide = values.astype(jnp.float32)

    def one_block(block_index):
        row_block = lax.dynamic_slice_in_dim(queries, block_index * block_rows, block_rows, 1).astype(jnp.float32)
        scores = jnp.einsum('hqd,hkd->hqk', row_block, key_wide) * score_scale
        row_max = lax.optimization_barrier(jnp.max(scores, axis=-1, keepdims=True))
        logsum = row_max + jnp.log(lax.optimization_barrier(jnp.sum(jnp.exp(scores - row_max), axis=-1, keepdims=True)))
        softmax_weights = jnp.exp(scores - logsum).astype(jnp.bfloat16)
        mixed = jnp.einsum('hqk,hkd->hqd', softmax_weights.astype(jnp.float32), value_wide)
        return (mixed.astype(jnp.bfloat16), logsum[..., 0])
    mixed, logsum = lax.map(one_block, jnp.arange(block_count, dtype=jnp.int32))
    mixed = jnp.transpose(mixed, (1, 0, 2, 3)).reshape(heads, seq_length, head_width)
    logsum = jnp.transpose(logsum, (1, 0, 2)).reshape(heads, seq_length)
    return (mixed, logsum)

def attention_back(queries, key_rows, values, logsum, grad_mixed):
    heads, seq_length, head_width = queries.shape
    block_rows = min(512, seq_length)
    block_count = seq_length // block_rows
    score_scale = head_width ** (-0.5)
    key_wide = key_rows.astype(jnp.float32)
    value_wide = values.astype(jnp.float32)

    def block_step(carry, block_index):
        grad_keys, grad_values = carry
        first_row = block_index * block_rows
        row_block = lax.dynamic_slice_in_dim(queries, first_row, block_rows, 1).astype(jnp.float32)
        log_block = lax.dynamic_slice_in_dim(logsum, first_row, block_rows, 1)
        grad_block = lax.dynamic_slice_in_dim(grad_mixed, first_row, block_rows, 1).astype(jnp.float32)
        scores = jnp.einsum('hqd,hkd->hqk', row_block, key_wide) * score_scale
        chances = jnp.exp(scores - log_block[..., None])
        chances_b = chances.astype(jnp.bfloat16).astype(jnp.float32)
        grad_values = grad_values + jnp.einsum('hqk,hqd->hkd', chances_b, grad_block)
        grad_scores = jnp.einsum('hqd,hkd->hqk', grad_block, value_wide)
        grad_logits = chances * (grad_scores - lax.optimization_barrier(jnp.sum(chances * grad_scores, axis=-1, keepdims=True)))
        logits_b = grad_logits.astype(jnp.bfloat16).astype(jnp.float32)
        grad_query = jnp.einsum('hqk,hkd->hqd', logits_b, key_wide) * score_scale
        grad_keys = grad_keys + jnp.einsum('hqk,hqd->hkd', logits_b, row_block) * score_scale
        return ((grad_keys, grad_values), grad_query)
    zeros = jnp.zeros((heads, seq_length, head_width), jnp.float32)
    (grad_keys, grad_values), grad_queries = lax.scan(block_step, (zeros, zeros), jnp.arange(block_count, dtype=jnp.int32))
    grad_queries = jnp.transpose(grad_queries, (1, 0, 2, 3)).reshape(heads, seq_length, head_width)
    return (grad_queries, grad_keys, grad_values)

def adamw_update(weight, moments, grad, rate, decay):
    first_moment = beta_one * moments[0] + (1.0 - beta_one) * grad
    second_moment = beta_two * moments[1] + (1.0 - beta_two) * grad * grad
    direction = first_moment / (1.0 - beta_one ** adam_step) / (jnp.sqrt(second_moment / (1.0 - beta_two ** adam_step)) + adam_eps)
    return (weight - rate * (direction + decay * weight), jnp.stack([first_moment, second_moment]))

def reference(layer_input, cotangent, attn_weight, attn_bias, out_weight, up_weight, up_bias, down_weight, norm_gains, norm_shifts, attn_weight_moments, attn_bias_moments, out_weight_moments, up_weight_moments, up_bias_moments, down_weight_moments, norm_gains_moments, norm_shifts_moments):
    heads = attn_bias.shape[0]
    head_width = attn_bias.shape[1] // 3
    w_attn = attn_weight.astype(jnp.bfloat16)
    w_output = out_weight.astype(jnp.bfloat16)
    w_upward = up_weight.astype(jnp.bfloat16)
    w_downward = down_weight.astype(jnp.bfloat16)
    small = lax.optimization_barrier((attn_bias.astype(jnp.bfloat16), up_bias.astype(jnp.bfloat16), norm_gains.astype(jnp.bfloat16), norm_shifts.astype(jnp.bfloat16)))
    bias_attn = small[0].astype(jnp.float32).reshape(-1)
    bias_upward = small[1].astype(jnp.float32)
    gain_rows = small[2].astype(jnp.float32)
    shift_rows = small[3].astype(jnp.float32)

    def one_sequence(totals, inputs):
        tokens, upstream = inputs
        qkv = (jnp.dot(tokens, w_attn, preferred_element_type=jnp.float32) + bias_attn).astype(jnp.bfloat16)
        queries, key_rows, values = split_heads(qkv, heads, head_width)
        mixed, logsum = attention_forward(queries, key_rows, values)
        attn = merge_heads(mixed)
        resid_one = jnp.dot(attn, w_output, preferred_element_type=jnp.float32) + shift_rows[0] + tokens.astype(jnp.float32)
        hidden_one, normed_one, spread_one = layer_norm(resid_one, gain_rows[0], shift_rows[1])
        hidden_one_b = hidden_one.astype(jnp.bfloat16)
        inner = jnp.dot(hidden_one_b, w_upward, preferred_element_type=jnp.float32) + bias_upward
        active = gelu_value(inner).astype(jnp.bfloat16)
        resid_two = jnp.dot(active, w_downward, preferred_element_type=jnp.float32) + shift_rows[2] + hidden_one
        result, normed_two, spread_two = layer_norm(resid_two, gain_rows[1], shift_rows[3])
        output = result.astype(jnp.bfloat16)
        upward = upstream.astype(jnp.float32)
        grad_two = norm_back(upward, gain_rows[1], normed_two, spread_two)
        grad_two_b = grad_two.astype(jnp.bfloat16)
        grad_down = jnp.dot(active.T, grad_two_b, preferred_element_type=jnp.float32)
        grad_inner = jnp.dot(grad_two_b, w_downward.T, preferred_element_type=jnp.float32) * gelu_slope(inner)
        grad_inner_b = grad_inner.astype(jnp.bfloat16)
        grad_upward = jnp.dot(hidden_one_b.T, grad_inner_b, preferred_element_type=jnp.float32)
        grad_hidden = grad_two + jnp.dot(grad_inner_b, w_upward.T, preferred_element_type=jnp.float32)
        grad_one = norm_back(grad_hidden, gain_rows[0], normed_one, spread_one)
        grad_one_b = grad_one.astype(jnp.bfloat16)
        grad_output = jnp.dot(attn.T, grad_one_b, preferred_element_type=jnp.float32)
        grad_attn = jnp.dot(grad_one_b, w_output.T, preferred_element_type=jnp.float32).astype(jnp.bfloat16)
        grad_mixed = jnp.transpose(grad_attn.reshape(tokens.shape[0], heads, head_width), (1, 0, 2))
        grad_queries, grad_keys, grad_values = attention_back(queries, key_rows, values, logsum, grad_mixed)
        grad_qkv = jnp.transpose(jnp.stack([grad_queries, grad_keys, grad_values]), (2, 1, 0, 3)).reshape(tokens.shape[0], -1)
        grad_qkv_b = grad_qkv.astype(jnp.bfloat16)
        grad_attn_w = jnp.dot(tokens.T, grad_qkv_b, preferred_element_type=jnp.float32)
        input_grad = grad_one + jnp.dot(grad_qkv_b, w_attn.T, preferred_element_type=jnp.float32)
        grad_gain = jnp.stack([lax.optimization_barrier(jnp.sum(grad_hidden * normed_one, axis=0)), lax.optimization_barrier(jnp.sum(upward * normed_two, axis=0))])
        grad_shift = jnp.stack([lax.optimization_barrier(jnp.sum(grad_one, axis=0)), lax.optimization_barrier(jnp.sum(grad_hidden, axis=0)), lax.optimization_barrier(jnp.sum(grad_two, axis=0)), lax.optimization_barrier(jnp.sum(upward, axis=0))])
        terms = (grad_attn_w, lax.optimization_barrier(jnp.sum(grad_qkv, axis=0)).reshape(heads, 3 * head_width), grad_output, grad_upward, lax.optimization_barrier(jnp.sum(grad_inner, axis=0)), grad_down, grad_gain, grad_shift)
        return (tuple((total + term for total, term in zip(totals, terms))), (output, input_grad))
    weights = (attn_weight, attn_bias, out_weight, up_weight, up_bias, down_weight, norm_gains, norm_shifts)
    moments = (attn_weight_moments, attn_bias_moments, out_weight_moments, up_weight_moments, up_bias_moments, down_weight_moments, norm_gains_moments, norm_shifts_moments)
    zero_grads = tuple((jnp.zeros(weight.shape, jnp.float32) for weight in weights))
    grads, (outputs, input_grads) = lax.scan(one_sequence, zero_grads, (layer_input, cotangent))
    rates = (matrix_rate, vector_rate, output_rate, matrix_rate, vector_rate, matrix_rate, vector_rate, vector_rate)
    decays = (decay_rate, 0.0, decay_rate, decay_rate, 0.0, decay_rate, 0.0, 0.0)
    updated = [adamw_update(weights[place], moments[place], grads[place], rates[place], decays[place]) for place in range(8)]
    new_weights = tuple((pair[0] for pair in updated))
    new_moments = tuple((pair[1] for pair in updated))
    return (outputs, input_grads, grads[0], grads[1], grads[2], grads[3], grads[4], grads[5], grads[6], grads[7], new_weights[0], new_weights[1], new_weights[2], new_weights[3], new_weights[4], new_weights[5], new_weights[6], new_weights[7], new_moments[0], new_moments[1], new_moments[2], new_moments[3], new_moments[4], new_moments[5], new_moments[6], new_moments[7])
```

```python
import jax
import jax.numpy as jnp
from jax import lax
from jax.sharding import PartitionSpec as P

norm_eps = 1e-05
beta_one = 0.9
beta_two = 0.999
adam_eps = 1e-08
adam_step = 4.0
matrix_rate = 0.01
output_rate = 0.1
vector_rate = 0.1
decay_rate = 0.1
inv_root_two = 0.7071067811865476
inv_root_tau = 0.3989422804014327


def layer_norm(resid, gain_row, shift_row):
    center = resid - jnp.mean(resid, axis=-1, keepdims=True)
    spread = lax.rsqrt(jnp.mean(center * center, axis=-1, keepdims=True) + norm_eps)
    normed = center * spread
    return (normed * gain_row + shift_row, normed, spread)


def norm_back(grad_out, gain_row, normed, spread):
    scaled = grad_out * gain_row
    return spread * (
        scaled
        - jnp.mean(scaled, axis=-1, keepdims=True)
        - normed * jnp.mean(scaled * normed, axis=-1, keepdims=True)
    )


def gelu_value(inner):
    return inner * 0.5 * (1.0 + jax.scipy.special.erf(inner * inv_root_two))


def gelu_slope(inner):
    return (
        0.5 * (1.0 + jax.scipy.special.erf(inner * inv_root_two))
        + inner * jnp.exp(-0.5 * inner * inner) * inv_root_tau
    )


def split_heads(qkv, heads, head_width):
    seq_length = qkv.shape[0]
    triple = jnp.transpose(qkv.reshape(seq_length, heads, 3, head_width), (2, 1, 0, 3))
    return (triple[0], triple[1], triple[2])


def merge_heads(mixed):
    heads, seq_length, head_width = mixed.shape
    return jnp.transpose(mixed, (1, 0, 2)).reshape(seq_length, heads * head_width)


def attention_forward(queries, key_rows, values):
    heads, seq_length, head_width = queries.shape
    block_rows = min(512, seq_length)
    block_count = seq_length // block_rows
    score_scale = head_width ** (-0.5)

    def one_block(block_index):
        row_block = lax.dynamic_slice_in_dim(queries, block_index * block_rows, block_rows, 1)
        scores = (
            jnp.einsum("hqd,hkd->hqk", row_block, key_rows, preferred_element_type=jnp.float32)
            * score_scale
        )
        row_max = jnp.max(scores, axis=-1, keepdims=True)
        logsum = row_max + jnp.log(jnp.sum(jnp.exp(scores - row_max), axis=-1, keepdims=True))
        softmax_weights = jnp.exp(scores - logsum).astype(jnp.bfloat16)
        mixed = jnp.einsum(
            "hqk,hkd->hqd", softmax_weights, values, preferred_element_type=jnp.float32
        )
        return (mixed.astype(jnp.bfloat16), logsum[..., 0])

    mixed, logsum = lax.map(one_block, jnp.arange(block_count, dtype=jnp.int32))
    mixed = jnp.transpose(mixed, (1, 0, 2, 3)).reshape(heads, seq_length, head_width)
    logsum = jnp.transpose(logsum, (1, 0, 2)).reshape(heads, seq_length)
    return (mixed, logsum)


def attention_back(queries, key_rows, values, logsum, grad_mixed):
    heads, seq_length, head_width = queries.shape
    block_rows = min(512, seq_length)
    block_count = seq_length // block_rows
    score_scale = head_width ** (-0.5)

    def block_step(carry, block_index):
        grad_keys, grad_values = carry
        first_row = block_index * block_rows
        row_block = lax.dynamic_slice_in_dim(queries, first_row, block_rows, 1)
        log_block = lax.dynamic_slice_in_dim(logsum, first_row, block_rows, 1)
        grad_block = lax.dynamic_slice_in_dim(grad_mixed, first_row, block_rows, 1)
        scores = (
            jnp.einsum("hqd,hkd->hqk", row_block, key_rows, preferred_element_type=jnp.float32)
            * score_scale
        )
        chances = jnp.exp(scores - log_block[..., None])
        chances_b = chances.astype(jnp.bfloat16)
        grad_values = grad_values + jnp.einsum(
            "hqk,hqd->hkd", chances_b, grad_block, preferred_element_type=jnp.float32
        )
        grad_scores = jnp.einsum(
            "hqd,hkd->hqk", grad_block, values, preferred_element_type=jnp.float32
        )
        grad_logits = chances * (
            grad_scores - jnp.sum(chances * grad_scores, axis=-1, keepdims=True)
        )
        logits_b = grad_logits.astype(jnp.bfloat16)
        grad_query = (
            jnp.einsum("hqk,hkd->hqd", logits_b, key_rows, preferred_element_type=jnp.float32)
            * score_scale
        )
        grad_keys = (
            grad_keys
            + jnp.einsum("hqk,hqd->hkd", logits_b, row_block, preferred_element_type=jnp.float32)
            * score_scale
        )
        return ((grad_keys, grad_values), grad_query)

    zeros = jnp.zeros((heads, seq_length, head_width), jnp.float32)
    (grad_keys, grad_values), grad_queries = lax.scan(
        block_step, (zeros, zeros), jnp.arange(block_count, dtype=jnp.int32)
    )
    grad_queries = jnp.transpose(grad_queries, (1, 0, 2, 3)).reshape(heads, seq_length, head_width)
    return (grad_queries, grad_keys, grad_values)


def adamw_update(weight, moments, grad, rate, decay):
    first_moment = beta_one * moments[0] + (1.0 - beta_one) * grad
    second_moment = beta_two * moments[1] + (1.0 - beta_two) * grad * grad
    direction = (
        first_moment
        / (1.0 - beta_one**adam_step)
        / (jnp.sqrt(second_moment / (1.0 - beta_two**adam_step)) + adam_eps)
    )
    return (weight - rate * (direction + decay * weight), jnp.stack([first_moment, second_moment]))

AXES = ("fsdp", "tensor")


class Layout:
    def __init__(self, local_heads, local_seqs):
        self.fsdp = lax.axis_size("fsdp")
        self.tensor = lax.axis_size("tensor")
        self.seqs = local_seqs
        self.core = 2 if local_heads % 2 == 0 and self.fsdp % 2 == 0 else 1
        self.outer = self.fsdp // self.core
        self.high = self.core * local_seqs
        self.low = self.tensor // self.high
        self.fsdp_index = lax.axis_index("fsdp")
        self.outer_index = self.fsdp_index // self.core
        self.core_index = self.fsdp_index % self.core
        self.high_index = lax.axis_index("tensor") // self.low

    def send(self, value, target):
        pairs = []
        for outer in range(self.outer):
            for core in range(self.core):
                for high in range(self.high):
                    for low in range(self.low):
                        o, c, h, l = target(outer, core, high, low)
                        source_id = (outer * self.core + core) * self.tensor + high * self.low + low
                        target_id = (o * self.core + c) * self.tensor + h * self.low + l
                        pairs.append((source_id, target_id))
        return lax.ppermute(value, AXES, pairs)

    def swap_core(self, value):
        return self.send(value, lambda o, c, h, l: (o, 1 - c, h, l))

    def to_low(self, value, step):
        return self.send(value, lambda o, c, h, l: (o, c, h, (l + step) % self.low))

    def to_high(self, value, step):
        return self.send(value, lambda o, c, h, l: (o, c, (h + step) % self.high, l))

    def to_outer(self, value, step):
        return self.send(value, lambda o, c, h, l: ((o + step) % self.outer, c, h, l))

    def to_sequence(self, blocks):
        within = self.high_index % self.seqs
        return [
            self.send(
                lax.dynamic_index_in_dim(blocks, (within + k) % self.seqs, 0, keepdims=False),
                lambda o, c, h, l, k=k: (
                    o,
                    h // self.seqs,
                    c * self.seqs + (h % self.seqs + k) % self.seqs,
                    l,
                ),
            )
            for k in range(self.seqs)
        ]

    def from_sequence(self, pieces):
        within = self.high_index % self.seqs
        back = []
        for k in range(self.seqs):
            back.append(
                self.send(
                    pieces[k],
                    lambda o, c, h, l, k=k: (
                        o,
                        h // self.seqs,
                        c * self.seqs + (h % self.seqs - k) % self.seqs,
                        l,
                    ),
                )
            )
        if self.seqs == 2:
            return jnp.where(within == 0, jnp.stack(back), jnp.stack(back[::-1]))
        stacked = jnp.stack(back)
        order = (jnp.arange(self.seqs) - within) % self.seqs
        return jnp.take(stacked, order, axis=0)

    def share(self, own):
        pieces = []
        for step in range(self.low):
            piece = own if step == 0 else self.to_low(own, -step)
            pieces.append(piece)
            if self.core == 2:
                pieces.append(self.swap_core(piece))
        return jnp.concatenate(pieces, axis=0)

    def reduce(self, partial):
        count = partial.shape[0] // (self.core * self.low)
        sums = []
        for step in range(self.low):
            base = step * self.core * count
            total = partial[base : base + count]
            if self.core == 2:
                other = partial[base + count : base + 2 * count].astype(jnp.bfloat16)
                total = total + self.swap_core(other).astype(jnp.float32)
            sums.append(total)
        result = sums[0]
        for step in range(1, self.low):
            result = result + self.to_low(sums[step].astype(jnp.bfloat16), step).astype(jnp.float32)
        return result

    def ordered(self, index, parts, axis):
        count = len(parts)
        if count == 1:
            return parts[0]
        if count == 2:
            return jnp.where(
                index == 0,
                jnp.concatenate(parts, axis=axis),
                jnp.concatenate(parts[::-1], axis=axis),
            )
        width = parts[0].shape[axis]
        shape = list(parts[0].shape)
        shape[axis] = width * count
        result = jnp.zeros(shape, parts[0].dtype)
        for step, part in enumerate(parts):
            result = lax.dynamic_update_slice_in_dim(
                result, part, ((index + step) % count) * width, axis
            )
        return result

    def core_rows(self, rows, core):
        count = rows.shape[0] // self.core
        return lax.dynamic_slice_in_dim(rows, core * count, count, 0)

    def gather_weight(self, rows, extra=None):
        mine = self.core_rows(rows, self.core_index)
        if extra is not None:
            mine = jnp.concatenate([mine, extra], axis=0)
        if self.core == 2:
            other = self.core_rows(rows, 1 - self.core_index)
            if extra is not None:
                other = jnp.concatenate([other, extra], axis=0)
            mine = self.ordered(self.core_index, [mine, self.swap_core(other)], 1)
        column = [mine] + [self.to_high(mine, -step) for step in range(1, self.high)]
        column = jnp.concatenate(column, axis=0)
        return self.ordered(
            self.outer_index,
            [column] + [self.to_outer(column, -step) for step in range(1, self.outer)],
            1,
        )

    def scatter_weight(self, grad, extra=None):
        if extra is not None:
            grad = jnp.concatenate([grad, extra], axis=1)
        width = grad.shape[2] // self.outer

        def columns(place):
            return lax.dynamic_slice_in_dim(grad, (place % self.outer) * width, width, 2)

        total = columns(self.outer_index)
        for step in range(1, self.outer):
            part = columns(self.outer_index + step).astype(jnp.bfloat16)
            total = total + self.to_outer(part, step).astype(jnp.float32)
        column = total[0]
        for step in range(1, self.high):
            part = total[step].astype(jnp.bfloat16)
            column = column + self.to_high(part, step).astype(jnp.float32)
        if self.core == 1:
            if extra is None:
                return column
            return column[: -extra.shape[1]], column[-extra.shape[1] :]
        width = width // self.core
        mine = lax.dynamic_slice_in_dim(column, self.core_index * width, width, 1)
        other = self.swap_core(
            lax.dynamic_slice_in_dim(column, (1 - self.core_index) * width, width, 1)
        )
        if extra is None:
            return self.ordered(self.core_index, [mine, other], 0)
        count = extra.shape[1]
        return (
            self.ordered(self.core_index, [mine[:-count], other[:-count]], 0),
            mine[-count:] + other[-count:],
        )

    def total(self, value):
        if self.core == 2:
            value = value + self.swap_core(value)
        bit = 1
        while bit < self.low:
            value = value + self.send(value, lambda o, c, h, l: (o, c, h, l ^ bit))
            bit *= 2
        bit = 1
        while bit < self.outer:
            value = value + self.send(value, lambda o, c, h, l: (o ^ bit, c, h, l))
            bit *= 2
        bit = 1
        while bit < self.high:
            value = value + self.send(value, lambda o, c, h, l: (o, c, h ^ bit, l))
            bit *= 2
        return value


SMALL_ROWS = 16


def pad_columns(rows, width):
    return jnp.pad(rows, [(0, 0)] * (rows.ndim - 1) + [(0, width - rows.shape[-1])])


def per_device(
    layer_input,
    cotangent,
    attn_weight,
    attn_bias,
    out_weight,
    up_weight,
    up_bias,
    down_weight,
    norm_gains,
    norm_shifts,
    attn_weight_moments,
    attn_bias_moments,
    out_weight_moments,
    up_weight_moments,
    up_bias_moments,
    down_weight_moments,
    norm_gains_moments,
    norm_shifts_moments,
):
    local_heads = attn_bias.shape[0]
    local_seqs, block_tokens, model_width = layer_input.shape
    lay = Layout(local_heads, local_seqs)
    fsdp, core, high = lay.fsdp, lay.core, lay.high
    bias_width = attn_bias.shape[1]
    head_width = bias_width * fsdp // 3
    part_heads = local_heads // core
    heads = part_heads * high
    shard_width = model_width // fsdp
    hidden_part = up_bias.shape[0]
    weights = (
        attn_weight,
        attn_bias,
        out_weight,
        up_weight,
        up_bias,
        down_weight,
        norm_gains,
        norm_shifts,
    )
    half = jnp.bfloat16
    wide = jnp.float32

    pairs = lay.to_sequence(jnp.stack([layer_input, cotangent], axis=1))
    tokens = jnp.concatenate([pair[0] for pair in pairs], axis=0)
    upward = jnp.concatenate([pair[1] for pair in pairs], axis=0).astype(wide)
    small = jnp.concatenate(
        [
            norm_gains.astype(half),
            norm_shifts.astype(half),
            pad_columns(attn_bias.astype(half).reshape(1, -1), shard_width),
            pad_columns(up_bias.astype(half).reshape(1, -1), shard_width),
            jnp.zeros((SMALL_ROWS - 8, shard_width), half),
        ],
        axis=0,
    )
    attn_rows = part_heads * 3 * head_width
    packed = lay.gather_weight(attn_weight.astype(half).T, small)
    packed = packed.reshape(high, attn_rows + SMALL_ROWS, model_width)
    w_attn = packed[:, :attn_rows].reshape(high * attn_rows, model_width)
    small = packed[:, attn_rows:]
    gain_rows = small[0, 0:2].astype(wide)
    shift_rows = small[0, 2:6].astype(wide)
    b_attn = small[:, 6].reshape(high, fsdp, shard_width)[:, :, : local_heads * bias_width]
    b_attn = b_attn.reshape(high, fsdp, core, part_heads, bias_width)
    b_attn = lax.dynamic_index_in_dim(b_attn, lay.core_index, 2, keepdims=False)
    b_attn = jnp.transpose(b_attn, (0, 2, 1, 3)).reshape(-1).astype(wide)
    b_upward = small[:, 7].reshape(high, fsdp, shard_width)[:, :, :hidden_part]
    b_upward = b_upward.reshape(high, core, (fsdp // core) * hidden_part)
    b_upward = lax.dynamic_index_in_dim(b_upward, lay.core_index, 1, keepdims=False)
    b_upward = b_upward.reshape(-1).astype(wide)
    w_output = lay.gather_weight(out_weight.astype(half))
    w_upward = lay.gather_weight(up_weight.astype(half).T)
    w_downward = lay.gather_weight(down_weight.astype(half))

    def times(left, right):
        return jnp.dot(left, right, preferred_element_type=wide)

    def times_t(left, right):
        return lax.dot_general(left, right, (((1,), (1,)), ((), ())), preferred_element_type=wide)

    def t_times(left, right):
        return lax.dot_general(left, right, (((0,), (0,)), ((), ())), preferred_element_type=wide)

    gathered = lay.share(tokens)
    seq_length = gathered.shape[0]
    qkv = (times_t(gathered, w_attn) + b_attn).astype(half)
    queries, key_rows, values = split_heads(qkv, heads, head_width)
    mixed, logsum = attention_forward(queries, key_rows, values)
    attn = merge_heads(mixed)
    attn_out = lay.reduce(times(attn, w_output))
    resid_one = attn_out + shift_rows[0] + tokens.astype(wide)
    hidden_one, normed_one, spread_one = layer_norm(resid_one, gain_rows[0], shift_rows[1])
    expanded = lay.share(hidden_one.astype(half))
    inner = times_t(expanded, w_upward) + b_upward
    active = gelu_value(inner).astype(half)
    ffn_out = lay.reduce(times(active, w_downward))
    resid_two = ffn_out + shift_rows[2] + hidden_one
    result, normed_two, spread_two = layer_norm(resid_two, gain_rows[1], shift_rows[3])
    output = result.astype(half).reshape(local_seqs, block_tokens, model_width)
    outputs = lay.from_sequence(output)

    grad_two = norm_back(upward, gain_rows[1], normed_two, spread_two)
    grad_full = lay.share(grad_two.astype(half))
    grad_inner = times_t(grad_full, w_downward) * gelu_slope(inner)
    grad_inner_b = grad_inner.astype(half)
    grad_hidden = grad_two + lay.reduce(times(grad_inner_b, w_upward))
    grad_down = t_times(active, grad_full)
    grad_upward = t_times(grad_inner_b, expanded)
    grad_one = norm_back(grad_hidden, gain_rows[0], normed_one, spread_one)
    one_full = lay.share(grad_one.astype(half))
    grad_attn = times_t(one_full, w_output).astype(half)
    grad_mixed = jnp.transpose(grad_attn.reshape(seq_length, heads, head_width), (1, 0, 2))
    grad_output = t_times(attn, one_full)
    grad_queries, grad_keys, grad_values = attention_back(
        queries, key_rows, values, logsum, grad_mixed
    )
    grad_qkv = jnp.transpose(
        jnp.stack([grad_queries, grad_keys, grad_values]), (2, 1, 0, 3)
    ).reshape(seq_length, -1)
    grad_qkv_b = grad_qkv.astype(half)
    input_grad = grad_one + lay.reduce(times(grad_qkv_b, w_attn))
    input_grads = lay.from_sequence(input_grad.reshape(local_seqs, block_tokens, model_width))
    grad_attn_w = t_times(grad_qkv_b, gathered)

    norm_sums = lay.total(
        jnp.stack(
            [
                jnp.sum(grad_hidden * normed_one, axis=0),
                jnp.sum(upward * normed_two, axis=0),
                jnp.sum(grad_one, axis=0),
                jnp.sum(grad_hidden, axis=0),
                jnp.sum(grad_two, axis=0),
                jnp.sum(upward, axis=0),
            ]
        )
    )
    norm_sums = lax.dynamic_slice_in_dim(norm_sums, lay.fsdp_index * shard_width, shard_width, 1)
    core_here = jnp.arange(core) == lay.core_index
    bias_sums = jnp.sum(grad_qkv, axis=0).reshape(high, part_heads, fsdp, bias_width)
    bias_sums = jnp.transpose(bias_sums, (0, 2, 1, 3))[:, :, None]
    bias_sums = jnp.where(core_here[:, None, None], bias_sums, 0.0)
    bias_sums = pad_columns(bias_sums.reshape(high, fsdp, -1), shard_width)
    up_sums = jnp.sum(grad_inner, axis=0).reshape(high, 1, (fsdp // core) * hidden_part)
    up_sums = jnp.where(core_here[:, None], up_sums, 0.0)
    up_sums = pad_columns(up_sums.reshape(high, fsdp, hidden_part), shard_width)
    small_sums = jnp.pad(
        jnp.stack([bias_sums.reshape(high, -1), up_sums.reshape(high, -1)], axis=1),
        ((0, 0), (0, SMALL_ROWS - 2), (0, 0)),
    )
    down_shard = lay.scatter_weight(grad_down.reshape(high, -1, model_width))
    up_shard = lay.scatter_weight(grad_upward.reshape(high, -1, model_width)).T
    out_shard = lay.scatter_weight(grad_output.reshape(high, -1, model_width))
    attn_shard, small_shard = lay.scatter_weight(
        grad_attn_w.reshape(high, -1, model_width), small_sums
    )
    grads = (
        attn_shard.T,
        small_shard[0, : local_heads * bias_width].reshape(local_heads, bias_width),
        out_shard,
        up_shard,
        small_shard[1, :hidden_part],
        down_shard,
        norm_sums[0:2],
        norm_sums[2:6],
    )
    moments = (
        attn_weight_moments,
        attn_bias_moments,
        out_weight_moments,
        up_weight_moments,
        up_bias_moments,
        down_weight_moments,
        norm_gains_moments,
        norm_shifts_moments,
    )
    rates = (
        matrix_rate,
        vector_rate,
        output_rate,
        matrix_rate,
        vector_rate,
        matrix_rate,
        vector_rate,
        vector_rate,
    )
    decays = (decay_rate, 0.0, decay_rate, decay_rate, 0.0, decay_rate, 0.0, 0.0)
    updated = [
        adamw_update(weights[place], moments[place], grads[place], rates[place], decays[place])
        for place in range(8)
    ]
    new_weights = tuple((pair[0] for pair in updated))
    new_moments = tuple((pair[1] for pair in updated))
    return (outputs, input_grads) + grads + new_weights + new_moments


def solution(mesh):
    return jax.shard_map(
        per_device,
        mesh=mesh,
        in_specs=(
            P("fsdp", "tensor", None),
            P("fsdp", "tensor", None),
            P("fsdp", "tensor"),
            P("tensor", "fsdp"),
            P("tensor", "fsdp"),
            P("fsdp", "tensor"),
            P(("tensor", "fsdp")),
            P("tensor", "fsdp"),
            P(None, "fsdp"),
            P(None, "fsdp"),
            P(None, "fsdp", "tensor"),
            P(None, "tensor", "fsdp"),
            P(None, "tensor", "fsdp"),
            P(None, "fsdp", "tensor"),
            P(None, ("tensor", "fsdp")),
            P(None, "tensor", "fsdp"),
            P(None, None, "fsdp"),
            P(None, None, "fsdp"),
        ),
        out_specs=(
            P("fsdp", "tensor", None),
            P("fsdp", "tensor", None),
            P("fsdp", "tensor"),
            P("tensor", "fsdp"),
            P("tensor", "fsdp"),
            P("fsdp", "tensor"),
            P(("tensor", "fsdp")),
            P("tensor", "fsdp"),
            P(None, "fsdp"),
            P(None, "fsdp"),
            P("fsdp", "tensor"),
            P("tensor", "fsdp"),
            P("tensor", "fsdp"),
            P("fsdp", "tensor"),
            P(("tensor", "fsdp")),
            P("tensor", "fsdp"),
            P(None, "fsdp"),
            P(None, "fsdp"),
            P(None, "fsdp", "tensor"),
            P(None, "tensor", "fsdp"),
            P(None, "tensor", "fsdp"),
            P(None, "fsdp", "tensor"),
            P(None, ("tensor", "fsdp")),
            P(None, "tensor", "fsdp"),
            P(None, None, "fsdp"),
            P(None, None, "fsdp"),
        ),
        check_vma=False,
    )
```

```python
import functools

import jax
import jax.numpy as jnp
from jax import lax
from jax.experimental import pallas as pl
from jax.experimental.pallas import tpu as pltpu
from jax.sharding import PartitionSpec as P

norm_eps = 1e-05
beta_one = 0.9
beta_two = 0.999
adam_eps = 1e-08
adam_step = 4.0
matrix_rate = 0.01
output_rate = 0.1
vector_rate = 0.1
decay_rate = 0.1
inv_root_two = 0.7071067811865476
inv_root_tau = 0.3989422804014327


def layer_norm(resid, gain_row, shift_row):
    center = resid - jnp.mean(resid, axis=-1, keepdims=True)
    spread = lax.rsqrt(jnp.mean(center * center, axis=-1, keepdims=True) + norm_eps)
    normed = center * spread
    return (normed * gain_row + shift_row, normed, spread)


def norm_back(grad_out, gain_row, normed, spread):
    scaled = grad_out * gain_row
    return spread * (
        scaled
        - jnp.mean(scaled, axis=-1, keepdims=True)
        - normed * jnp.mean(scaled * normed, axis=-1, keepdims=True)
    )


def gelu_value(inner):
    return inner * 0.5 * (1.0 + jax.scipy.special.erf(inner * inv_root_two))


def gelu_slope(inner):
    return (
        0.5 * (1.0 + jax.scipy.special.erf(inner * inv_root_two))
        + inner * jnp.exp(-0.5 * inner * inner) * inv_root_tau
    )


def adamw_update(weight, moments, grad, rate, decay):
    first_moment = beta_one * moments[0] + (1.0 - beta_one) * grad
    second_moment = beta_two * moments[1] + (1.0 - beta_two) * grad * grad
    direction = (
        first_moment
        / (1.0 - beta_one**adam_step)
        / (jnp.sqrt(second_moment / (1.0 - beta_two**adam_step)) + adam_eps)
    )
    return (weight - rate * (direction + decay * weight), jnp.stack([first_moment, second_moment]))


half = jnp.bfloat16
wide = jnp.float32
VMEM_BYTES = 40 * 1024 * 1024


def times(left, right):
    return lax.dot_general(left, right, (((1,), (0,)), ((), ())), preferred_element_type=wide)


def times_t(left, right):
    return lax.dot_general(left, right, (((1,), (1,)), ((), ())), preferred_element_type=wide)


def t_times(left, right):
    return lax.dot_general(left, right, (((0,), (0,)), ((), ())), preferred_element_type=wide)


def whole_block(*shape):
    return pl.BlockSpec(shape, lambda step: (0,) * len(shape))


def sum_shapes(rows, other, width):
    shapes = [jax.ShapeDtypeStruct((rows - other, width), wide)]
    if other:
        shapes.append(jax.ShapeDtypeStruct((other, width), half))
    return shapes, [whole_block(*shape.shape) for shape in shapes]


def write_sums(total, refs):
    mine = refs[0].shape[0]
    refs[0][...] = total[:mine]
    if len(refs) > 1:
        refs[1][...] = total[mine:].astype(half)


def params():
    return pltpu.CompilerParams(
        dimension_semantics=("arbitrary",), vmem_limit_bytes=VMEM_BYTES
    )


def up_kernel(x_ref, up_ref, bias_ref, down_ref, active_ref, slope_ref, *rest):
    sums, total = rest[:-1], rest[-1]
    inner = times_t(x_ref[...], up_ref[...]) + bias_ref[...]
    chance = 0.5 * (1.0 + lax.erf(inner * inv_root_two))
    active = (inner * chance).astype(half)
    active_ref[...] = active
    slope_ref[...] = chance + inner * jnp.exp(-0.5 * inner * inner) * inv_root_tau
    part = times(active, down_ref[...])
    step = pl.program_id(0)

    @pl.when(step == 0)
    def _():
        total[...] = part

    @pl.when(step > 0)
    def _():
        total[...] += part

    @pl.when(step == pl.num_programs(0) - 1)
    def _():
        write_sums(total[...], sums)


def ffn_forward(x, w_upward, b_upward, w_downward, other):
    rows, width = x.shape
    hidden = w_upward.shape[0]
    tile = 256
    shapes, specs = sum_shapes(rows, other, width)
    return pl.pallas_call(
        up_kernel,
        grid=(hidden // tile,),
        in_specs=[
            whole_block(rows, width),
            pl.BlockSpec((tile, width), lambda step: (step, 0)),
            pl.BlockSpec((1, tile), lambda step: (0, step)),
            pl.BlockSpec((tile, width), lambda step: (step, 0)),
        ],
        out_specs=[
            pl.BlockSpec((rows, tile), lambda step: (0, step)),
            pl.BlockSpec((rows, tile), lambda step: (0, step)),
        ]
        + specs,
        out_shape=[
            jax.ShapeDtypeStruct((rows, hidden), half),
            jax.ShapeDtypeStruct((rows, hidden), wide),
        ]
        + shapes,
        scratch_shapes=[pltpu.VMEM((rows, width), wide)],
        compiler_params=params(),
        cost_estimate=pl.CostEstimate(
            flops=4 * rows * width * hidden,
            bytes_accessed=rows * hidden * 6 + hidden * width * 4,
            transcendentals=2 * rows * hidden,
        ),
        name="ffn_forward",
    )(x, w_upward, b_upward, w_downward)


def down_kernel(grad_ref, slope_ref, down_ref, up_ref, inner_ref, bias_ref, *rest):
    sums, total = rest[:-1], rest[-1]
    grad_inner = times_t(grad_ref[...], down_ref[...]) * slope_ref[...]
    bias_ref[...] = jnp.sum(grad_inner, axis=0, keepdims=True)
    grad_inner_b = grad_inner.astype(half)
    inner_ref[...] = grad_inner_b
    part = times(grad_inner_b, up_ref[...])
    step = pl.program_id(0)

    @pl.when(step == 0)
    def _():
        total[...] = part

    @pl.when(step > 0)
    def _():
        total[...] += part

    @pl.when(step == pl.num_programs(0) - 1)
    def _():
        write_sums(total[...], sums)


def ffn_backward(grad, slope, w_downward, w_upward, other):
    rows, width = grad.shape
    hidden = w_upward.shape[0]
    tile = 256
    shapes, specs = sum_shapes(rows, other, width)
    return pl.pallas_call(
        down_kernel,
        grid=(hidden // tile,),
        in_specs=[
            whole_block(rows, width),
            pl.BlockSpec((rows, tile), lambda step: (0, step)),
            pl.BlockSpec((tile, width), lambda step: (step, 0)),
            pl.BlockSpec((tile, width), lambda step: (step, 0)),
        ],
        out_specs=[
            pl.BlockSpec((rows, tile), lambda step: (0, step)),
            pl.BlockSpec((1, tile), lambda step: (0, step)),
        ]
        + specs,
        out_shape=[
            jax.ShapeDtypeStruct((rows, hidden), half),
            jax.ShapeDtypeStruct((1, hidden), wide),
        ]
        + shapes,
        scratch_shapes=[pltpu.VMEM((rows, width), wide)],
        compiler_params=params(),
        cost_estimate=pl.CostEstimate(
            flops=4 * rows * width * hidden,
            bytes_accessed=rows * hidden * 6 + hidden * width * 4,
            transcendentals=0,
        ),
        name="ffn_backward",
    )(grad, slope, w_downward, w_upward)


def attention_kernel(first, chunk, head_width, qkv_ref, out_ref, attn_ref, log_ref, *rest):
    sums, mixed = rest[:-1], rest[-1]
    head = pl.program_id(0)
    scale = head_width ** (-0.5)
    keys = jnp.transpose(qkv_ref[head_width : 2 * head_width, :])
    values = qkv_ref[2 * head_width : 3 * head_width, :]
    count = attn_ref.shape[1]
    for start in range(0, count, chunk):
        here = slice(first + start, first + start + chunk)
        scores = times(keys, qkv_ref[0:head_width, here]) * scale
        top = jnp.max(scores, axis=0, keepdims=True)
        powers = jnp.exp(scores - top)
        norm = jnp.sum(powers, axis=0, keepdims=True)
        weights = (powers * (1.0 / norm)).astype(half)
        log_ref[0, :, start : start + chunk] = top + jnp.log(norm)
        block = times(values, weights).astype(half)
        attn_ref[:, start : start + chunk] = block
        mixed[pl.ds(pl.multiple_of(head * head_width, head_width), head_width), pl.ds(start, chunk)] = block

    @pl.when(head == pl.num_programs(0) - 1)
    def _():
        write_sums(t_times(mixed[...], out_ref[...]), sums)


def attention_forward(qkv, w_output, first, count, other, head_width):
    length = qkv.shape[1]
    heads = qkv.shape[0] // (3 * head_width)
    width = w_output.shape[1]
    chunk = 256 if count % 256 == 0 else 128
    shapes, specs = sum_shapes(count, other, width)
    return pl.pallas_call(
        functools.partial(attention_kernel, first, chunk, head_width),
        grid=(heads,),
        in_specs=[
            pl.BlockSpec((3 * head_width, length), lambda head: (head, 0)),
            whole_block(heads * head_width, width),
        ],
        out_specs=[
            pl.BlockSpec((head_width, count), lambda head: (head, 0)),
            pl.BlockSpec((1, 1, count), lambda head: (head, 0, 0)),
        ]
        + specs,
        out_shape=[
            jax.ShapeDtypeStruct((heads * head_width, count), half),
            jax.ShapeDtypeStruct((heads, 1, count), wide),
        ]
        + shapes,
        scratch_shapes=[pltpu.VMEM((heads * head_width, count), half)],
        compiler_params=params(),
        cost_estimate=pl.CostEstimate(
            flops=16 * heads * count * length * head_width,
            bytes_accessed=qkv.size * 2 + count * width * 6,
            transcendentals=heads * count * length,
        ),
        name="attention_forward",
    )(qkv, w_output)


def attention_back_kernel(chunk, head_width, qkv_ref, log_ref, grad_ref, out_ref, bias_ref):
    scale = head_width ** (-0.5)
    key_rows = qkv_ref[head_width : 2 * head_width, :]
    keys = jnp.transpose(key_rows)
    values = jnp.transpose(qkv_ref[2 * head_width : 3 * head_width, :])
    length = keys.shape[0]
    grad_keys = jnp.zeros((length, head_width), wide)
    grad_values = jnp.zeros((length, head_width), wide)
    query_sum = jnp.zeros((head_width, 1), wide)
    for start in range(0, length, chunk):
        here = slice(start, start + chunk)
        queries = qkv_ref[0:head_width, here]
        grads = grad_ref[:, here]
        scores = times(keys, queries) * scale
        chances = jnp.exp(scores - log_ref[0, :, here])
        grad_scores = times(values, grads)
        mean = jnp.sum(chances * grad_scores, axis=0, keepdims=True)
        logits = (chances * (grad_scores - mean)).astype(half)
        grad_values = grad_values + times(chances.astype(half), jnp.transpose(grads))
        grad_keys = grad_keys + times(logits, jnp.transpose(queries))
        grad_query = times(key_rows, logits) * scale
        out_ref[0:head_width, here] = grad_query.astype(half)
        query_sum = query_sum + jnp.sum(grad_query, axis=1, keepdims=True)
    grad_keys = jnp.transpose(grad_keys) * scale
    grad_values = jnp.transpose(grad_values)
    out_ref[head_width : 2 * head_width, :] = grad_keys.astype(half)
    out_ref[2 * head_width : 3 * head_width, :] = grad_values.astype(half)
    sums = jnp.concatenate(
        [
            query_sum,
            jnp.sum(grad_keys, axis=1, keepdims=True),
            jnp.sum(grad_values, axis=1, keepdims=True),
        ],
        axis=0,
    )
    bias_ref[...] = jnp.broadcast_to(sums, bias_ref.shape)


def attention_backward(qkv, logsum, grad, head_width):
    length = qkv.shape[1]
    heads = qkv.shape[0] // (3 * head_width)
    chunk = 256
    return pl.pallas_call(
        functools.partial(attention_back_kernel, chunk, head_width),
        grid=(heads,),
        in_specs=[
            pl.BlockSpec((3 * head_width, length), lambda head: (head, 0)),
            pl.BlockSpec((1, 1, length), lambda head: (head, 0, 0)),
            pl.BlockSpec((head_width, length), lambda head: (head, 0)),
        ],
        out_specs=[
            pl.BlockSpec((3 * head_width, length), lambda head: (head, 0)),
            pl.BlockSpec((3 * head_width, 128), lambda head: (head, 0)),
        ],
        out_shape=[
            jax.ShapeDtypeStruct(qkv.shape, half),
            jax.ShapeDtypeStruct((qkv.shape[0], 128), wide),
        ],
        compiler_params=params(),
        cost_estimate=pl.CostEstimate(
            flops=40 * heads * length * length * head_width,
            bytes_accessed=qkv.size * 5,
            transcendentals=heads * length * length,
        ),
        name="attention_backward",
    )(qkv, logsum, grad)


def gate(value, *before):
    return lax.optimization_barrier((value,) + before)[0]


AXES = ("fsdp", "tensor")


class Layout:
    def __init__(self, local_heads, local_seqs):
        self.fsdp = lax.axis_size("fsdp")
        self.tensor = lax.axis_size("tensor")
        self.seqs = local_seqs
        self.core = 2 if local_heads % 2 == 0 and self.fsdp % 2 == 0 else 1
        self.outer = self.fsdp // self.core
        self.high = self.core * local_seqs
        self.low = self.tensor // self.high
        self.fsdp_index = lax.axis_index("fsdp")
        self.outer_index = self.fsdp_index // self.core
        self.core_index = self.fsdp_index % self.core
        self.high_index = lax.axis_index("tensor") // self.low

    def send(self, value, target):
        pairs = []
        for outer in range(self.outer):
            for core in range(self.core):
                for high in range(self.high):
                    for low in range(self.low):
                        o, c, h, l = target(outer, core, high, low)
                        source_id = (outer * self.core + core) * self.tensor + high * self.low + low
                        target_id = (o * self.core + c) * self.tensor + h * self.low + l
                        pairs.append((source_id, target_id))
        return lax.ppermute(value, AXES, pairs)

    def swap_core(self, value):
        return self.send(value, lambda o, c, h, l: (o, 1 - c, h, l))

    def to_low(self, value, step):
        return self.send(value, lambda o, c, h, l: (o, c, h, (l + step) % self.low))

    def to_high(self, value, step):
        return self.send(value, lambda o, c, h, l: (o, c, (h + step) % self.high, l))

    def to_outer(self, value, step):
        return self.send(value, lambda o, c, h, l: ((o + step) % self.outer, c, h, l))

    def to_sequence(self, blocks):
        within = self.high_index % self.seqs
        return [
            self.send(
                lax.dynamic_index_in_dim(blocks, (within + k) % self.seqs, 0, keepdims=False),
                lambda o, c, h, l, k=k: (
                    o,
                    h // self.seqs,
                    c * self.seqs + (h % self.seqs + k) % self.seqs,
                    l,
                ),
            )
            for k in range(self.seqs)
        ]

    def from_sequence(self, pieces):
        within = self.high_index % self.seqs
        back = []
        for k in range(self.seqs):
            back.append(
                self.send(
                    pieces[k],
                    lambda o, c, h, l, k=k: (
                        o,
                        h // self.seqs,
                        c * self.seqs + (h % self.seqs - k) % self.seqs,
                        l,
                    ),
                )
            )
        if self.seqs == 2:
            return jnp.where(within == 0, jnp.stack(back), jnp.stack(back[::-1]))
        stacked = jnp.stack(back)
        order = (jnp.arange(self.seqs) - within) % self.seqs
        return jnp.take(stacked, order, axis=0)

    def share(self, own):
        far = [self.to_low(own, -step) for step in range(1, self.low)]
        near = [own]
        if self.core == 2:
            near.append(self.swap_core(own))
            far += [self.swap_core(piece) for piece in far]
        return jnp.concatenate(near, axis=0), jnp.concatenate(far, axis=0)

    def start_reduce(self, parts):
        total = parts[0]
        if self.core == 2:
            total = total + self.swap_core(parts[1]).astype(wide)
        total = total.astype(half)
        count = total.shape[0] // (self.low - 1)
        return [
            self.to_low(total[(step - 1) * count : step * count], step)
            for step in range(1, self.low)
        ]

    def finish_reduce(self, parts, received):
        total = parts[0]
        if self.core == 2:
            total = total + self.swap_core(parts[1]).astype(wide)
        for piece in received:
            total = total + piece.astype(wide)
        return total

    def ordered(self, index, parts, axis):
        count = len(parts)
        if count == 1:
            return parts[0]
        if count == 2:
            return jnp.where(
                index == 0,
                jnp.concatenate(parts, axis=axis),
                jnp.concatenate(parts[::-1], axis=axis),
            )
        width = parts[0].shape[axis]
        shape = list(parts[0].shape)
        shape[axis] = width * count
        result = jnp.zeros(shape, parts[0].dtype)
        for step, part in enumerate(parts):
            result = lax.dynamic_update_slice_in_dim(
                result, part, ((index + step) % count) * width, axis
            )
        return result

    def core_rows(self, rows, core):
        count = rows.shape[0] // self.core
        return lax.dynamic_slice_in_dim(rows, core * count, count, 0)

    def pair_weights(self, matrices, extra=None):
        def pack(core):
            rows = [self.core_rows(matrix, core) for matrix in matrices]
            if extra is not None:
                rows.append(extra)
            return jnp.concatenate(rows, axis=0)

        if self.core == 1:
            return pack(0)
        other = self.swap_core(pack(1 - self.core_index))
        return self.ordered(self.core_index, [pack(self.core_index), other], 1)

    def high_weights(self, rows):
        return [rows] + [self.to_high(rows, -step) for step in range(1, self.high)]

    def outer_weights(self, column):
        return [
            [rows] + [self.to_outer(rows, -step) for step in range(1, self.outer)]
            for rows in column
        ]

    def rows_of(self, gathered, first, count):
        return jnp.concatenate(
            [
                self.ordered(self.outer_index, [part[first : first + count] for part in parts], 1)
                for parts in gathered
            ],
            axis=0,
        )

    def scatter_outer(self, grads):
        width = grads[0].shape[1] // self.outer

        def columns(grad, place):
            return lax.dynamic_slice_in_dim(grad, (place % self.outer) * width, width, 1)

        received = [
            [
                self.to_outer(columns(grad, self.outer_index + step).astype(half), step)
                for step in range(1, self.outer)
            ]
            for grad in grads
        ]
        sums = []
        for grad, parts in zip(grads, received):
            total = columns(grad, self.outer_index).astype(wide)
            for part in parts:
                total = total + part.astype(wide)
            sums.append(total)
        return sums

    def scatter_high(self, sums):
        received = [
            self.to_high(sums[step].astype(half), step) for step in range(1, self.high)
        ]
        total = sums[0]
        for part in received:
            total = total + part.astype(wide)
        return total

    def scatter_core(self, column):
        if self.core == 1:
            return [column]
        width = column.shape[1] // self.core
        mine = lax.dynamic_slice_in_dim(column, self.core_index * width, width, 1)
        other = self.swap_core(
            lax.dynamic_slice_in_dim(column, (1 - self.core_index) * width, width, 1)
        )
        first = self.core_index == 0
        return [jnp.where(first, mine, other), jnp.where(first, other, mine)]

    def total(self, value):
        if self.core == 2:
            value = value + self.swap_core(value)
        bit = 1
        while bit < self.low:
            value = value + self.send(value, lambda o, c, h, l: (o, c, h, l ^ bit))
            bit *= 2
        bit = 1
        while bit < self.outer:
            value = value + self.send(value, lambda o, c, h, l: (o ^ bit, c, h, l))
            bit *= 2
        bit = 1
        while bit < self.high:
            value = value + self.send(value, lambda o, c, h, l: (o, c, h ^ bit, l))
            bit *= 2
        return value


SMALL_ROWS = 16


def pad_columns(rows, width):
    return jnp.pad(rows, [(0, 0)] * (rows.ndim - 1) + [(0, width - rows.shape[-1])])


def per_device(
    layer_input,
    cotangent,
    attn_weight,
    attn_bias,
    out_weight,
    up_weight,
    up_bias,
    down_weight,
    norm_gains,
    norm_shifts,
    attn_weight_moments,
    attn_bias_moments,
    out_weight_moments,
    up_weight_moments,
    up_bias_moments,
    down_weight_moments,
    norm_gains_moments,
    norm_shifts_moments,
):
    local_heads = attn_bias.shape[0]
    local_seqs, block_tokens, model_width = layer_input.shape
    lay = Layout(local_heads, local_seqs)
    fsdp, core, high = lay.fsdp, lay.core, lay.high
    bias_width = attn_bias.shape[1]
    head_width = bias_width * fsdp // 3
    part_heads = local_heads // core
    shard_width = model_width // fsdp
    hidden_part = up_bias.shape[0]
    own_tokens = local_seqs * block_tokens
    near_tokens = core * own_tokens
    far_tokens = near_tokens * (lay.low - 1)
    near_other = near_tokens - near_tokens // core
    far_other = far_tokens - far_tokens // core
    weights = (
        attn_weight,
        attn_bias,
        out_weight,
        up_weight,
        up_bias,
        down_weight,
        norm_gains,
        norm_shifts,
    )

    tokens = jnp.concatenate(lay.to_sequence(layer_input), axis=0)
    small = jnp.concatenate(
        [
            norm_gains.astype(half),
            norm_shifts.astype(half),
            pad_columns(attn_bias.astype(half).reshape(1, -1), shard_width),
            pad_columns(up_bias.astype(half).reshape(1, -1), shard_width),
            jnp.zeros((SMALL_ROWS - 8, shard_width), half),
        ],
        axis=0,
    )
    attn_rows = part_heads * 3 * head_width
    out_rows = part_heads * head_width
    hidden_rows = up_weight.shape[1] // core
    column = lay.high_weights(
        lay.pair_weights([attn_weight.astype(half).T, out_weight.astype(half)], small)
    )
    gathered = lay.outer_weights(column)
    w_attn = lay.rows_of(gathered, 0, attn_rows)
    w_output = lay.rows_of(gathered, attn_rows, out_rows)
    small = lay.rows_of(gathered, attn_rows + out_rows, SMALL_ROWS)
    small = small.reshape(high, SMALL_ROWS, model_width)
    gain_rows = small[0, 0:2].astype(wide)
    shift_rows = small[0, 2:6].astype(wide)
    b_attn = small[:, 6].reshape(high, fsdp, shard_width)[:, :, : local_heads * bias_width]
    b_attn = b_attn.reshape(high, fsdp, core, part_heads, bias_width)
    b_attn = lax.dynamic_index_in_dim(b_attn, lay.core_index, 2, keepdims=False)
    b_attn = jnp.transpose(b_attn, (0, 2, 1, 3)).reshape(-1, 1).astype(wide)
    b_upward = small[:, 7].reshape(high, fsdp, shard_width)[:, :, :hidden_part]
    b_upward = b_upward.reshape(high, core, (fsdp // core) * hidden_part)
    b_upward = lax.dynamic_index_in_dim(b_upward, lay.core_index, 1, keepdims=False)
    b_upward = b_upward.reshape(1, -1).astype(wide)

    near, far = lay.share(tokens)
    tokens_full = jnp.concatenate([near, far], axis=0)
    second = lay.pair_weights([up_weight.astype(half).T, down_weight.astype(half)])
    second = lay.high_weights(gate(second, tokens, *column))
    upward = lay.to_sequence(gate(cotangent, *second))
    upward = jnp.concatenate(upward, axis=0).astype(wide)
    gathered = lay.outer_weights(second)
    w_upward = lay.rows_of(gathered, 0, hidden_rows)
    w_downward = lay.rows_of(gathered, hidden_rows, hidden_rows)

    qkv = (times_t(w_attn, tokens_full) + b_attn).astype(half)
    attn_far, log_far, *parts_far = attention_forward(
        qkv, w_output, near_tokens, far_tokens, far_other, head_width
    )
    received = lay.start_reduce(parts_far)
    attn_near, log_near, *parts_near = attention_forward(
        qkv, w_output, 0, near_tokens, near_other, head_width
    )
    logsum = jnp.concatenate([log_near, log_far], axis=2)
    attn_out = lay.finish_reduce(parts_near, received)
    resid_one = attn_out + shift_rows[0] + tokens.astype(wide)
    hidden_one, normed_one, spread_one = layer_norm(resid_one, gain_rows[0], shift_rows[1])
    hidden_near, hidden_far = lay.share(hidden_one.astype(half))
    active_far, slope_far, *parts_far = ffn_forward(
        hidden_far, w_upward, b_upward, w_downward, far_other
    )
    received = lay.start_reduce(parts_far)
    active_near, slope_near, *parts_near = ffn_forward(
        hidden_near, w_upward, b_upward, w_downward, near_other
    )
    ffn_out = lay.finish_reduce(parts_near, received)
    resid_two = ffn_out + shift_rows[2] + hidden_one
    result, normed_two, spread_two = layer_norm(resid_two, gain_rows[1], shift_rows[3])

    grad_two = norm_back(upward, gain_rows[1], normed_two, spread_two)
    grad_near, grad_far = lay.share(grad_two.astype(half))
    output = result.astype(half).reshape(local_seqs, block_tokens, model_width)
    outputs = lay.from_sequence(output)
    inner_far, up_far, *parts_far = ffn_backward(
        grad_far, slope_far, w_downward, w_upward, far_other
    )
    received = lay.start_reduce(parts_far)
    inner_near, up_near, *parts_near = ffn_backward(
        grad_near, slope_near, w_downward, w_upward, near_other
    )
    grad_down = t_times(active_near, grad_near) + t_times(active_far, grad_far)
    grad_upward = t_times(inner_near, hidden_near) + t_times(inner_far, hidden_far)
    grad_hidden = grad_two + lay.finish_reduce(parts_near, received)
    grad_one = norm_back(grad_hidden, gain_rows[0], normed_one, spread_one)
    second_grads = [
        jnp.concatenate(
            [
                grad_upward[place * hidden_rows : (place + 1) * hidden_rows],
                grad_down[place * hidden_rows : (place + 1) * hidden_rows],
            ],
            axis=0,
        )
        for place in range(high)
    ]
    second_sums = lay.scatter_outer(second_grads)
    one_near, one_far = lay.share(grad_one.astype(half))
    one_full = jnp.concatenate([one_near, one_far], axis=0)
    grad_attn = times_t(w_output, one_full).astype(half)
    grad_qkv, bias_sums = attention_backward(qkv, logsum, grad_attn, head_width)
    grad_far_qkv = grad_qkv[:, near_tokens:]
    far_mine = t_times(grad_far_qkv[:, : far_tokens - far_other], w_attn)
    parts_far = [far_mine]
    parts_near = [t_times(grad_qkv[:, : near_tokens - near_other], w_attn)]
    if core == 2:
        parts_far.append(t_times(grad_far_qkv[:, far_tokens - far_other :], w_attn).astype(half))
        parts_near.append(
            t_times(grad_qkv[:, near_tokens - near_other : near_tokens], w_attn).astype(half)
        )
    received = lay.start_reduce(parts_far)
    input_grad = grad_one + lay.finish_reduce(parts_near, received)
    input_grads = lay.from_sequence(
        input_grad.astype(half).reshape(local_seqs, block_tokens, model_width)
    ).astype(wide)
    grad_attn_w = times(grad_qkv, tokens_full)
    grad_output = times(attn_near, one_near) + times(attn_far, one_far)

    norm_sums = lay.total(
        jnp.stack(
            [
                jnp.sum(grad_hidden * normed_one, axis=0),
                jnp.sum(upward * normed_two, axis=0),
                jnp.sum(grad_one, axis=0),
                jnp.sum(grad_hidden, axis=0),
                jnp.sum(grad_two, axis=0),
                jnp.sum(upward, axis=0),
            ]
        )
    )
    norm_sums = lax.dynamic_slice_in_dim(norm_sums, lay.fsdp_index * shard_width, shard_width, 1)
    core_here = jnp.arange(core) == lay.core_index
    bias_sums = bias_sums[:, 0].reshape(high, part_heads, fsdp, bias_width)
    bias_sums = jnp.transpose(bias_sums, (0, 2, 1, 3))[:, :, None]
    bias_sums = jnp.where(core_here[:, None, None], bias_sums, 0.0)
    bias_sums = pad_columns(bias_sums.reshape(high, fsdp, -1), shard_width)
    up_sums = (up_near + up_far).reshape(high, 1, (fsdp // core) * hidden_part)
    up_sums = jnp.where(core_here[:, None], up_sums, 0.0)
    up_sums = pad_columns(up_sums.reshape(high, fsdp, hidden_part), shard_width)
    small_sums = jnp.pad(
        jnp.stack([bias_sums.reshape(high, -1), up_sums.reshape(high, -1)], axis=1),
        ((0, 0), (0, SMALL_ROWS - 2), (0, 0)),
    )
    second_sums = [gate(part, grad_qkv) for part in second_sums]
    second_shards = lay.scatter_core(lay.scatter_high(second_sums))
    up_shard = jnp.concatenate([part[:hidden_rows] for part in second_shards], axis=0).T
    down_shard = jnp.concatenate([part[hidden_rows:] for part in second_shards], axis=0)
    first_grads = [
        jnp.concatenate(
            [
                grad_attn_w[place * attn_rows : (place + 1) * attn_rows],
                grad_output[place * out_rows : (place + 1) * out_rows],
                small_sums[place],
            ],
            axis=0,
        )
        for place in range(high)
    ]
    first_shards = lay.scatter_core(lay.scatter_high(lay.scatter_outer(first_grads)))
    attn_shard = jnp.concatenate([part[:attn_rows] for part in first_shards], axis=0).T
    out_shard = jnp.concatenate(
        [part[attn_rows : attn_rows + out_rows] for part in first_shards], axis=0
    )
    small_shard = sum(part[attn_rows + out_rows :] for part in first_shards)
    grads = (
        attn_shard,
        small_shard[0, : local_heads * bias_width].reshape(local_heads, bias_width),
        out_shard,
        up_shard,
        small_shard[1, :hidden_part],
        down_shard,
        norm_sums[0:2],
        norm_sums[2:6],
    )
    moments = (
        attn_weight_moments,
        attn_bias_moments,
        out_weight_moments,
        up_weight_moments,
        up_bias_moments,
        down_weight_moments,
        norm_gains_moments,
        norm_shifts_moments,
    )
    rates = (
        matrix_rate,
        vector_rate,
        output_rate,
        matrix_rate,
        vector_rate,
        matrix_rate,
        vector_rate,
        vector_rate,
    )
    decays = (decay_rate, 0.0, decay_rate, decay_rate, 0.0, decay_rate, 0.0, 0.0)
    updated = [
        adamw_update(weights[place], moments[place], grads[place], rates[place], decays[place])
        for place in range(8)
    ]
    new_weights = tuple((pair[0] for pair in updated))
    new_moments = tuple((pair[1] for pair in updated))
    return (outputs, input_grads) + grads + new_weights + new_moments


def solution(mesh):
    return jax.shard_map(
        per_device,
        mesh=mesh,
        in_specs=(
            P("fsdp", "tensor", None),
            P("fsdp", "tensor", None),
            P("fsdp", "tensor"),
            P("tensor", "fsdp"),
            P("tensor", "fsdp"),
            P("fsdp", "tensor"),
            P(("tensor", "fsdp")),
            P("tensor", "fsdp"),
            P(None, "fsdp"),
            P(None, "fsdp"),
            P(None, "fsdp", "tensor"),
            P(None, "tensor", "fsdp"),
            P(None, "tensor", "fsdp"),
            P(None, "fsdp", "tensor"),
            P(None, ("tensor", "fsdp")),
            P(None, "tensor", "fsdp"),
            P(None, None, "fsdp"),
            P(None, None, "fsdp"),
        ),
        out_specs=(
            P("fsdp", "tensor", None),
            P("fsdp", "tensor", None),
            P("fsdp", "tensor"),
            P("tensor", "fsdp"),
            P("tensor", "fsdp"),
            P("fsdp", "tensor"),
            P(("tensor", "fsdp")),
            P("tensor", "fsdp"),
            P(None, "fsdp"),
            P(None, "fsdp"),
            P("fsdp", "tensor"),
            P("tensor", "fsdp"),
            P("tensor", "fsdp"),
            P("fsdp", "tensor"),
            P(("tensor", "fsdp")),
            P("tensor", "fsdp"),
            P(None, "fsdp"),
            P(None, "fsdp"),
            P(None, "fsdp", "tensor"),
            P(None, "tensor", "fsdp"),
            P(None, "tensor", "fsdp"),
            P(None, "fsdp", "tensor"),
            P(None, ("tensor", "fsdp")),
            P(None, "tensor", "fsdp"),
            P(None, None, "fsdp"),
            P(None, None, "fsdp"),
        ),
        check_vma=False,
    )
```

```python
import functools

import jax
import jax.numpy as jnp
from jax import lax
from jax.experimental import pallas as pl
from jax.experimental.pallas import tpu as pltpu
from jax.sharding import PartitionSpec as P

norm_eps = 1e-05
beta_one = 0.9
beta_two = 0.999
adam_eps = 1e-08
adam_step = 4.0
matrix_rate = 0.01
output_rate = 0.1
vector_rate = 0.1
decay_rate = 0.1
inv_root_two = 0.7071067811865476
inv_root_tau = 0.3989422804014327


def layer_norm(resid, gain_row, shift_row):
    center = resid - jnp.mean(resid, axis=-1, keepdims=True)
    spread = lax.rsqrt(jnp.mean(center * center, axis=-1, keepdims=True) + norm_eps)
    normed = center * spread
    return (normed * gain_row + shift_row, normed, spread)


def norm_back(grad_out, gain_row, normed, spread):
    scaled = grad_out * gain_row
    return spread * (
        scaled
        - jnp.mean(scaled, axis=-1, keepdims=True)
        - normed * jnp.mean(scaled * normed, axis=-1, keepdims=True)
    )


def gelu_value(inner):
    return inner * 0.5 * (1.0 + jax.scipy.special.erf(inner * inv_root_two))


def gelu_slope(inner):
    return (
        0.5 * (1.0 + jax.scipy.special.erf(inner * inv_root_two))
        + inner * jnp.exp(-0.5 * inner * inner) * inv_root_tau
    )


def adamw_update(weight, moments, grad, rate, decay):
    first_moment = beta_one * moments[0] + (1.0 - beta_one) * grad
    second_moment = beta_two * moments[1] + (1.0 - beta_two) * grad * grad
    direction = (
        first_moment
        / (1.0 - beta_one**adam_step)
        / (jnp.sqrt(second_moment / (1.0 - beta_two**adam_step)) + adam_eps)
    )
    return (weight - rate * (direction + decay * weight), jnp.stack([first_moment, second_moment]))


half = jnp.bfloat16
wide = jnp.float32
VMEM_BYTES = 40 * 1024 * 1024


def times(left, right):
    return lax.dot_general(left, right, (((1,), (0,)), ((), ())), preferred_element_type=wide)


def times_t(left, right):
    return lax.dot_general(left, right, (((1,), (1,)), ((), ())), preferred_element_type=wide)


def t_times(left, right):
    return lax.dot_general(left, right, (((0,), (0,)), ((), ())), preferred_element_type=wide)


def whole_block(*shape):
    return pl.BlockSpec(shape, lambda step: (0,) * len(shape))


def sum_shapes(rows, other, width):
    shapes = [jax.ShapeDtypeStruct((rows - other, width), wide)]
    if other:
        shapes.append(jax.ShapeDtypeStruct((other, width), half))
    return shapes, [whole_block(*shape.shape) for shape in shapes]


def write_sums(total, refs):
    mine = refs[0].shape[0]
    refs[0][...] = total[:mine]
    if len(refs) > 1:
        refs[1][...] = total[mine:].astype(half)


def params():
    return pltpu.CompilerParams(
        dimension_semantics=("arbitrary",), vmem_limit_bytes=VMEM_BYTES
    )


def up_kernel(x_ref, up_ref, bias_ref, down_ref, active_ref, slope_ref, *rest):
    sums, total = rest[:-1], rest[-1]
    inner = times_t(x_ref[...], up_ref[...]) + bias_ref[...]
    chance = 0.5 * (1.0 + lax.erf(inner * inv_root_two))
    active = (inner * chance).astype(half)
    active_ref[...] = active
    slope_ref[...] = chance + inner * jnp.exp(-0.5 * inner * inner) * inv_root_tau
    part = times(active, down_ref[...])
    step = pl.program_id(0)

    @pl.when(step == 0)
    def _():
        total[...] = part

    @pl.when(step > 0)
    def _():
        total[...] += part

    @pl.when(step == pl.num_programs(0) - 1)
    def _():
        write_sums(total[...], sums)


def ffn_forward(x, w_upward, b_upward, w_downward, other):
    rows, width = x.shape
    hidden = w_upward.shape[0]
    tile = 256
    shapes, specs = sum_shapes(rows, other, width)
    return pl.pallas_call(
        up_kernel,
        grid=(hidden // tile,),
        in_specs=[
            whole_block(rows, width),
            pl.BlockSpec((tile, width), lambda step: (step, 0)),
            pl.BlockSpec((1, tile), lambda step: (0, step)),
            pl.BlockSpec((tile, width), lambda step: (step, 0)),
        ],
        out_specs=[
            pl.BlockSpec((rows, tile), lambda step: (0, step)),
            pl.BlockSpec((rows, tile), lambda step: (0, step)),
        ]
        + specs,
        out_shape=[
            jax.ShapeDtypeStruct((rows, hidden), half),
            jax.ShapeDtypeStruct((rows, hidden), wide),
        ]
        + shapes,
        scratch_shapes=[pltpu.VMEM((rows, width), wide)],
        compiler_params=params(),
        cost_estimate=pl.CostEstimate(
            flops=4 * rows * width * hidden,
            bytes_accessed=rows * hidden * 6 + hidden * width * 4,
            transcendentals=2 * rows * hidden,
        ),
        name="ffn_forward",
    )(x, w_upward, b_upward, w_downward)


def down_kernel(grad_ref, slope_ref, down_ref, up_ref, inner_ref, bias_ref, *rest):
    sums, total = rest[:-1], rest[-1]
    grad_inner = times_t(grad_ref[...], down_ref[...]) * slope_ref[...]
    bias_ref[...] = jnp.sum(grad_inner, axis=0, keepdims=True)
    grad_inner_b = grad_inner.astype(half)
    inner_ref[...] = grad_inner_b
    part = times(grad_inner_b, up_ref[...])
    step = pl.program_id(0)

    @pl.when(step == 0)
    def _():
        total[...] = part

    @pl.when(step > 0)
    def _():
        total[...] += part

    @pl.when(step == pl.num_programs(0) - 1)
    def _():
        write_sums(total[...], sums)


def ffn_backward(grad, slope, w_downward, w_upward, other):
    rows, width = grad.shape
    hidden = w_upward.shape[0]
    tile = 256
    shapes, specs = sum_shapes(rows, other, width)
    return pl.pallas_call(
        down_kernel,
        grid=(hidden // tile,),
        in_specs=[
            whole_block(rows, width),
            pl.BlockSpec((rows, tile), lambda step: (0, step)),
            pl.BlockSpec((tile, width), lambda step: (step, 0)),
            pl.BlockSpec((tile, width), lambda step: (step, 0)),
        ],
        out_specs=[
            pl.BlockSpec((rows, tile), lambda step: (0, step)),
            pl.BlockSpec((1, tile), lambda step: (0, step)),
        ]
        + specs,
        out_shape=[
            jax.ShapeDtypeStruct((rows, hidden), half),
            jax.ShapeDtypeStruct((1, hidden), wide),
        ]
        + shapes,
        scratch_shapes=[pltpu.VMEM((rows, width), wide)],
        compiler_params=params(),
        cost_estimate=pl.CostEstimate(
            flops=4 * rows * width * hidden,
            bytes_accessed=rows * hidden * 6 + hidden * width * 4,
            transcendentals=0,
        ),
        name="ffn_backward",
    )(grad, slope, w_downward, w_upward)


def attention_kernel(first, chunk, head_width, qkv_ref, out_ref, attn_ref, log_ref, *rest):
    sums, mixed = rest[:-1], rest[-1]
    head = pl.program_id(0)
    scale = head_width ** (-0.5)
    keys = jnp.transpose(qkv_ref[head_width : 2 * head_width, :])
    values = qkv_ref[2 * head_width : 3 * head_width, :]
    count = attn_ref.shape[1]
    for start in range(0, count, chunk):
        here = slice(first + start, first + start + chunk)
        scores = times(keys, qkv_ref[0:head_width, here]) * scale
        top = jnp.max(scores, axis=0, keepdims=True)
        powers = jnp.exp(scores - top)
        norm = jnp.sum(powers, axis=0, keepdims=True)
        weights = (powers * (1.0 / norm)).astype(half)
        log_ref[0, :, start : start + chunk] = top + jnp.log(norm)
        block = times(values, weights).astype(half)
        attn_ref[:, start : start + chunk] = block
        mixed[pl.ds(pl.multiple_of(head * head_width, head_width), head_width), pl.ds(start, chunk)] = block

    @pl.when(head == pl.num_programs(0) - 1)
    def _():
        write_sums(t_times(mixed[...], out_ref[...]), sums)


def attention_forward(qkv, w_output, first, count, other, head_width):
    length = qkv.shape[1]
    heads = qkv.shape[0] // (3 * head_width)
    width = w_output.shape[1]
    chunk = 256 if count % 256 == 0 else 128
    shapes, specs = sum_shapes(count, other, width)
    return pl.pallas_call(
        functools.partial(attention_kernel, first, chunk, head_width),
        grid=(heads,),
        in_specs=[
            pl.BlockSpec((3 * head_width, length), lambda head: (head, 0)),
            whole_block(heads * head_width, width),
        ],
        out_specs=[
            pl.BlockSpec((head_width, count), lambda head: (head, 0)),
            pl.BlockSpec((1, 1, count), lambda head: (head, 0, 0)),
        ]
        + specs,
        out_shape=[
            jax.ShapeDtypeStruct((heads * head_width, count), half),
            jax.ShapeDtypeStruct((heads, 1, count), wide),
        ]
        + shapes,
        scratch_shapes=[pltpu.VMEM((heads * head_width, count), half)],
        compiler_params=params(),
        cost_estimate=pl.CostEstimate(
            flops=16 * heads * count * length * head_width,
            bytes_accessed=qkv.size * 2 + count * width * 6,
            transcendentals=heads * count * length,
        ),
        name="attention_forward",
    )(qkv, w_output)


def attention_back_kernel(chunk, head_width, qkv_ref, log_ref, grad_ref, out_ref, bias_ref):
    scale = head_width ** (-0.5)
    key_rows = qkv_ref[head_width : 2 * head_width, :]
    keys = jnp.transpose(key_rows)
    values = jnp.transpose(qkv_ref[2 * head_width : 3 * head_width, :])
    length = keys.shape[0]
    grad_keys = jnp.zeros((length, head_width), wide)
    grad_values = jnp.zeros((length, head_width), wide)
    query_sum = jnp.zeros((head_width, 1), wide)
    for start in range(0, length, chunk):
        here = slice(start, start + chunk)
        queries = qkv_ref[0:head_width, here]
        grads = grad_ref[:, here]
        scores = times(keys, queries) * scale
        chances = jnp.exp(scores - log_ref[0, :, here])
        grad_scores = times(values, grads)
        mean = jnp.sum(chances * grad_scores, axis=0, keepdims=True)
        logits = (chances * (grad_scores - mean)).astype(half)
        grad_values = grad_values + times(chances.astype(half), jnp.transpose(grads))
        grad_keys = grad_keys + times(logits, jnp.transpose(queries))
        grad_query = times(key_rows, logits) * scale
        out_ref[0:head_width, here] = grad_query.astype(half)
        query_sum = query_sum + jnp.sum(grad_query, axis=1, keepdims=True)
    grad_keys = jnp.transpose(grad_keys) * scale
    grad_values = jnp.transpose(grad_values)
    out_ref[head_width : 2 * head_width, :] = grad_keys.astype(half)
    out_ref[2 * head_width : 3 * head_width, :] = grad_values.astype(half)
    sums = jnp.concatenate(
        [
            query_sum,
            jnp.sum(grad_keys, axis=1, keepdims=True),
            jnp.sum(grad_values, axis=1, keepdims=True),
        ],
        axis=0,
    )
    bias_ref[...] = jnp.broadcast_to(sums, bias_ref.shape)


def attention_backward(qkv, logsum, grad, head_width):
    length = qkv.shape[1]
    heads = qkv.shape[0] // (3 * head_width)
    chunk = 256
    return pl.pallas_call(
        functools.partial(attention_back_kernel, chunk, head_width),
        grid=(heads,),
        in_specs=[
            pl.BlockSpec((3 * head_width, length), lambda head: (head, 0)),
            pl.BlockSpec((1, 1, length), lambda head: (head, 0, 0)),
            pl.BlockSpec((head_width, length), lambda head: (head, 0)),
        ],
        out_specs=[
            pl.BlockSpec((3 * head_width, length), lambda head: (head, 0)),
            pl.BlockSpec((3 * head_width, 128), lambda head: (head, 0)),
        ],
        out_shape=[
            jax.ShapeDtypeStruct(qkv.shape, half),
            jax.ShapeDtypeStruct((qkv.shape[0], 128), wide),
        ],
        compiler_params=params(),
        cost_estimate=pl.CostEstimate(
            flops=40 * heads * length * length * head_width,
            bytes_accessed=qkv.size * 5,
            transcendentals=heads * length * length,
        ),
        name="attention_backward",
    )(qkv, logsum, grad)


def update_kernel(plan, core_count, core_ref, *refs):
    parts, refs = refs[:core_count], refs[core_count:]
    inputs, outputs = refs[: 2 * len(plan)], refs[2 * len(plan) :]
    first = 0
    for index, (rows, flip, rate) in enumerate(plan):
        weight_ref, pair_ref = inputs[2 * index : 2 * index + 2]
        grad_ref, new_ref, moments_ref = outputs[3 * index : 3 * index + 3]
        blocks = [part[first : first + rows, :] for part in parts]
        if core_count == 2:
            lead = core_ref[0] == 0
            blocks = [
                jnp.where(lead, blocks[0], blocks[1]),
                jnp.where(lead, blocks[1], blocks[0]),
            ]
        grad = jnp.concatenate(blocks, axis=0)
        if flip:
            grad = jnp.transpose(grad)
        first += rows
        weight = weight_ref[...]
        first_moment = beta_one * pair_ref[0] + (1.0 - beta_one) * grad
        second_moment = beta_two * pair_ref[1] + (1.0 - beta_two) * grad * grad
        direction = (
            first_moment
            / (1.0 - beta_one**adam_step)
            / (jnp.sqrt(second_moment / (1.0 - beta_two**adam_step)) + adam_eps)
        )
        grad_ref[...] = grad
        new_ref[...] = weight - rate * (direction + decay_rate * weight)
        moments_ref[0] = first_moment
        moments_ref[1] = second_moment


def update_matrices(core_index, parts, matrices):
    plan, operands, shapes = [], [], []
    for weight, pair, flip, rate in matrices:
        rows = weight.shape[1 if flip else 0] // len(parts)
        plan.append((rows, flip, rate))
        operands += [weight, pair]
        shapes += [weight.shape, weight.shape, pair.shape]
    used = sum(rows for rows, _, _ in plan)
    results = pl.pallas_call(
        functools.partial(update_kernel, tuple(plan), len(parts)),
        grid=(1,),
        in_specs=[pl.BlockSpec(memory_space=pltpu.SMEM)]
        + [whole_block(used, part.shape[1]) for part in parts]
        + [whole_block(*operand.shape) for operand in operands],
        out_specs=[whole_block(*shape) for shape in shapes],
        out_shape=[jax.ShapeDtypeStruct(shape, wide) for shape in shapes],
        compiler_params=params(),
        cost_estimate=pl.CostEstimate(
            flops=20 * sum(weight.size for weight, _, _, _ in matrices),
            bytes_accessed=32 * sum(weight.size for weight, _, _, _ in matrices),
            transcendentals=0,
        ),
        name="adamw",
    )(jnp.reshape(core_index, (1,)).astype(jnp.int32), *[part[:used] for part in parts], *operands)
    return [tuple(results[3 * index : 3 * index + 3]) for index in range(len(plan))]


def gate(value, *before):
    return lax.optimization_barrier((value,) + before)[0]


AXES = ("fsdp", "tensor")


class Layout:
    def __init__(self, local_heads, local_seqs):
        self.fsdp = lax.axis_size("fsdp")
        self.tensor = lax.axis_size("tensor")
        self.seqs = local_seqs
        self.core = 2 if local_heads % 2 == 0 and self.fsdp % 2 == 0 else 1
        self.outer = self.fsdp // self.core
        self.high = self.core * local_seqs
        self.low = self.tensor // self.high
        self.fsdp_index = lax.axis_index("fsdp")
        self.outer_index = self.fsdp_index // self.core
        self.core_index = self.fsdp_index % self.core
        self.high_index = lax.axis_index("tensor") // self.low

    def send(self, value, target):
        pairs = []
        for outer in range(self.outer):
            for core in range(self.core):
                for high in range(self.high):
                    for low in range(self.low):
                        o, c, h, l = target(outer, core, high, low)
                        source_id = (outer * self.core + core) * self.tensor + high * self.low + low
                        target_id = (o * self.core + c) * self.tensor + h * self.low + l
                        pairs.append((source_id, target_id))
        return lax.ppermute(value, AXES, pairs)

    def swap_core(self, value):
        return self.send(value, lambda o, c, h, l: (o, 1 - c, h, l))

    def to_low(self, value, step):
        return self.send(value, lambda o, c, h, l: (o, c, h, (l + step) % self.low))

    def to_high(self, value, step):
        return self.send(value, lambda o, c, h, l: (o, c, (h + step) % self.high, l))

    def to_outer(self, value, step):
        return self.send(value, lambda o, c, h, l: ((o + step) % self.outer, c, h, l))

    def to_sequence(self, blocks):
        within = self.high_index % self.seqs
        return [
            self.send(
                lax.dynamic_index_in_dim(blocks, (within + k) % self.seqs, 0, keepdims=False),
                lambda o, c, h, l, k=k: (
                    o,
                    h // self.seqs,
                    c * self.seqs + (h % self.seqs + k) % self.seqs,
                    l,
                ),
            )
            for k in range(self.seqs)
        ]

    def from_sequence(self, pieces):
        within = self.high_index % self.seqs
        back = []
        for k in range(self.seqs):
            back.append(
                self.send(
                    pieces[k],
                    lambda o, c, h, l, k=k: (
                        o,
                        h // self.seqs,
                        c * self.seqs + (h % self.seqs - k) % self.seqs,
                        l,
                    ),
                )
            )
        if self.seqs == 2:
            return jnp.where(within == 0, jnp.stack(back), jnp.stack(back[::-1]))
        stacked = jnp.stack(back)
        order = (jnp.arange(self.seqs) - within) % self.seqs
        return jnp.take(stacked, order, axis=0)

    def share(self, own):
        far = [self.to_low(own, -step) for step in range(1, self.low)]
        near = [own]
        if self.core == 2:
            near.append(self.swap_core(own))
            far += [self.swap_core(piece) for piece in far]
        return jnp.concatenate(near, axis=0), jnp.concatenate(far, axis=0)

    def start_reduce(self, parts, later):
        total = parts[0]
        if self.core == 2:
            total = total + self.swap_core(parts[1]).astype(wide)
        total = total.astype(half)
        total, later = lax.optimization_barrier((total, later))
        count = total.shape[0] // (self.low - 1)
        return later, [
            self.to_low(total[(step - 1) * count : step * count], step)
            for step in range(1, self.low)
        ]

    def finish_reduce(self, parts, received):
        total = parts[0]
        if self.core == 2:
            total = total + self.swap_core(parts[1]).astype(wide)
        for piece in received:
            total = total + piece.astype(wide)
        return total

    def ordered(self, index, parts, axis):
        count = len(parts)
        if count == 1:
            return parts[0]
        if count == 2:
            return jnp.where(
                index == 0,
                jnp.concatenate(parts, axis=axis),
                jnp.concatenate(parts[::-1], axis=axis),
            )
        width = parts[0].shape[axis]
        shape = list(parts[0].shape)
        shape[axis] = width * count
        result = jnp.zeros(shape, parts[0].dtype)
        for step, part in enumerate(parts):
            result = lax.dynamic_update_slice_in_dim(
                result, part, ((index + step) % count) * width, axis
            )
        return result

    def core_rows(self, rows, core):
        count = rows.shape[0] // self.core
        return lax.dynamic_slice_in_dim(rows, core * count, count, 0)

    def pair_weights(self, matrices, extra=None):
        def pack(core):
            rows = [self.core_rows(matrix, core) for matrix in matrices]
            if extra is not None:
                rows.append(extra)
            return jnp.concatenate(rows, axis=0)

        if self.core == 1:
            return pack(0)
        other = self.swap_core(pack(1 - self.core_index))
        return self.ordered(self.core_index, [pack(self.core_index), other], 1)

    def near_high(self, rows):
        steps = sorted({1, self.high - 1})
        return {step: self.to_high(rows, -step) for step in steps}

    def far_high(self, rows):
        return {step: self.to_high(rows, -step) for step in range(2, self.high - 1)}

    def outer_weights(self, rows):
        return [rows] + [self.to_outer(rows, -step) for step in range(1, self.outer)]

    def rows_of(self, gathered, first, count):
        return jnp.concatenate(
            [
                self.ordered(self.outer_index, [part[first : first + count] for part in parts], 1)
                for parts in gathered
            ],
            axis=0,
        )

    def scatter_outer(self, grads):
        width = grads[0].shape[1] // self.outer
        rows = grads[0].shape[0]

        def columns(grad, place):
            return lax.dynamic_slice_in_dim(grad, (place % self.outer) * width, width, 1)

        cut = self.high // 2
        order = list(range(1, self.high)) + [0]
        sums, before = {}, ()
        for group in (order[:cut], order[cut:]):
            received = []
            for step in range(1, self.outer):
                parts = [columns(grads[place], self.outer_index + step) for place in group]
                block = gate(jnp.concatenate(parts, axis=0).astype(half), *before)
                received.append(self.to_outer(block, step))
            before = tuple(received)
            for index, place in enumerate(group):
                total = columns(grads[place], self.outer_index)
                for part in received:
                    total = total + part[index * rows : (index + 1) * rows].astype(wide)
                sums[place] = total
        return [sums[place] for place in range(self.high)]

    def scatter_high(self, sums, *before):
        received = [
            self.to_high(sums[step].astype(half), step) for step in range(1, self.high)
        ]
        total = gate(sums[0], *before) if before else sums[0]
        for part in received:
            total = total + part.astype(wide)
        return total

    def scatter_core(self, column):
        if self.core == 1:
            return [column]
        width = column.shape[1] // self.core
        mine = lax.dynamic_slice_in_dim(column, self.core_index * width, width, 1)
        other = self.swap_core(
            lax.dynamic_slice_in_dim(column, (1 - self.core_index) * width, width, 1)
        )
        return [mine, other]

    def total(self, value, before_low, before_outer):
        def over(value, count, target):
            bit = 1
            while bit < count:
                value = value + self.send(value, functools.partial(target, bit))
                bit *= 2
            return value

        if self.core == 2:
            value = value + self.swap_core(value)
        value = over(value, self.high, lambda bit, o, c, h, l: (o, c, h ^ bit, l))
        value = gate(value, before_low)
        value = over(value, self.low, lambda bit, o, c, h, l: (o, c, h, l ^ bit))
        value = gate(value, before_outer)
        return over(value, self.outer, lambda bit, o, c, h, l: (o ^ bit, c, h, l))


SMALL_ROWS = 16


def pad_columns(rows, width):
    return jnp.pad(rows, [(0, 0)] * (rows.ndim - 1) + [(0, width - rows.shape[-1])])


def per_device(
    layer_input,
    cotangent,
    attn_weight,
    attn_bias,
    out_weight,
    up_weight,
    up_bias,
    down_weight,
    norm_gains,
    norm_shifts,
    attn_weight_moments,
    attn_bias_moments,
    out_weight_moments,
    up_weight_moments,
    up_bias_moments,
    down_weight_moments,
    norm_gains_moments,
    norm_shifts_moments,
):
    local_heads = attn_bias.shape[0]
    local_seqs, block_tokens, model_width = layer_input.shape
    lay = Layout(local_heads, local_seqs)
    fsdp, core, high = lay.fsdp, lay.core, lay.high
    bias_width = attn_bias.shape[1]
    head_width = bias_width * fsdp // 3
    part_heads = local_heads // core
    shard_width = model_width // fsdp
    hidden_part = up_bias.shape[0]
    own_tokens = local_seqs * block_tokens
    near_tokens = core * own_tokens
    far_tokens = near_tokens * (lay.low - 1)
    near_other = near_tokens - near_tokens // core
    far_other = far_tokens - far_tokens // core

    tokens = jnp.concatenate(lay.to_sequence(layer_input), axis=0)
    small = jnp.concatenate(
        [
            norm_gains.astype(half),
            norm_shifts.astype(half),
            pad_columns(attn_bias.astype(half).reshape(1, -1), shard_width),
            pad_columns(up_bias.astype(half).reshape(1, -1), shard_width),
            jnp.zeros((SMALL_ROWS - 8, shard_width), half),
        ],
        axis=0,
    )
    attn_rows = part_heads * 3 * head_width
    out_rows = part_heads * head_width
    hidden_rows = up_weight.shape[1] // core
    first = lay.pair_weights([attn_weight.astype(half).T, out_weight.astype(half)], small)
    first_near = lay.near_high(first)
    first_far = lay.far_high(gate(first, *first_near.values()))
    gathered = {0: lay.outer_weights(first)}
    for step, rows in {**first_near, **first_far}.items():
        gathered[step] = lay.outer_weights(rows)
    gathered = [gathered[step] for step in range(high)]
    w_attn = lay.rows_of(gathered, 0, attn_rows)
    w_output = lay.rows_of(gathered, attn_rows, out_rows)
    small = lay.rows_of(gathered, attn_rows + out_rows, SMALL_ROWS)
    small = small.reshape(high, SMALL_ROWS, model_width)
    gain_rows = small[0, 0:2].astype(wide)
    shift_rows = small[0, 2:6].astype(wide)
    b_attn = small[:, 6].reshape(high, fsdp, shard_width)[:, :, : local_heads * bias_width]
    b_attn = b_attn.reshape(high, fsdp, core, part_heads, bias_width)
    b_attn = lax.dynamic_index_in_dim(b_attn, lay.core_index, 2, keepdims=False)
    b_attn = jnp.transpose(b_attn, (0, 2, 1, 3)).reshape(-1, 1).astype(wide)
    b_upward = small[:, 7].reshape(high, fsdp, shard_width)[:, :, :hidden_part]
    b_upward = b_upward.reshape(high, core, (fsdp // core) * hidden_part)
    b_upward = lax.dynamic_index_in_dim(b_upward, lay.core_index, 1, keepdims=False)
    b_upward = b_upward.reshape(1, -1).astype(wide)

    near, far = lay.share(tokens)
    tokens_full = jnp.concatenate([near, far], axis=0)
    second = lay.pair_weights([up_weight.astype(half).T, down_weight.astype(half)])
    gathered = {0: lay.outer_weights(second)}
    second = gate(second, *first_near.values(), *first_far.values())
    second_near = lay.near_high(second)

    qkv = (times_t(w_attn, tokens_full) + b_attn).astype(half)
    attn_far, log_far, *parts_far = attention_forward(
        qkv, w_output, near_tokens, far_tokens, far_other, head_width
    )
    for step, rows in second_near.items():
        gathered[step] = lay.outer_weights(gate(rows, attn_far))
    second_far = lay.far_high(gate(second, attn_far, *second_near.values()))
    near_qkv, received = lay.start_reduce(parts_far, qkv)
    attn_near, log_near, *parts_near = attention_forward(
        near_qkv, w_output, 0, near_tokens, near_other, head_width
    )
    logsum = jnp.concatenate([log_near, log_far], axis=2)
    attn_out = lay.finish_reduce(parts_near, received)
    resid_one = attn_out + shift_rows[0] + tokens.astype(wide)
    for step, rows in second_far.items():
        gathered[step] = lay.outer_weights(gate(rows, resid_one))
    gathered = [gathered[step] for step in range(high)]
    w_upward = lay.rows_of(gathered, 0, hidden_rows)
    w_downward = lay.rows_of(gathered, hidden_rows, hidden_rows)
    upward = lay.to_sequence(gate(cotangent, attn_near, *second_far.values()))
    hidden_one, normed_one, spread_one = layer_norm(resid_one, gain_rows[0], shift_rows[1])
    hidden_near, hidden_far = lay.share(hidden_one.astype(half))
    hidden_far, *upward = lax.optimization_barrier((hidden_far, *upward))
    upward = jnp.concatenate(upward, axis=0).astype(wide)
    active_far, slope_far, *parts_far = ffn_forward(
        hidden_far, w_upward, b_upward, w_downward, far_other
    )
    hidden_near, received = lay.start_reduce(parts_far, hidden_near)
    active_near, slope_near, *parts_near = ffn_forward(
        hidden_near, w_upward, b_upward, w_downward, near_other
    )
    ffn_out = lay.finish_reduce(parts_near, received)
    resid_two = ffn_out + shift_rows[2] + hidden_one
    result, normed_two, spread_two = layer_norm(resid_two, gain_rows[1], shift_rows[3])

    grad_two = norm_back(upward, gain_rows[1], normed_two, spread_two)
    grad_near, grad_far = lay.share(grad_two.astype(half))
    output = result.astype(half).reshape(local_seqs, block_tokens, model_width)
    outputs = lay.from_sequence(gate(output, grad_far))
    inner_far, up_far, *parts_far = ffn_backward(
        grad_far, slope_far, w_downward, w_upward, far_other
    )
    grad_near, received = lay.start_reduce(parts_far, grad_near)
    inner_near, up_near, *parts_near = ffn_backward(
        grad_near, slope_near, w_downward, w_upward, near_other
    )
    grad_down = t_times(active_near, grad_near) + t_times(active_far, grad_far)
    grad_upward = t_times(inner_near, hidden_near) + t_times(inner_far, hidden_far)
    grad_hidden = grad_two + lay.finish_reduce(parts_near, received)
    grad_one = norm_back(grad_hidden, gain_rows[0], normed_one, spread_one)
    second_grads = [
        jnp.concatenate(
            [
                grad_upward[place * hidden_rows : (place + 1) * hidden_rows],
                grad_down[place * hidden_rows : (place + 1) * hidden_rows],
            ],
            axis=0,
        )
        for place in range(high)
    ]
    second_sums = lay.scatter_outer(second_grads)
    one_near, one_far = lay.share(grad_one.astype(half))
    one_full = jnp.concatenate([one_near, one_far], axis=0)
    grad_attn = times_t(w_output, one_full).astype(half)
    grad_qkv, bias_sums = attention_backward(qkv, logsum, grad_attn, head_width)
    grad_far_qkv = grad_qkv[:, near_tokens:]
    far_mine = t_times(grad_far_qkv[:, : far_tokens - far_other], w_attn)
    parts_far = [far_mine]
    if core == 2:
        parts_far.append(t_times(grad_far_qkv[:, far_tokens - far_other :], w_attn).astype(half))
    grad_qkv, received = lay.start_reduce(parts_far, grad_qkv)
    parts_near = [t_times(grad_qkv[:, : near_tokens - near_other], w_attn)]
    if core == 2:
        parts_near.append(
            t_times(grad_qkv[:, near_tokens - near_other : near_tokens], w_attn).astype(half)
        )
    input_grad = grad_one + lay.finish_reduce(parts_near, received)
    input_grads = lay.from_sequence(
        input_grad.astype(half).reshape(local_seqs, block_tokens, model_width)
    ).astype(wide)
    grad_attn_w = times(grad_qkv, tokens_full)
    grad_output = times(attn_near, one_near) + times(attn_far, one_far)

    norm_sums = lay.total(
        jnp.stack(
            [
                jnp.sum(grad_hidden * normed_one, axis=0),
                jnp.sum(upward * normed_two, axis=0),
                jnp.sum(grad_one, axis=0),
                jnp.sum(grad_hidden, axis=0),
                jnp.sum(grad_two, axis=0),
                jnp.sum(upward, axis=0),
            ]
        ),
        one_far,
        grad_qkv,
    )
    norm_sums = lax.dynamic_slice_in_dim(norm_sums, lay.fsdp_index * shard_width, shard_width, 1)
    core_here = jnp.arange(core) == lay.core_index
    bias_sums = bias_sums[:, 0].reshape(high, part_heads, fsdp, bias_width)
    bias_sums = jnp.transpose(bias_sums, (0, 2, 1, 3))[:, :, None]
    bias_sums = jnp.where(core_here[:, None, None], bias_sums, 0.0)
    bias_sums = pad_columns(bias_sums.reshape(high, fsdp, -1), shard_width)
    up_sums = (up_near + up_far).reshape(high, 1, (fsdp // core) * hidden_part)
    up_sums = jnp.where(core_here[:, None], up_sums, 0.0)
    up_sums = pad_columns(up_sums.reshape(high, fsdp, hidden_part), shard_width)
    small_sums = jnp.pad(
        jnp.stack([bias_sums.reshape(high, -1), up_sums.reshape(high, -1)], axis=1),
        ((0, 0), (0, SMALL_ROWS - 2), (0, 0)),
    )
    second_parts = lay.scatter_core(lay.scatter_high(second_sums, grad_qkv))
    second_new = update_matrices(
        lay.core_index,
        second_parts,
        [(up_weight, up_weight_moments, True, matrix_rate), (down_weight, down_weight_moments, False, matrix_rate)],
    )
    first_grads = [
        jnp.concatenate(
            [
                grad_attn_w[place * attn_rows : (place + 1) * attn_rows],
                grad_output[place * out_rows : (place + 1) * out_rows],
                small_sums[place],
            ],
            axis=0,
        )
        for place in range(high)
    ]
    first_parts = lay.scatter_core(lay.scatter_high(lay.scatter_outer(first_grads)))
    first_new = update_matrices(
        lay.core_index,
        first_parts,
        [(attn_weight, attn_weight_moments, True, matrix_rate), (out_weight, out_weight_moments, False, output_rate)],
    )
    small_shard = sum(part[attn_rows + out_rows :] for part in first_parts)
    vectors = (
        (attn_bias, attn_bias_moments, small_shard[0, : local_heads * bias_width].reshape(local_heads, bias_width)),
        (up_bias, up_bias_moments, small_shard[1, :hidden_part]),
        (norm_gains, norm_gains_moments, norm_sums[0:2]),
        (norm_shifts, norm_shifts_moments, norm_sums[2:6]),
    )
    bias_new, up_bias_new, gains_new, shifts_new = [
        (grad,) + adamw_update(weight, pair, grad, vector_rate, 0.0) for weight, pair, grad in vectors
    ]
    everything = (
        first_new[0],
        bias_new,
        first_new[1],
        second_new[0],
        up_bias_new,
        second_new[1],
        gains_new,
        shifts_new,
    )
    grads, new_weights, new_moments = zip(*everything)
    return (outputs, input_grads) + grads + new_weights + new_moments


def solution(mesh):
    return jax.shard_map(
        per_device,
        mesh=mesh,
        in_specs=(
            P("fsdp", "tensor", None),
            P("fsdp", "tensor", None),
            P("fsdp", "tensor"),
            P("tensor", "fsdp"),
            P("tensor", "fsdp"),
            P("fsdp", "tensor"),
            P(("tensor", "fsdp")),
            P("tensor", "fsdp"),
            P(None, "fsdp"),
            P(None, "fsdp"),
            P(None, "fsdp", "tensor"),
            P(None, "tensor", "fsdp"),
            P(None, "tensor", "fsdp"),
            P(None, "fsdp", "tensor"),
            P(None, ("tensor", "fsdp")),
            P(None, "tensor", "fsdp"),
            P(None, None, "fsdp"),
            P(None, None, "fsdp"),
        ),
        out_specs=(
            P("fsdp", "tensor", None),
            P("fsdp", "tensor", None),
            P("fsdp", "tensor"),
            P("tensor", "fsdp"),
            P("tensor", "fsdp"),
            P("fsdp", "tensor"),
            P(("tensor", "fsdp")),
            P("tensor", "fsdp"),
            P(None, "fsdp"),
            P(None, "fsdp"),
            P("fsdp", "tensor"),
            P("tensor", "fsdp"),
            P("tensor", "fsdp"),
            P("fsdp", "tensor"),
            P(("tensor", "fsdp")),
            P("tensor", "fsdp"),
            P(None, "fsdp"),
            P(None, "fsdp"),
            P(None, "fsdp", "tensor"),
            P(None, "tensor", "fsdp"),
            P(None, "tensor", "fsdp"),
            P(None, "fsdp", "tensor"),
            P(None, ("tensor", "fsdp")),
            P(None, "tensor", "fsdp"),
            P(None, None, "fsdp"),
            P(None, None, "fsdp"),
        ),
        check_vma=False,
    )
```

```python
import functools

import jax
import jax.numpy as jnp
from jax import lax
from jax.experimental import pallas as pl
from jax.experimental.pallas import tpu as pltpu
from jax.sharding import PartitionSpec as P

norm_eps = 1e-05
beta_one = 0.9
beta_two = 0.999
adam_eps = 1e-08
adam_step = 4.0
matrix_rate = 0.01
output_rate = 0.1
vector_rate = 0.1
decay_rate = 0.1
inv_root_two = 0.7071067811865476
inv_root_tau = 0.3989422804014327


def layer_norm(resid, gain_row, shift_row):
    center = resid - jnp.mean(resid, axis=-1, keepdims=True)
    spread = lax.rsqrt(jnp.mean(center * center, axis=-1, keepdims=True) + norm_eps)
    normed = center * spread
    return (normed * gain_row + shift_row, normed, spread)


def norm_back(grad_out, gain_row, normed, spread):
    scaled = grad_out * gain_row
    return spread * (
        scaled
        - jnp.mean(scaled, axis=-1, keepdims=True)
        - normed * jnp.mean(scaled * normed, axis=-1, keepdims=True)
    )


def gelu_value(inner):
    return inner * 0.5 * (1.0 + jax.scipy.special.erf(inner * inv_root_two))


def gelu_slope(inner):
    return (
        0.5 * (1.0 + jax.scipy.special.erf(inner * inv_root_two))
        + inner * jnp.exp(-0.5 * inner * inner) * inv_root_tau
    )


def adamw_update(weight, moments, grad, rate, decay):
    first_moment = beta_one * moments[0] + (1.0 - beta_one) * grad
    second_moment = beta_two * moments[1] + (1.0 - beta_two) * grad * grad
    direction = (
        first_moment
        / (1.0 - beta_one**adam_step)
        / (jnp.sqrt(second_moment / (1.0 - beta_two**adam_step)) + adam_eps)
    )
    return (weight - rate * (direction + decay * weight), jnp.stack([first_moment, second_moment]))


half = jnp.bfloat16
wide = jnp.float32
VMEM_BYTES = 40 * 1024 * 1024


def times(left, right):
    return lax.dot_general(left, right, (((1,), (0,)), ((), ())), preferred_element_type=wide)


def times_t(left, right):
    return lax.dot_general(left, right, (((1,), (1,)), ((), ())), preferred_element_type=wide)


def t_times(left, right):
    return lax.dot_general(left, right, (((0,), (0,)), ((), ())), preferred_element_type=wide)


def whole_block(*shape):
    return pl.BlockSpec(shape, lambda step: (0,) * len(shape))


def sum_shapes(rows, other, width):
    shapes = [jax.ShapeDtypeStruct((rows - other, width), wide)]
    if other:
        shapes.append(jax.ShapeDtypeStruct((other, width), half))
    return shapes, [whole_block(*shape.shape) for shape in shapes]


def write_sums(total, refs):
    mine = refs[0].shape[0]
    refs[0][...] = total[:mine]
    if len(refs) > 1:
        refs[1][...] = total[mine:].astype(half)


def params():
    return pltpu.CompilerParams(
        dimension_semantics=("arbitrary",), vmem_limit_bytes=VMEM_BYTES
    )


def up_kernel(x_ref, up_ref, bias_ref, down_ref, active_ref, slope_ref, *rest):
    sums, total = rest[:-1], rest[-1]
    inner = times_t(x_ref[...], up_ref[...]) + bias_ref[...]
    chance = 0.5 * (1.0 + lax.erf(inner * inv_root_two))
    active = (inner * chance).astype(half)
    active_ref[...] = active
    slope_ref[...] = chance + inner * jnp.exp(-0.5 * inner * inner) * inv_root_tau
    part = times(active, down_ref[...])
    step = pl.program_id(0)

    @pl.when(step == 0)
    def _():
        total[...] = part

    @pl.when(step > 0)
    def _():
        total[...] += part

    @pl.when(step == pl.num_programs(0) - 1)
    def _():
        write_sums(total[...], sums)


def ffn_forward(x, w_upward, b_upward, w_downward, other):
    rows, width = x.shape
    hidden = w_upward.shape[0]
    tile = 256
    shapes, specs = sum_shapes(rows, other, width)
    return pl.pallas_call(
        up_kernel,
        grid=(hidden // tile,),
        in_specs=[
            whole_block(rows, width),
            pl.BlockSpec((tile, width), lambda step: (step, 0)),
            pl.BlockSpec((1, tile), lambda step: (0, step)),
            pl.BlockSpec((tile, width), lambda step: (step, 0)),
        ],
        out_specs=[
            pl.BlockSpec((rows, tile), lambda step: (0, step)),
            pl.BlockSpec((rows, tile), lambda step: (0, step)),
        ]
        + specs,
        out_shape=[
            jax.ShapeDtypeStruct((rows, hidden), half),
            jax.ShapeDtypeStruct((rows, hidden), wide),
        ]
        + shapes,
        scratch_shapes=[pltpu.VMEM((rows, width), wide)],
        compiler_params=params(),
        cost_estimate=pl.CostEstimate(
            flops=4 * rows * width * hidden,
            bytes_accessed=rows * hidden * 6 + hidden * width * 4,
            transcendentals=2 * rows * hidden,
        ),
        name="ffn_forward",
    )(x, w_upward, b_upward, w_downward)


def down_kernel(grad_ref, slope_ref, down_ref, up_ref, inner_ref, bias_ref, *rest):
    sums, total = rest[:-1], rest[-1]
    grad_inner = times_t(grad_ref[...], down_ref[...]) * slope_ref[...]
    bias_ref[...] = jnp.sum(grad_inner, axis=0, keepdims=True)
    grad_inner_b = grad_inner.astype(half)
    inner_ref[...] = grad_inner_b
    part = times(grad_inner_b, up_ref[...])
    step = pl.program_id(0)

    @pl.when(step == 0)
    def _():
        total[...] = part

    @pl.when(step > 0)
    def _():
        total[...] += part

    @pl.when(step == pl.num_programs(0) - 1)
    def _():
        write_sums(total[...], sums)


def ffn_backward(grad, slope, w_downward, w_upward, other):
    rows, width = grad.shape
    hidden = w_upward.shape[0]
    tile = 256
    shapes, specs = sum_shapes(rows, other, width)
    return pl.pallas_call(
        down_kernel,
        grid=(hidden // tile,),
        in_specs=[
            whole_block(rows, width),
            pl.BlockSpec((rows, tile), lambda step: (0, step)),
            pl.BlockSpec((tile, width), lambda step: (step, 0)),
            pl.BlockSpec((tile, width), lambda step: (step, 0)),
        ],
        out_specs=[
            pl.BlockSpec((rows, tile), lambda step: (0, step)),
            pl.BlockSpec((1, tile), lambda step: (0, step)),
        ]
        + specs,
        out_shape=[
            jax.ShapeDtypeStruct((rows, hidden), half),
            jax.ShapeDtypeStruct((1, hidden), wide),
        ]
        + shapes,
        scratch_shapes=[pltpu.VMEM((rows, width), wide)],
        compiler_params=params(),
        cost_estimate=pl.CostEstimate(
            flops=4 * rows * width * hidden,
            bytes_accessed=rows * hidden * 6 + hidden * width * 4,
            transcendentals=0,
        ),
        name="ffn_backward",
    )(grad, slope, w_downward, w_upward)


def attention_kernel(first, chunk, head_width, qkv_ref, out_ref, attn_ref, log_ref, *rest):
    sums, mixed = rest[:-1], rest[-1]
    head = pl.program_id(0)
    scale = head_width ** (-0.5)
    keys = jnp.transpose(qkv_ref[head_width : 2 * head_width, :])
    values = qkv_ref[2 * head_width : 3 * head_width, :]
    count = attn_ref.shape[1]
    for start in range(0, count, chunk):
        here = slice(first + start, first + start + chunk)
        scores = times(keys, qkv_ref[0:head_width, here]) * scale
        top = jnp.max(scores, axis=0, keepdims=True)
        powers = jnp.exp(scores - top)
        norm = jnp.sum(powers, axis=0, keepdims=True)
        weights = (powers * (1.0 / norm)).astype(half)
        log_ref[0, :, start : start + chunk] = top + jnp.log(norm)
        block = times(values, weights).astype(half)
        attn_ref[:, start : start + chunk] = block
        mixed[pl.ds(pl.multiple_of(head * head_width, head_width), head_width), pl.ds(start, chunk)] = block

    @pl.when(head == pl.num_programs(0) - 1)
    def _():
        write_sums(t_times(mixed[...], out_ref[...]), sums)


def attention_forward(qkv, w_output, first, count, other, head_width):
    length = qkv.shape[1]
    heads = qkv.shape[0] // (3 * head_width)
    width = w_output.shape[1]
    chunk = 256 if count % 256 == 0 else 128
    shapes, specs = sum_shapes(count, other, width)
    return pl.pallas_call(
        functools.partial(attention_kernel, first, chunk, head_width),
        grid=(heads,),
        in_specs=[
            pl.BlockSpec((3 * head_width, length), lambda head: (head, 0)),
            whole_block(heads * head_width, width),
        ],
        out_specs=[
            pl.BlockSpec((head_width, count), lambda head: (head, 0)),
            pl.BlockSpec((1, 1, count), lambda head: (head, 0, 0)),
        ]
        + specs,
        out_shape=[
            jax.ShapeDtypeStruct((heads * head_width, count), half),
            jax.ShapeDtypeStruct((heads, 1, count), wide),
        ]
        + shapes,
        scratch_shapes=[pltpu.VMEM((heads * head_width, count), half)],
        compiler_params=params(),
        cost_estimate=pl.CostEstimate(
            flops=16 * heads * count * length * head_width,
            bytes_accessed=qkv.size * 2 + count * width * 6,
            transcendentals=heads * count * length,
        ),
        name="attention_forward",
    )(qkv, w_output)


def attention_back_kernel(chunk, head_width, qkv_ref, log_ref, grad_ref, out_ref, bias_ref):
    scale = head_width ** (-0.5)
    key_rows = qkv_ref[head_width : 2 * head_width, :]
    keys = jnp.transpose(key_rows)
    values = jnp.transpose(qkv_ref[2 * head_width : 3 * head_width, :])
    length = keys.shape[0]
    grad_keys = jnp.zeros((length, head_width), wide)
    grad_values = jnp.zeros((length, head_width), wide)
    query_sum = jnp.zeros((head_width, 1), wide)
    for start in range(0, length, chunk):
        here = slice(start, start + chunk)
        queries = qkv_ref[0:head_width, here]
        grads = grad_ref[:, here]
        scores = times(keys, queries) * scale
        chances = jnp.exp(scores - log_ref[0, :, here])
        grad_scores = times(values, grads)
        mean = jnp.sum(chances * grad_scores, axis=0, keepdims=True)
        logits = (chances * (grad_scores - mean)).astype(half)
        grad_values = grad_values + times(chances.astype(half), jnp.transpose(grads))
        grad_keys = grad_keys + times(logits, jnp.transpose(queries))
        grad_query = times(key_rows, logits) * scale
        out_ref[0:head_width, here] = grad_query.astype(half)
        query_sum = query_sum + jnp.sum(grad_query, axis=1, keepdims=True)
    grad_keys = jnp.transpose(grad_keys) * scale
    grad_values = jnp.transpose(grad_values)
    out_ref[head_width : 2 * head_width, :] = grad_keys.astype(half)
    out_ref[2 * head_width : 3 * head_width, :] = grad_values.astype(half)
    sums = jnp.concatenate(
        [
            query_sum,
            jnp.sum(grad_keys, axis=1, keepdims=True),
            jnp.sum(grad_values, axis=1, keepdims=True),
        ],
        axis=0,
    )
    bias_ref[...] = jnp.broadcast_to(sums, bias_ref.shape)


def attention_backward(qkv, logsum, grad, head_width, first, heads):
    length = qkv.shape[1]
    chunk = 256
    return pl.pallas_call(
        functools.partial(attention_back_kernel, chunk, head_width),
        grid=(heads,),
        in_specs=[
            pl.BlockSpec((3 * head_width, length), lambda head: (head + first, 0)),
            pl.BlockSpec((1, 1, length), lambda head: (head + first, 0, 0)),
            pl.BlockSpec((head_width, length), lambda head: (head + first, 0)),
        ],
        out_specs=[
            pl.BlockSpec((3 * head_width, length), lambda head: (head, 0)),
            pl.BlockSpec((3 * head_width, 128), lambda head: (head, 0)),
        ],
        out_shape=[
            jax.ShapeDtypeStruct((heads * 3 * head_width, length), half),
            jax.ShapeDtypeStruct((heads * 3 * head_width, 128), wide),
        ],
        compiler_params=params(),
        cost_estimate=pl.CostEstimate(
            flops=40 * heads * length * length * head_width,
            bytes_accessed=heads * length * head_width * 15,
            transcendentals=heads * length * length,
        ),
        name="attention_backward",
    )(qkv, logsum, grad)


def update_kernel(plan, core_count, core_ref, *refs):
    parts, refs = refs[:core_count], refs[core_count:]
    inputs, outputs = refs[: 2 * len(plan)], refs[2 * len(plan) :]
    first = 0
    for index, (rows, flip, rate) in enumerate(plan):
        weight_ref, pair_ref = inputs[2 * index : 2 * index + 2]
        grad_ref, new_ref, moments_ref = outputs[3 * index : 3 * index + 3]
        blocks = [part[first : first + rows, :] for part in parts]
        if core_count == 2:
            lead = core_ref[0] == 0
            blocks = [
                jnp.where(lead, blocks[0], blocks[1]),
                jnp.where(lead, blocks[1], blocks[0]),
            ]
        grad = jnp.concatenate(blocks, axis=0)
        if flip:
            grad = jnp.transpose(grad)
        first += rows
        weight = weight_ref[...]
        first_moment = beta_one * pair_ref[0] + (1.0 - beta_one) * grad
        second_moment = beta_two * pair_ref[1] + (1.0 - beta_two) * grad * grad
        direction = (
            first_moment
            / (1.0 - beta_one**adam_step)
            / (jnp.sqrt(second_moment / (1.0 - beta_two**adam_step)) + adam_eps)
        )
        grad_ref[...] = grad
        new_ref[...] = weight - rate * (direction + decay_rate * weight)
        moments_ref[0] = first_moment
        moments_ref[1] = second_moment


def update_matrices(core_index, parts, matrices):
    plan, operands, shapes = [], [], []
    for weight, pair, flip, rate in matrices:
        rows = weight.shape[1 if flip else 0] // len(parts)
        plan.append((rows, flip, rate))
        operands += [weight, pair]
        shapes += [weight.shape, weight.shape, pair.shape]
    used = sum(rows for rows, _, _ in plan)
    results = pl.pallas_call(
        functools.partial(update_kernel, tuple(plan), len(parts)),
        grid=(1,),
        in_specs=[pl.BlockSpec(memory_space=pltpu.SMEM)]
        + [whole_block(used, part.shape[1]) for part in parts]
        + [whole_block(*operand.shape) for operand in operands],
        out_specs=[whole_block(*shape) for shape in shapes],
        out_shape=[jax.ShapeDtypeStruct(shape, wide) for shape in shapes],
        compiler_params=params(),
        cost_estimate=pl.CostEstimate(
            flops=20 * sum(weight.size for weight, _, _, _ in matrices),
            bytes_accessed=32 * sum(weight.size for weight, _, _, _ in matrices),
            transcendentals=0,
        ),
        name="adamw",
    )(jnp.reshape(core_index, (1,)).astype(jnp.int32), *[part[:used] for part in parts], *operands)
    return [tuple(results[3 * index : 3 * index + 3]) for index in range(len(plan))]


def spread(shape, axis, place, width, start, count):
    index = lax.broadcasted_iota(jnp.int32, shape, axis)
    column = lax.broadcasted_iota(jnp.int32, shape, 1 - axis)
    held = (place + index // count) * width + start + index % count
    return jnp.where(column == held, 1.0, 0.0).astype(half)


def head_spread(sizes, core, head):
    high, part_heads, fsdp, shard, bias, hidden = sizes
    start = (core * part_heads + head) * bias
    return spread((fsdp * bias, fsdp * shard), 0, 0, shard, start, bias)


def hidden_spread(sizes, core_count, core):
    high, part_heads, fsdp, shard, bias, hidden = sizes
    share = fsdp // core_count
    return spread((fsdp * shard, share * hidden), 1, core * share, shard, 0, hidden)


def unpack_kernel(sizes, core_count, core_ref, small_ref, attn_ref, up_ref, norm_ref):
    high, part_heads, fsdp, shard, bias, hidden = sizes
    core = core_ref[0]
    small = small_ref[...]
    features = fsdp * bias
    for head in range(part_heads):
        rows = times_t(head_spread(sizes, core, head), small)
        for place in range(high):
            first = (place * part_heads + head) * features
            column = place * SMALL_ROWS + 6
            attn_ref[first : first + features, :] = rows[:, column : column + 1]
    rows = times(small, hidden_spread(sizes, core_count, core))
    count = rows.shape[1]
    for place in range(high):
        row = place * SMALL_ROWS + 7
        up_ref[:, place * count : (place + 1) * count] = rows[row : row + 1, :]
    norm_ref[...] = small[:SMALL_ROWS].astype(wide)


def unpack_small(sizes, core_count, core_index, small):
    high, part_heads, fsdp, shard, bias, hidden = sizes
    shapes = [
        (high * part_heads * fsdp * bias, 1),
        (1, high * (fsdp // core_count) * hidden),
        (SMALL_ROWS, fsdp * shard),
    ]
    return pl.pallas_call(
        functools.partial(unpack_kernel, sizes, core_count),
        grid=(1,),
        in_specs=[pl.BlockSpec(memory_space=pltpu.SMEM), whole_block(*small.shape)],
        out_specs=[whole_block(*shape) for shape in shapes],
        out_shape=[jax.ShapeDtypeStruct(shape, wide) for shape in shapes],
        compiler_params=params(),
        name="unpack_small",
    )(core_index, small)


def pack_kernel(sizes, core_count, core_ref, attn_ref, up_ref, out_ref):
    high, part_heads, fsdp, shard, bias, hidden = sizes
    core = core_ref[0]
    features = fsdp * bias
    count = up_ref.shape[1] // high
    hot = hidden_spread(sizes, core_count, core)
    for place in range(high):
        row = jnp.zeros((SMALL_ROWS, fsdp * shard), wide)
        for head in range(part_heads):
            first = (place * part_heads + head) * features
            sums = attn_ref[first : first + features, 0:SMALL_ROWS].astype(half)
            row = row + t_times(sums, head_spread(sizes, core, head))
        ups = jnp.broadcast_to(up_ref[:, place * count : (place + 1) * count], (SMALL_ROWS, count))
        ups = times_t(ups.astype(half), hot)
        line = lax.broadcasted_iota(jnp.int32, row.shape, 0)
        first = place * SMALL_ROWS
        out_ref[first : first + SMALL_ROWS, :] = jnp.where(line < 8, row, ups)


def pack_small(sizes, core_count, core_index, attn_sums, up_sums):
    high, part_heads, fsdp, shard, bias, hidden = sizes
    shape = (high * SMALL_ROWS, fsdp * shard)
    return pl.pallas_call(
        functools.partial(pack_kernel, sizes, core_count),
        grid=(1,),
        in_specs=[
            pl.BlockSpec(memory_space=pltpu.SMEM),
            whole_block(*attn_sums.shape),
            whole_block(*up_sums.shape),
        ],
        out_specs=whole_block(*shape),
        out_shape=jax.ShapeDtypeStruct(shape, wide),
        compiler_params=params(),
        name="pack_small",
    )(core_index, attn_sums, up_sums)


SMALL_ROWS = 16


def gate(value, *before):
    return lax.optimization_barrier((value,) + before)[0]


AXES = ("fsdp", "tensor")


class Layout:
    def __init__(self, local_heads, local_seqs):
        self.fsdp = lax.axis_size("fsdp")
        self.tensor = lax.axis_size("tensor")
        self.seqs = local_seqs
        self.core = 2 if local_heads % 2 == 0 and self.fsdp % 2 == 0 else 1
        self.outer = self.fsdp // self.core
        self.high = self.core * local_seqs
        self.low = self.tensor // self.high
        self.order = list(range(1, self.high, 2)) + list(range(0, self.high, 2))
        self.fsdp_index = lax.axis_index("fsdp")
        self.outer_index = self.fsdp_index // self.core
        self.core_index = self.fsdp_index % self.core
        self.high_index = lax.axis_index("tensor") // self.low

    def send(self, value, target):
        pairs = []
        for outer in range(self.outer):
            for core in range(self.core):
                for high in range(self.high):
                    for low in range(self.low):
                        o, c, h, l = target(outer, core, high, low)
                        source_id = (outer * self.core + core) * self.tensor + high * self.low + low
                        target_id = (o * self.core + c) * self.tensor + h * self.low + l
                        pairs.append((source_id, target_id))
        return lax.ppermute(value, AXES, pairs)

    def swap_core(self, value):
        return self.send(value, lambda o, c, h, l: (o, 1 - c, h, l))

    def to_low(self, value, step):
        return self.send(value, lambda o, c, h, l: (o, c, h, (l + step) % self.low))

    def to_high(self, value, step):
        return self.send(value, lambda o, c, h, l: (o, c, (h + step) % self.high, l))

    def to_outer(self, value, step):
        return self.send(value, lambda o, c, h, l: ((o + step) % self.outer, c, h, l))

    def to_sequence(self, blocks):
        within = self.high_index % self.seqs
        return [
            self.send(
                lax.dynamic_index_in_dim(blocks, (within + k) % self.seqs, 0, keepdims=False),
                lambda o, c, h, l, k=k: (
                    o,
                    h // self.seqs,
                    c * self.seqs + (h % self.seqs + k) % self.seqs,
                    l,
                ),
            )
            for k in range(self.seqs)
        ]

    def from_sequence(self, pieces):
        within = self.high_index % self.seqs
        back = []
        for k in range(self.seqs):
            back.append(
                self.send(
                    pieces[k],
                    lambda o, c, h, l, k=k: (
                        o,
                        h // self.seqs,
                        c * self.seqs + (h % self.seqs - k) % self.seqs,
                        l,
                    ),
                )
            )
        if self.seqs == 2:
            return jnp.where(within == 0, jnp.stack(back), jnp.stack(back[::-1]))
        stacked = jnp.stack(back)
        order = (jnp.arange(self.seqs) - within) % self.seqs
        return jnp.take(stacked, order, axis=0)

    def share(self, own):
        far = [self.to_low(own, -step) for step in range(1, self.low)]
        near = [own]
        if self.core == 2:
            near.append(self.swap_core(own))
            far += [self.swap_core(piece) for piece in far]
        return jnp.concatenate(near, axis=0), jnp.concatenate(far, axis=0)

    def start_reduce(self, parts, later):
        total = parts[0]
        if self.core == 2:
            total = total + self.swap_core(parts[1]).astype(wide)
        total = total.astype(half)
        total, later = lax.optimization_barrier((total, later))
        count = total.shape[0] // (self.low - 1)
        return later, [
            self.to_low(total[(step - 1) * count : step * count], step)
            for step in range(1, self.low)
        ]

    def finish_reduce(self, parts, received):
        total = parts[0]
        if self.core == 2:
            total = total + self.swap_core(parts[1]).astype(wide)
        for piece in received:
            total = total + piece.astype(wide)
        return total

    def ordered(self, index, parts, axis):
        count = len(parts)
        if count == 1:
            return parts[0]
        if count == 2:
            return jnp.where(
                index == 0,
                jnp.concatenate(parts, axis=axis),
                jnp.concatenate(parts[::-1], axis=axis),
            )
        width = parts[0].shape[axis]
        shape = list(parts[0].shape)
        shape[axis] = width * count
        result = jnp.zeros(shape, parts[0].dtype)
        for step, part in enumerate(parts):
            result = lax.dynamic_update_slice_in_dim(
                result, part, ((index + step) % count) * width, axis
            )
        return result

    def core_rows(self, rows, core):
        count = rows.shape[0] // self.core
        return lax.dynamic_slice_in_dim(rows, core * count, count, 0)

    def pair_weights(self, matrices, extra=None):
        def pack(core):
            rows = [self.core_rows(matrix, core) for matrix in matrices]
            if extra is not None:
                rows.append(extra)
            return jnp.concatenate(rows, axis=0)

        if self.core == 1:
            return pack(0)
        other = self.swap_core(pack(1 - self.core_index))
        return self.ordered(self.core_index, [pack(self.core_index), other], 1)

    def swap_high(self, value, bits):
        return self.send(value, lambda o, c, h, l: (o, c, h ^ bits, l))

    def outer_weights(self, rows):
        return [rows] + [self.to_outer(rows, -step) for step in range(1, self.outer)]

    def rows_of(self, gathered, first, count):
        return jnp.concatenate(
            [
                self.ordered(self.outer_index, [part[first : first + count] for part in parts], 1)
                for parts in gathered
            ],
            axis=0,
        )

    def columns(self, grad, step):
        width = grad.shape[1] // self.outer
        place = (self.outer_index + step) % self.outer
        return lax.dynamic_slice_in_dim(grad, place * width, width, 1)

    def start_outer(self, grad, *before):
        return [
            self.to_outer(gate(self.columns(grad, step).astype(half), *before), step)
            for step in range(1, self.outer)
        ]

    def finish_outer(self, grad, received):
        total = self.columns(grad, 0)
        for part in received:
            total = total + part.astype(wide)
        return total

    def finish_high(self, even, received):
        total = even + received.astype(wide)
        if self.high == 2:
            return total
        rows = total.shape[0] // 2
        return total[:rows] + self.swap_high(total[rows:].astype(half), 2).astype(wide)

    def scatter_core(self, column):
        if self.core == 1:
            return [column]
        width = column.shape[1] // self.core
        mine = lax.dynamic_slice_in_dim(column, self.core_index * width, width, 1)
        other = self.swap_core(
            lax.dynamic_slice_in_dim(column, (1 - self.core_index) * width, width, 1)
        )
        return [mine, other]

    def total(self, value, before_low, before_outer):
        def over(value, count, target):
            bit = 1
            while bit < count:
                value = value + self.send(value, functools.partial(target, bit))
                bit *= 2
            return value

        if self.core == 2:
            value = value + self.swap_core(value)
        value = over(value, self.high, lambda bit, o, c, h, l: (o, c, h ^ bit, l))
        value = gate(value, before_low)
        value = over(value, self.low, lambda bit, o, c, h, l: (o, c, h, l ^ bit))
        value = gate(value, before_outer)
        return over(value, self.outer, lambda bit, o, c, h, l: (o ^ bit, c, h, l))


def pad_columns(rows, width):
    return jnp.pad(rows, [(0, 0)] * (rows.ndim - 1) + [(0, width - rows.shape[-1])])


def per_device(
    layer_input,
    cotangent,
    attn_weight,
    attn_bias,
    out_weight,
    up_weight,
    up_bias,
    down_weight,
    norm_gains,
    norm_shifts,
    attn_weight_moments,
    attn_bias_moments,
    out_weight_moments,
    up_weight_moments,
    up_bias_moments,
    down_weight_moments,
    norm_gains_moments,
    norm_shifts_moments,
):
    local_heads = attn_bias.shape[0]
    local_seqs, block_tokens, model_width = layer_input.shape
    lay = Layout(local_heads, local_seqs)
    fsdp, core, high = lay.fsdp, lay.core, lay.high
    bias_width = attn_bias.shape[1]
    head_width = bias_width * fsdp // 3
    part_heads = local_heads // core
    shard_width = model_width // fsdp
    hidden_part = up_bias.shape[0]
    own_tokens = local_seqs * block_tokens
    near_tokens = core * own_tokens
    far_tokens = near_tokens * (lay.low - 1)
    near_other = near_tokens - near_tokens // core
    far_other = far_tokens - far_tokens // core

    tokens = jnp.concatenate(lay.to_sequence(layer_input), axis=0)
    small = jnp.concatenate(
        [
            norm_gains.astype(half),
            norm_shifts.astype(half),
            pad_columns(attn_bias.astype(half).reshape(1, -1), shard_width),
            pad_columns(up_bias.astype(half).reshape(1, -1), shard_width),
            jnp.zeros((SMALL_ROWS - 8, shard_width), half),
        ],
        axis=0,
    )
    attn_rows = part_heads * 3 * head_width
    out_rows = part_heads * head_width
    hidden_rows = up_weight.shape[1] // core
    first = lay.pair_weights([attn_weight.astype(half).T, out_weight.astype(half)], small)
    up_later, down_later = gate((up_weight, down_weight), first)
    second = lay.pair_weights([up_later.astype(half).T, down_later.astype(half)])

    def spread_first(rows):
        places = {0: rows}
        for bits in (1, 2):
            if bits < high:
                places[bits] = lay.swap_high(rows, bits)
        return places

    first_places = spread_first(first)
    first_outer = {0: lay.outer_weights(first)}
    second_outer = {0: lay.outer_weights(second)}
    if high == 4:
        first_places[3] = lay.swap_high(gate(first_places[2], first_places[1]), 1)
    for place in range(1, high):
        rows = gate(first_places[place], *second_outer[0][1:])
        first_outer[place] = lay.outer_weights(rows)
    gathered = [first_outer[place] for place in lay.order]
    w_attn = lay.rows_of(gathered, 0, attn_rows)
    w_output = lay.rows_of(gathered, attn_rows, out_rows)
    small = lay.rows_of(gathered, attn_rows + out_rows, SMALL_ROWS)
    sizes = (high, part_heads, fsdp, shard_width, bias_width, hidden_part)
    core_index = jnp.reshape(lay.core_index, (1,)).astype(jnp.int32)
    b_attn, b_upward, norm_rows = unpack_small(sizes, core, core_index, small)
    gain_rows = norm_rows[0:2]
    shift_rows = norm_rows[2:6]

    near, far = lay.share(tokens)
    tokens_full = jnp.concatenate([near, far], axis=0)
    second_places = spread_first(gate(second, *first_places.values()))

    qkv = (times_t(w_attn, tokens_full) + b_attn).astype(half)
    attn_far, log_far, *parts_far = attention_forward(
        qkv, w_output, near_tokens, far_tokens, far_other, head_width
    )
    for place in range(1, min(high, 3)):
        second_outer[place] = lay.outer_weights(gate(second_places[place], attn_far))
    if high == 4:
        last = gate(second_places[2], second_places[1], attn_far)
        second_places[3] = lay.swap_high(last, 1)
    near_qkv, received = lay.start_reduce(parts_far, qkv)
    attn_near, log_near, *parts_near = attention_forward(
        near_qkv, w_output, 0, near_tokens, near_other, head_width
    )
    logsum = jnp.concatenate([log_near, log_far], axis=2)
    attn_out = lay.finish_reduce(parts_near, received)
    resid_one = attn_out + shift_rows[0] + tokens.astype(wide)
    hidden_one, normed_one, spread_one = layer_norm(resid_one, gain_rows[0], shift_rows[1])
    hidden_near, hidden_far = lay.share(hidden_one.astype(half))
    if high == 4:
        second_outer[3] = lay.outer_weights(gate(second_places[3], hidden_one))
    upward = lay.to_sequence(gate(cotangent, hidden_one, *second_places.values()))
    gathered = [second_outer[place] for place in lay.order]
    w_upward = lay.rows_of(gathered, 0, hidden_rows)
    w_downward = lay.rows_of(gathered, hidden_rows, hidden_rows)
    hidden_far, *upward = lax.optimization_barrier((hidden_far, *upward))
    upward = jnp.concatenate(upward, axis=0).astype(wide)
    active_far, slope_far, *parts_far = ffn_forward(
        hidden_far, w_upward, b_upward, w_downward, far_other
    )
    hidden_near, received = lay.start_reduce(parts_far, hidden_near)
    active_near, slope_near, *parts_near = ffn_forward(
        hidden_near, w_upward, b_upward, w_downward, near_other
    )
    ffn_out = lay.finish_reduce(parts_near, received)
    resid_two = ffn_out + shift_rows[2] + hidden_one
    result, normed_two, spread_two = layer_norm(resid_two, gain_rows[1], shift_rows[3])

    grad_two = norm_back(upward, gain_rows[1], normed_two, spread_two)
    grad_near, grad_far = lay.share(grad_two.astype(half))
    output = result.astype(half).reshape(local_seqs, block_tokens, model_width)
    inner_far, up_far, *parts_far = ffn_backward(
        grad_far, slope_far, w_downward, w_upward, far_other
    )
    later, received = lay.start_reduce(parts_far, (grad_near, grad_far, active_near, active_far))
    grad_near, grad_far, active_near, active_far = later
    grad_down = t_times(active_near, grad_near) + t_times(active_far, grad_far)
    down_received = lay.start_outer(grad_down)
    inner_near, up_near, *parts_near = ffn_backward(
        gate(grad_near, grad_down), slope_near, w_downward, w_upward, near_other
    )
    grad_hidden = grad_two + lay.finish_reduce(parts_near, received)
    outputs = lay.from_sequence(gate(output, inner_near))
    grad_one = norm_back(grad_hidden, gain_rows[0], normed_one, spread_one)
    grad_one_b = grad_one.astype(half)
    one_near, one_far = lay.share(grad_one_b)
    hidden_near, hidden_far = gate((hidden_near, hidden_far), grad_one_b)
    grad_upward = t_times(inner_near, hidden_near) + t_times(inner_far, hidden_far)
    up_received = lay.start_outer(grad_upward, *down_received)
    cut_rows = grad_down.shape[0] // 2
    down_sums = lay.finish_outer(gate(grad_down, grad_upward), down_received)
    down_odd = down_sums[:cut_rows].astype(half)
    down_high = lay.swap_high(down_odd, 1)
    one_full = jnp.concatenate([one_near, one_far], axis=0)
    grad_attn = times_t(w_output, gate(one_full, down_odd)).astype(half)
    half_heads = part_heads * high // 2
    odd_qkv, odd_sums = attention_backward(qkv, logsum, grad_attn, head_width, 0, half_heads)

    up_sums = lay.finish_outer(gate(grad_upward, odd_qkv), up_received)
    up_odd = up_sums[:cut_rows].astype(half)
    up_high = lay.swap_high(up_odd, 1)
    grad_output = times(attn_near, one_near) + times(attn_far, one_far)
    up_total = gate(up_near + up_far, odd_qkv)
    odd_sizes = (high // 2,) + sizes[1:]
    hidden_half = up_total.shape[1] // 2

    def first_block(grad_qkv, sums, ups, out_grad):
        packed = pack_small(odd_sizes, core, core_index, sums, ups)
        grad = times(grad_qkv, tokens_full)
        return jnp.concatenate(
            [
                block
                for place in range(high // 2)
                for block in (
                    grad[place * attn_rows : (place + 1) * attn_rows],
                    out_grad[place * out_rows : (place + 1) * out_rows],
                    packed[place * SMALL_ROWS : (place + 1) * SMALL_ROWS],
                )
            ],
            axis=0,
        )

    out_half = grad_output.shape[0] // 2
    odd_grads = first_block(odd_qkv, odd_sums, up_total[:, :hidden_half], grad_output[:out_half])
    odd_received = lay.start_outer(odd_grads)
    even_qkv, even_sums = attention_backward(
        gate(qkv, up_odd, odd_grads), logsum, grad_attn, head_width, half_heads, half_heads
    )
    qkv_rows = odd_qkv.shape[0]

    def input_part(first, count):
        here = slice(first, first + count)
        return t_times(odd_qkv[:, here], w_attn[:qkv_rows]) + t_times(
            even_here[:, here], w_attn[qkv_rows:]
        )

    even_here = even_qkv
    far_mine, near_mine = far_tokens - far_other, near_tokens - near_other
    parts_far = [input_part(near_tokens, far_mine)]
    if core == 2:
        parts_far.append(input_part(near_tokens + far_mine, far_other).astype(half))
    even_here, received = lay.start_reduce(parts_far, even_qkv)
    parts_near = [input_part(0, near_mine)]
    if core == 2:
        parts_near.append(input_part(near_mine, near_other).astype(half))
    input_grad = grad_one + lay.finish_reduce(parts_near, received)
    input_grads = lay.from_sequence(
        input_grad.astype(half).reshape(local_seqs, block_tokens, model_width)
    ).astype(wide)
    even_grads = first_block(even_here, even_sums, up_total[:, hidden_half:], grad_output[out_half:])
    even_received = lay.start_outer(even_grads)

    norm_sums = lay.total(
        jnp.stack(
            [
                jnp.sum(grad_hidden * normed_one, axis=0),
                jnp.sum(upward * normed_two, axis=0),
                jnp.sum(grad_one, axis=0),
                jnp.sum(grad_hidden, axis=0),
                jnp.sum(grad_two, axis=0),
                jnp.sum(upward, axis=0),
            ]
        ),
        one_far,
        even_qkv,
    )
    norm_sums = lax.dynamic_slice_in_dim(norm_sums, lay.fsdp_index * shard_width, shard_width, 1)
    down_parts = lay.scatter_core(
        lay.finish_high(gate(down_sums[cut_rows:], odd_grads), down_high)
    )
    up_parts = lay.scatter_core(lay.finish_high(gate(up_sums[cut_rows:], even_qkv), up_high))
    odd_total = lay.finish_outer(odd_grads, odd_received).astype(half)
    odd_high = lay.swap_high(odd_total, 1)
    even_total = lay.finish_outer(even_grads, even_received)
    first_parts = lay.scatter_core(lay.finish_high(even_total, odd_high))
    down_parts = [gate(part, even_grads) for part in down_parts]
    up_parts = [gate(part, even_grads) for part in up_parts]
    second_new = update_matrices(
        lay.core_index, down_parts, [(down_weight, down_weight_moments, False, matrix_rate)]
    )
    second_new = (
        update_matrices(lay.core_index, up_parts, [(up_weight, up_weight_moments, True, matrix_rate)])
        + second_new
    )
    first_new = update_matrices(
        lay.core_index,
        first_parts,
        [(attn_weight, attn_weight_moments, True, matrix_rate), (out_weight, out_weight_moments, False, output_rate)],
    )
    small_shard = sum(part[attn_rows + out_rows :] for part in first_parts)
    vectors = (
        (attn_bias, attn_bias_moments, small_shard[0, : local_heads * bias_width].reshape(local_heads, bias_width)),
        (up_bias, up_bias_moments, small_shard[8, :hidden_part]),
        (norm_gains, norm_gains_moments, norm_sums[0:2]),
        (norm_shifts, norm_shifts_moments, norm_sums[2:6]),
    )
    bias_new, up_bias_new, gains_new, shifts_new = [
        (grad,) + adamw_update(weight, pair, grad, vector_rate, 0.0) for weight, pair, grad in vectors
    ]
    everything = (
        first_new[0],
        bias_new,
        first_new[1],
        second_new[0],
        up_bias_new,
        second_new[1],
        gains_new,
        shifts_new,
    )
    grads, new_weights, new_moments = zip(*everything)
    return (outputs, input_grads) + grads + new_weights + new_moments


def solution(mesh):
    return jax.shard_map(
        per_device,
        mesh=mesh,
        in_specs=(
            P("fsdp", "tensor", None),
            P("fsdp", "tensor", None),
            P("fsdp", "tensor"),
            P("tensor", "fsdp"),
            P("tensor", "fsdp"),
            P("fsdp", "tensor"),
            P(("tensor", "fsdp")),
            P("tensor", "fsdp"),
            P(None, "fsdp"),
            P(None, "fsdp"),
            P(None, "fsdp", "tensor"),
            P(None, "tensor", "fsdp"),
            P(None, "tensor", "fsdp"),
            P(None, "fsdp", "tensor"),
            P(None, ("tensor", "fsdp")),
            P(None, "tensor", "fsdp"),
            P(None, None, "fsdp"),
            P(None, None, "fsdp"),
        ),
        out_specs=(
            P("fsdp", "tensor", None),
            P("fsdp", "tensor", None),
            P("fsdp", "tensor"),
            P("tensor", "fsdp"),
            P("tensor", "fsdp"),
            P("fsdp", "tensor"),
            P(("tensor", "fsdp")),
            P("tensor", "fsdp"),
            P(None, "fsdp"),
            P(None, "fsdp"),
            P("fsdp", "tensor"),
            P("tensor", "fsdp"),
            P("tensor", "fsdp"),
            P("fsdp", "tensor"),
            P(("tensor", "fsdp")),
            P("tensor", "fsdp"),
            P(None, "fsdp"),
            P(None, "fsdp"),
            P(None, "fsdp", "tensor"),
            P(None, "tensor", "fsdp"),
            P(None, "tensor", "fsdp"),
            P(None, "fsdp", "tensor"),
            P(None, ("tensor", "fsdp")),
            P(None, "tensor", "fsdp"),
            P(None, None, "fsdp"),
            P(None, None, "fsdp"),
        ),
        check_vma=False,
    )
```

```python
import functools

import jax
import jax.numpy as jnp
from jax import lax
from jax.experimental import pallas as pl
from jax.experimental.pallas import tpu as pltpu
from jax.sharding import PartitionSpec as P

norm_eps = 1e-05
beta_one = 0.9
beta_two = 0.999
adam_eps = 1e-08
adam_step = 4.0
matrix_rate = 0.01
output_rate = 0.1
vector_rate = 0.1
decay_rate = 0.1
inv_root_two = 0.7071067811865476
inv_root_tau = 0.3989422804014327


def layer_norm(resid, gain_row, shift_row):
    center = resid - jnp.mean(resid, axis=-1, keepdims=True)
    spread = lax.rsqrt(jnp.mean(center * center, axis=-1, keepdims=True) + norm_eps)
    normed = center * spread
    return (normed * gain_row + shift_row, normed, spread)


def norm_back(grad_out, gain_row, normed, spread):
    scaled = grad_out * gain_row
    return spread * (
        scaled
        - jnp.mean(scaled, axis=-1, keepdims=True)
        - normed * jnp.mean(scaled * normed, axis=-1, keepdims=True)
    )


def gelu_value(inner):
    return inner * 0.5 * (1.0 + jax.scipy.special.erf(inner * inv_root_two))


def gelu_slope(inner):
    return (
        0.5 * (1.0 + jax.scipy.special.erf(inner * inv_root_two))
        + inner * jnp.exp(-0.5 * inner * inner) * inv_root_tau
    )


def adamw_update(weight, moments, grad, rate, decay):
    first_moment = beta_one * moments[0] + (1.0 - beta_one) * grad
    second_moment = beta_two * moments[1] + (1.0 - beta_two) * grad * grad
    direction = (
        first_moment
        / (1.0 - beta_one**adam_step)
        / (jnp.sqrt(second_moment / (1.0 - beta_two**adam_step)) + adam_eps)
    )
    return (weight - rate * (direction + decay * weight), jnp.stack([first_moment, second_moment]))


half = jnp.bfloat16
wide = jnp.float32
VMEM_BYTES = 40 * 1024 * 1024


def times(left, right):
    return lax.dot_general(left, right, (((1,), (0,)), ((), ())), preferred_element_type=wide)


def times_t(left, right):
    return lax.dot_general(left, right, (((1,), (1,)), ((), ())), preferred_element_type=wide)


def t_times(left, right):
    return lax.dot_general(left, right, (((0,), (0,)), ((), ())), preferred_element_type=wide)


def whole_block(*shape):
    return pl.BlockSpec(shape, lambda step: (0,) * len(shape))


def sum_shapes(rows, other, width):
    shapes = [jax.ShapeDtypeStruct((rows - other, width), wide)]
    if other:
        shapes.append(jax.ShapeDtypeStruct((other, width), half))
    return shapes, [whole_block(*shape.shape) for shape in shapes]


def write_sums(total, refs):
    mine = refs[0].shape[0]
    refs[0][...] = total[:mine]
    if len(refs) > 1:
        refs[1][...] = total[mine:].astype(half)


def params():
    return pltpu.CompilerParams(
        dimension_semantics=("arbitrary",), vmem_limit_bytes=VMEM_BYTES
    )


def up_kernel(x_ref, up_ref, bias_ref, down_ref, active_ref, slope_ref, *rest):
    sums, total = rest[:-1], rest[-1]
    inner = times_t(x_ref[...], up_ref[...]) + bias_ref[...]
    chance = 0.5 * (1.0 + lax.erf(inner * inv_root_two))
    active = (inner * chance).astype(half)
    active_ref[...] = active
    slope_ref[...] = chance + inner * jnp.exp(-0.5 * inner * inner) * inv_root_tau
    part = times(active, down_ref[...])
    step = pl.program_id(0)

    @pl.when(step == 0)
    def _():
        total[...] = part

    @pl.when(step > 0)
    def _():
        total[...] += part

    @pl.when(step == pl.num_programs(0) - 1)
    def _():
        write_sums(total[...], sums)


def ffn_forward(x, w_upward, b_upward, w_downward, other):
    rows, width = x.shape
    hidden = w_upward.shape[0]
    tile = 256
    shapes, specs = sum_shapes(rows, other, width)
    return pl.pallas_call(
        up_kernel,
        grid=(hidden // tile,),
        in_specs=[
            whole_block(rows, width),
            pl.BlockSpec((tile, width), lambda step: (step, 0)),
            pl.BlockSpec((1, tile), lambda step: (0, step)),
            pl.BlockSpec((tile, width), lambda step: (step, 0)),
        ],
        out_specs=[
            pl.BlockSpec((rows, tile), lambda step: (0, step)),
            pl.BlockSpec((rows, tile), lambda step: (0, step)),
        ]
        + specs,
        out_shape=[
            jax.ShapeDtypeStruct((rows, hidden), half),
            jax.ShapeDtypeStruct((rows, hidden), wide),
        ]
        + shapes,
        scratch_shapes=[pltpu.VMEM((rows, width), wide)],
        compiler_params=params(),
        cost_estimate=pl.CostEstimate(
            flops=4 * rows * width * hidden,
            bytes_accessed=rows * hidden * 6 + hidden * width * 4,
            transcendentals=2 * rows * hidden,
        ),
        name="ffn_forward",
    )(x, w_upward, b_upward, w_downward)


def down_kernel(grad_ref, slope_ref, down_ref, up_ref, inner_ref, bias_ref, *rest):
    sums, total = rest[:-1], rest[-1]
    grad_inner = times_t(grad_ref[...], down_ref[...]) * slope_ref[...]
    bias_ref[...] = jnp.sum(grad_inner, axis=0, keepdims=True)
    grad_inner_b = grad_inner.astype(half)
    inner_ref[...] = grad_inner_b
    part = times(grad_inner_b, up_ref[...])
    step = pl.program_id(0)

    @pl.when(step == 0)
    def _():
        total[...] = part

    @pl.when(step > 0)
    def _():
        total[...] += part

    @pl.when(step == pl.num_programs(0) - 1)
    def _():
        write_sums(total[...], sums)


def ffn_backward(grad, slope, w_downward, w_upward, other):
    rows, width = grad.shape
    hidden = w_upward.shape[0]
    tile = 256
    shapes, specs = sum_shapes(rows, other, width)
    return pl.pallas_call(
        down_kernel,
        grid=(hidden // tile,),
        in_specs=[
            whole_block(rows, width),
            pl.BlockSpec((rows, tile), lambda step: (0, step)),
            pl.BlockSpec((tile, width), lambda step: (step, 0)),
            pl.BlockSpec((tile, width), lambda step: (step, 0)),
        ],
        out_specs=[
            pl.BlockSpec((rows, tile), lambda step: (0, step)),
            pl.BlockSpec((1, tile), lambda step: (0, step)),
        ]
        + specs,
        out_shape=[
            jax.ShapeDtypeStruct((rows, hidden), half),
            jax.ShapeDtypeStruct((1, hidden), wide),
        ]
        + shapes,
        scratch_shapes=[pltpu.VMEM((rows, width), wide)],
        compiler_params=params(),
        cost_estimate=pl.CostEstimate(
            flops=4 * rows * width * hidden,
            bytes_accessed=rows * hidden * 6 + hidden * width * 4,
            transcendentals=0,
        ),
        name="ffn_backward",
    )(grad, slope, w_downward, w_upward)


def attention_kernel(first, chunk, head_width, qkv_ref, out_ref, attn_ref, log_ref, *rest):
    sums, mixed = rest[:-1], rest[-1]
    head = pl.program_id(0)
    scale = head_width ** (-0.5)
    keys = jnp.transpose(qkv_ref[head_width : 2 * head_width, :])
    values = qkv_ref[2 * head_width : 3 * head_width, :]
    count = attn_ref.shape[1]
    for start in range(0, count, chunk):
        here = slice(first + start, first + start + chunk)
        scores = times(keys, qkv_ref[0:head_width, here]) * scale
        top = jnp.max(scores, axis=0, keepdims=True)
        powers = jnp.exp(scores - top)
        norm = jnp.sum(powers, axis=0, keepdims=True)
        weights = (powers * (1.0 / norm)).astype(half)
        log_ref[0, :, start : start + chunk] = top + jnp.log(norm)
        block = times(values, weights).astype(half)
        attn_ref[:, start : start + chunk] = block
        mixed[pl.ds(pl.multiple_of(head * head_width, head_width), head_width), pl.ds(start, chunk)] = block

    @pl.when(head == pl.num_programs(0) - 1)
    def _():
        write_sums(t_times(mixed[...], out_ref[...]), sums)


def attention_forward(qkv, w_output, first, count, other, head_width):
    length = qkv.shape[1]
    heads = qkv.shape[0] // (3 * head_width)
    width = w_output.shape[1]
    chunk = 256 if count % 256 == 0 else 128
    shapes, specs = sum_shapes(count, other, width)
    return pl.pallas_call(
        functools.partial(attention_kernel, first, chunk, head_width),
        grid=(heads,),
        in_specs=[
            pl.BlockSpec((3 * head_width, length), lambda head: (head, 0)),
            whole_block(heads * head_width, width),
        ],
        out_specs=[
            pl.BlockSpec((head_width, count), lambda head: (head, 0)),
            pl.BlockSpec((1, 1, count), lambda head: (head, 0, 0)),
        ]
        + specs,
        out_shape=[
            jax.ShapeDtypeStruct((heads * head_width, count), half),
            jax.ShapeDtypeStruct((heads, 1, count), wide),
        ]
        + shapes,
        scratch_shapes=[pltpu.VMEM((heads * head_width, count), half)],
        compiler_params=params(),
        cost_estimate=pl.CostEstimate(
            flops=16 * heads * count * length * head_width,
            bytes_accessed=qkv.size * 2 + count * width * 6,
            transcendentals=heads * count * length,
        ),
        name="attention_forward",
    )(qkv, w_output)


def attention_back_kernel(chunk, head_width, qkv_ref, log_ref, grad_ref, out_ref, bias_ref):
    scale = head_width ** (-0.5)
    key_rows = qkv_ref[head_width : 2 * head_width, :]
    keys = jnp.transpose(key_rows)
    values = jnp.transpose(qkv_ref[2 * head_width : 3 * head_width, :])
    length = keys.shape[0]
    grad_keys = jnp.zeros((length, head_width), wide)
    grad_values = jnp.zeros((length, head_width), wide)
    query_sum = jnp.zeros((head_width, 1), wide)
    for start in range(0, length, chunk):
        here = slice(start, start + chunk)
        queries = qkv_ref[0:head_width, here]
        grads = grad_ref[:, here]
        scores = times(keys, queries) * scale
        chances = jnp.exp(scores - log_ref[0, :, here])
        grad_scores = times(values, grads)
        mean = jnp.sum(chances * grad_scores, axis=0, keepdims=True)
        logits = (chances * (grad_scores - mean)).astype(half)
        grad_values = grad_values + times(chances.astype(half), jnp.transpose(grads))
        grad_keys = grad_keys + times(logits, jnp.transpose(queries))
        grad_query = times(key_rows, logits) * scale
        out_ref[0:head_width, here] = grad_query.astype(half)
        query_sum = query_sum + jnp.sum(grad_query, axis=1, keepdims=True)
    grad_keys = jnp.transpose(grad_keys) * scale
    grad_values = jnp.transpose(grad_values)
    out_ref[head_width : 2 * head_width, :] = grad_keys.astype(half)
    out_ref[2 * head_width : 3 * head_width, :] = grad_values.astype(half)
    sums = jnp.concatenate(
        [
            query_sum,
            jnp.sum(grad_keys, axis=1, keepdims=True),
            jnp.sum(grad_values, axis=1, keepdims=True),
        ],
        axis=0,
    )
    bias_ref[...] = jnp.broadcast_to(sums, bias_ref.shape)


def attention_backward(qkv, logsum, grad, head_width, first, heads):
    length = qkv.shape[1]
    chunk = 256
    return pl.pallas_call(
        functools.partial(attention_back_kernel, chunk, head_width),
        grid=(heads,),
        in_specs=[
            pl.BlockSpec((3 * head_width, length), lambda head: (head + first, 0)),
            pl.BlockSpec((1, 1, length), lambda head: (head + first, 0, 0)),
            pl.BlockSpec((head_width, length), lambda head: (head + first, 0)),
        ],
        out_specs=[
            pl.BlockSpec((3 * head_width, length), lambda head: (head, 0)),
            pl.BlockSpec((3 * head_width, 128), lambda head: (head, 0)),
        ],
        out_shape=[
            jax.ShapeDtypeStruct((heads * 3 * head_width, length), half),
            jax.ShapeDtypeStruct((heads * 3 * head_width, 128), wide),
        ],
        compiler_params=params(),
        cost_estimate=pl.CostEstimate(
            flops=40 * heads * length * length * head_width,
            bytes_accessed=heads * length * head_width * 15,
            transcendentals=heads * length * length,
        ),
        name="attention_backward",
    )(qkv, logsum, grad)


def update_kernel(plan, core_count, core_ref, *refs):
    parts, refs = refs[:core_count], refs[core_count:]
    inputs, outputs = refs[: 2 * len(plan)], refs[2 * len(plan) :]
    first = 0
    for index, (rows, flip, rate) in enumerate(plan):
        weight_ref, pair_ref = inputs[2 * index : 2 * index + 2]
        grad_ref, new_ref, moments_ref = outputs[3 * index : 3 * index + 3]
        blocks = [part[first : first + rows, :] for part in parts]
        if core_count == 2:
            lead = core_ref[0] == 0
            blocks = [
                jnp.where(lead, blocks[0], blocks[1]),
                jnp.where(lead, blocks[1], blocks[0]),
            ]
        grad = jnp.concatenate(blocks, axis=0)
        if flip:
            grad = jnp.transpose(grad)
        first += rows
        weight = weight_ref[...]
        first_moment = beta_one * pair_ref[0] + (1.0 - beta_one) * grad
        second_moment = beta_two * pair_ref[1] + (1.0 - beta_two) * grad * grad
        direction = (
            first_moment
            / (1.0 - beta_one**adam_step)
            / (jnp.sqrt(second_moment / (1.0 - beta_two**adam_step)) + adam_eps)
        )
        grad_ref[...] = grad
        new_ref[...] = weight - rate * (direction + decay_rate * weight)
        moments_ref[0] = first_moment
        moments_ref[1] = second_moment


def update_matrices(core_index, parts, matrices):
    plan, operands, shapes = [], [], []
    for weight, pair, flip, rate in matrices:
        rows = weight.shape[1 if flip else 0] // len(parts)
        plan.append((rows, flip, rate))
        operands += [weight, pair]
        shapes += [weight.shape, weight.shape, pair.shape]
    used = sum(rows for rows, _, _ in plan)
    results = pl.pallas_call(
        functools.partial(update_kernel, tuple(plan), len(parts)),
        grid=(1,),
        in_specs=[pl.BlockSpec(memory_space=pltpu.SMEM)]
        + [whole_block(used, part.shape[1]) for part in parts]
        + [whole_block(*operand.shape) for operand in operands],
        out_specs=[whole_block(*shape) for shape in shapes],
        out_shape=[jax.ShapeDtypeStruct(shape, wide) for shape in shapes],
        compiler_params=params(),
        cost_estimate=pl.CostEstimate(
            flops=20 * sum(weight.size for weight, _, _, _ in matrices),
            bytes_accessed=32 * sum(weight.size for weight, _, _, _ in matrices),
            transcendentals=0,
        ),
        name="adamw",
    )(jnp.reshape(core_index, (1,)).astype(jnp.int32), *[part[:used] for part in parts], *operands)
    return [tuple(results[3 * index : 3 * index + 3]) for index in range(len(plan))]


def spread(shape, axis, place, width, start, count):
    index = lax.broadcasted_iota(jnp.int32, shape, axis)
    column = lax.broadcasted_iota(jnp.int32, shape, 1 - axis)
    held = (place + index // count) * width + start + index % count
    return jnp.where(column == held, 1.0, 0.0).astype(half)


def head_spread(sizes, core, head):
    high, part_heads, fsdp, shard, bias, hidden = sizes
    start = (core * part_heads + head) * bias
    return spread((fsdp * bias, fsdp * shard), 0, 0, shard, start, bias)


def hidden_spread(sizes, core_count, core):
    high, part_heads, fsdp, shard, bias, hidden = sizes
    share = fsdp // core_count
    return spread((fsdp * shard, share * hidden), 1, core * share, shard, 0, hidden)


def unpack_kernel(sizes, core_count, core_ref, small_ref, attn_ref, up_ref, norm_ref):
    high, part_heads, fsdp, shard, bias, hidden = sizes
    core = core_ref[0]
    small = small_ref[...]
    features = fsdp * bias
    for head in range(part_heads):
        rows = times_t(head_spread(sizes, core, head), small)
        for place in range(high):
            first = (place * part_heads + head) * features
            column = place * SMALL_ROWS + 6
            attn_ref[first : first + features, :] = rows[:, column : column + 1]
    rows = times(small, hidden_spread(sizes, core_count, core))
    count = rows.shape[1]
    for place in range(high):
        row = place * SMALL_ROWS + 7
        up_ref[:, place * count : (place + 1) * count] = rows[row : row + 1, :]
    norm_ref[...] = small[:SMALL_ROWS].astype(wide)


def unpack_small(sizes, core_count, core_index, small):
    high, part_heads, fsdp, shard, bias, hidden = sizes
    shapes = [
        (high * part_heads * fsdp * bias, 1),
        (1, high * (fsdp // core_count) * hidden),
        (SMALL_ROWS, fsdp * shard),
    ]
    return pl.pallas_call(
        functools.partial(unpack_kernel, sizes, core_count),
        grid=(1,),
        in_specs=[pl.BlockSpec(memory_space=pltpu.SMEM), whole_block(*small.shape)],
        out_specs=[whole_block(*shape) for shape in shapes],
        out_shape=[jax.ShapeDtypeStruct(shape, wide) for shape in shapes],
        compiler_params=params(),
        name="unpack_small",
    )(core_index, small)


def pack_kernel(sizes, core_count, core_ref, attn_ref, up_ref, out_ref):
    high, part_heads, fsdp, shard, bias, hidden = sizes
    core = core_ref[0]
    features = fsdp * bias
    count = up_ref.shape[1] // high
    hot = hidden_spread(sizes, core_count, core)
    for place in range(high):
        row = jnp.zeros((SMALL_ROWS, fsdp * shard), wide)
        for head in range(part_heads):
            first = (place * part_heads + head) * features
            sums = attn_ref[first : first + features, 0:SMALL_ROWS].astype(half)
            row = row + t_times(sums, head_spread(sizes, core, head))
        ups = jnp.broadcast_to(up_ref[:, place * count : (place + 1) * count], (SMALL_ROWS, count))
        ups = times_t(ups.astype(half), hot)
        line = lax.broadcasted_iota(jnp.int32, row.shape, 0)
        first = place * SMALL_ROWS
        out_ref[first : first + SMALL_ROWS, :] = jnp.where(line < 8, row, ups)


def pack_small(sizes, core_count, core_index, attn_sums, up_sums):
    high, part_heads, fsdp, shard, bias, hidden = sizes
    shape = (high * SMALL_ROWS, fsdp * shard)
    return pl.pallas_call(
        functools.partial(pack_kernel, sizes, core_count),
        grid=(1,),
        in_specs=[
            pl.BlockSpec(memory_space=pltpu.SMEM),
            whole_block(*attn_sums.shape),
            whole_block(*up_sums.shape),
        ],
        out_specs=whole_block(*shape),
        out_shape=jax.ShapeDtypeStruct(shape, wide),
        compiler_params=params(),
        name="pack_small",
    )(core_index, attn_sums, up_sums)


SMALL_ROWS = 16


def gate(value, *before):
    return lax.optimization_barrier((value,) + before)[0]


AXES = ("fsdp", "tensor")


class Layout:
    def __init__(self, local_heads, local_seqs):
        self.fsdp = lax.axis_size("fsdp")
        self.tensor = lax.axis_size("tensor")
        self.seqs = local_seqs
        self.core = 2 if local_heads % 2 == 0 and self.fsdp % 2 == 0 else 1
        self.outer = self.fsdp // self.core
        self.high = self.core * local_seqs
        self.low = self.tensor // self.high
        self.order = list(range(1, self.high, 2)) + list(range(0, self.high, 2))
        self.fsdp_index = lax.axis_index("fsdp")
        self.outer_index = self.fsdp_index // self.core
        self.core_index = self.fsdp_index % self.core
        self.high_index = lax.axis_index("tensor") // self.low

    def send(self, value, target):
        pairs = []
        for outer in range(self.outer):
            for core in range(self.core):
                for high in range(self.high):
                    for low in range(self.low):
                        o, c, h, l = target(outer, core, high, low)
                        source_id = (outer * self.core + core) * self.tensor + high * self.low + low
                        target_id = (o * self.core + c) * self.tensor + h * self.low + l
                        pairs.append((source_id, target_id))
        return lax.ppermute(value, AXES, pairs)

    def swap_core(self, value):
        return self.send(value, lambda o, c, h, l: (o, 1 - c, h, l))

    def to_low(self, value, step):
        return self.send(value, lambda o, c, h, l: (o, c, h, (l + step) % self.low))

    def to_high(self, value, step):
        return self.send(value, lambda o, c, h, l: (o, c, (h + step) % self.high, l))

    def to_outer(self, value, step):
        return self.send(value, lambda o, c, h, l: ((o + step) % self.outer, c, h, l))

    def to_sequence(self, blocks):
        within = self.high_index % self.seqs
        return [
            self.send(
                lax.dynamic_index_in_dim(blocks, (within + k) % self.seqs, 0, keepdims=False),
                lambda o, c, h, l, k=k: (
                    o,
                    h // self.seqs,
                    c * self.seqs + (h % self.seqs + k) % self.seqs,
                    l,
                ),
            )
            for k in range(self.seqs)
        ]

    def from_sequence(self, pieces):
        within = self.high_index % self.seqs
        back = []
        for k in range(self.seqs):
            back.append(
                self.send(
                    pieces[k],
                    lambda o, c, h, l, k=k: (
                        o,
                        h // self.seqs,
                        c * self.seqs + (h % self.seqs - k) % self.seqs,
                        l,
                    ),
                )
            )
        if self.seqs == 2:
            return jnp.where(within == 0, jnp.stack(back), jnp.stack(back[::-1]))
        stacked = jnp.stack(back)
        order = (jnp.arange(self.seqs) - within) % self.seqs
        return jnp.take(stacked, order, axis=0)

    def share_near(self, own):
        far = [self.to_low(own, -step) for step in range(1, self.low)]
        near = [own]
        if self.core == 2:
            near.append(self.swap_core(own))
        return jnp.concatenate(near, axis=0), far

    def share_far(self, far, *before):
        far = [gate(piece, *before) for piece in far] if before else list(far)
        if self.core == 2:
            far += [self.swap_core(piece) for piece in far]
        return jnp.concatenate(far, axis=0)

    def share(self, own):
        near, far = self.share_near(own)
        return near, self.share_far(far)

    def start_reduce(self, parts, later):
        total = parts[0]
        if self.core == 2:
            total = total + self.swap_core(parts[1]).astype(wide)
        total = total.astype(half)
        total, later = lax.optimization_barrier((total, later))
        count = total.shape[0] // (self.low - 1)
        return later, [
            self.to_low(total[(step - 1) * count : step * count], step)
            for step in range(1, self.low)
        ]

    def finish_reduce(self, parts, received):
        total = parts[0]
        if self.core == 2:
            total = total + self.swap_core(parts[1]).astype(wide)
        for piece in received:
            total = total + piece.astype(wide)
        return total

    def ordered(self, index, parts, axis):
        count = len(parts)
        if count == 1:
            return parts[0]
        if count == 2:
            return jnp.where(
                index == 0,
                jnp.concatenate(parts, axis=axis),
                jnp.concatenate(parts[::-1], axis=axis),
            )
        width = parts[0].shape[axis]
        shape = list(parts[0].shape)
        shape[axis] = width * count
        result = jnp.zeros(shape, parts[0].dtype)
        for step, part in enumerate(parts):
            result = lax.dynamic_update_slice_in_dim(
                result, part, ((index + step) % count) * width, axis
            )
        return result

    def core_rows(self, rows, core):
        count = rows.shape[0] // self.core
        return lax.dynamic_slice_in_dim(rows, core * count, count, 0)

    def pair_weights(self, matrices, extra=None):
        def pack(core):
            rows = [self.core_rows(matrix, core) for matrix in matrices]
            if extra is not None:
                rows.append(extra)
            return jnp.concatenate(rows, axis=0)

        if self.core == 1:
            return pack(0)
        other = self.swap_core(pack(1 - self.core_index))
        return self.ordered(self.core_index, [pack(self.core_index), other], 1)

    def swap_high(self, value, bits):
        return self.send(value, lambda o, c, h, l: (o, c, h ^ bits, l))

    def outer_weights(self, rows):
        return [rows] + [self.to_outer(rows, -step) for step in range(1, self.outer)]

    def rows_of(self, gathered, first, count):
        return jnp.concatenate(
            [
                self.ordered(self.outer_index, [part[first : first + count] for part in parts], 1)
                for parts in gathered
            ],
            axis=0,
        )

    def columns(self, grad, step):
        width = grad.shape[1] // self.outer
        place = (self.outer_index + step) % self.outer
        return lax.dynamic_slice_in_dim(grad, place * width, width, 1)

    def start_outer(self, grad, *before):
        return [
            self.to_outer(gate(self.columns(grad, step).astype(half), *before), step)
            for step in range(1, self.outer)
        ]

    def finish_outer(self, grad, received):
        total = self.columns(grad, 0)
        for part in received:
            total = total + part.astype(wide)
        return total

    def join_high(self, even, received):
        total = even + received.astype(wide)
        if self.high == 2:
            return total, None
        rows = total.shape[0] // 2
        return total[:rows], total[rows:].astype(half)

    def finish_high(self, total, leaving, *before):
        if leaving is None:
            return total
        received = self.swap_high(leaving, 2)
        return gate(total, *before) + received.astype(wide)

    def scatter_core(self, column):
        if self.core == 1:
            return [column]
        width = column.shape[1] // self.core
        mine = lax.dynamic_slice_in_dim(column, self.core_index * width, width, 1)
        other = self.swap_core(
            lax.dynamic_slice_in_dim(column, (1 - self.core_index) * width, width, 1)
        )
        return [mine, other]

    def total(self, value, before_low, before_outer):
        def over(value, count, target):
            bit = 1
            while bit < count:
                value = value + self.send(value, functools.partial(target, bit))
                bit *= 2
            return value

        if self.core == 2:
            value = value + self.swap_core(value)
        value = over(value, self.high, lambda bit, o, c, h, l: (o, c, h ^ bit, l))
        value = gate(value, before_low)
        value = over(value, self.low, lambda bit, o, c, h, l: (o, c, h, l ^ bit))
        value = gate(value, before_outer)
        return over(value, self.outer, lambda bit, o, c, h, l: (o ^ bit, c, h, l))


def pad_columns(rows, width):
    return jnp.pad(rows, [(0, 0)] * (rows.ndim - 1) + [(0, width - rows.shape[-1])])


def per_device(
    layer_input,
    cotangent,
    attn_weight,
    attn_bias,
    out_weight,
    up_weight,
    up_bias,
    down_weight,
    norm_gains,
    norm_shifts,
    attn_weight_moments,
    attn_bias_moments,
    out_weight_moments,
    up_weight_moments,
    up_bias_moments,
    down_weight_moments,
    norm_gains_moments,
    norm_shifts_moments,
):
    local_heads = attn_bias.shape[0]
    local_seqs, block_tokens, model_width = layer_input.shape
    lay = Layout(local_heads, local_seqs)
    fsdp, core, high = lay.fsdp, lay.core, lay.high
    bias_width = attn_bias.shape[1]
    head_width = bias_width * fsdp // 3
    part_heads = local_heads // core
    shard_width = model_width // fsdp
    hidden_part = up_bias.shape[0]
    own_tokens = local_seqs * block_tokens
    near_tokens = core * own_tokens
    far_tokens = near_tokens * (lay.low - 1)
    near_other = near_tokens - near_tokens // core
    far_other = far_tokens - far_tokens // core

    tokens = jnp.concatenate(lay.to_sequence(layer_input), axis=0)
    small = jnp.concatenate(
        [
            norm_gains.astype(half),
            norm_shifts.astype(half),
            pad_columns(attn_bias.astype(half).reshape(1, -1), shard_width),
            pad_columns(up_bias.astype(half).reshape(1, -1), shard_width),
            jnp.zeros((SMALL_ROWS - 8, shard_width), half),
        ],
        axis=0,
    )
    attn_rows = part_heads * 3 * head_width
    out_rows = part_heads * head_width
    hidden_rows = up_weight.shape[1] // core
    first = lay.pair_weights([attn_weight.astype(half).T, out_weight.astype(half)], small)
    up_later, down_later = gate((up_weight, down_weight), first)
    second = lay.pair_weights([up_later.astype(half).T, down_later.astype(half)])

    def spread_first(rows):
        places = {0: rows}
        for bits in (1, 2):
            if bits < high:
                places[bits] = lay.swap_high(rows, bits)
        return places

    first_places = spread_first(first)
    first_outer = {0: lay.outer_weights(first)}
    second_outer = {0: lay.outer_weights(second)}
    if high == 4:
        first_places[3] = lay.swap_high(gate(first_places[2], first_places[1]), 1)
    for place in range(1, high):
        rows = gate(first_places[place], *second_outer[0][1:])
        first_outer[place] = lay.outer_weights(rows)
    gathered = [first_outer[place] for place in lay.order]
    w_attn = lay.rows_of(gathered, 0, attn_rows)
    w_output = lay.rows_of(gathered, attn_rows, out_rows)
    small = lay.rows_of(gathered, attn_rows + out_rows, SMALL_ROWS)
    sizes = (high, part_heads, fsdp, shard_width, bias_width, hidden_part)
    core_index = jnp.reshape(lay.core_index, (1,)).astype(jnp.int32)
    b_attn, b_upward, norm_rows = unpack_small(sizes, core, core_index, small)
    gain_rows = norm_rows[0:2]
    shift_rows = norm_rows[2:6]

    near, far = lay.share(gate(tokens, *first_places.values()) if high == 2 else gate(tokens, first_places[2]))
    tokens_full = jnp.concatenate([near, far], axis=0)
    second_places = spread_first(gate(second, *first_places.values()))

    qkv = (times_t(w_attn, tokens_full) + b_attn).astype(half)
    attn_far, log_far, *parts_far = attention_forward(
        qkv, w_output, near_tokens, far_tokens, far_other, head_width
    )
    for place in range(1, min(high, 3)):
        second_outer[place] = lay.outer_weights(gate(second_places[place], attn_far))
    if high == 4:
        last = gate(second_places[2], second_places[1], attn_far)
        second_places[3] = lay.swap_high(last, 1)
    near_qkv, received = lay.start_reduce(parts_far, qkv)
    attn_near, log_near, *parts_near = attention_forward(
        near_qkv, w_output, 0, near_tokens, near_other, head_width
    )
    logsum = jnp.concatenate([log_near, log_far], axis=2)
    attn_out = lay.finish_reduce(parts_near, received)
    resid_one = attn_out + shift_rows[0] + tokens.astype(wide)
    hidden_one, normed_one, spread_one = layer_norm(resid_one, gain_rows[0], shift_rows[1])
    hidden_near, hidden_far = lay.share(hidden_one.astype(half))
    if high == 4:
        second_outer[3] = lay.outer_weights(gate(second_places[3], hidden_one))
    upward = lay.to_sequence(gate(cotangent, hidden_one, *second_places.values()))
    gathered = [second_outer[place] for place in lay.order]
    w_upward = lay.rows_of(gathered, 0, hidden_rows)
    w_downward = lay.rows_of(gathered, hidden_rows, hidden_rows)
    hidden_far, *upward = lax.optimization_barrier((hidden_far, *upward))
    upward = jnp.concatenate(upward, axis=0).astype(wide)
    active_far, slope_far, *parts_far = ffn_forward(
        hidden_far, w_upward, b_upward, w_downward, far_other
    )
    hidden_near, received = lay.start_reduce(parts_far, hidden_near)
    active_near, slope_near, *parts_near = ffn_forward(
        hidden_near, w_upward, b_upward, w_downward, near_other
    )
    ffn_out = lay.finish_reduce(parts_near, received)
    resid_two = ffn_out + shift_rows[2] + hidden_one
    result, normed_two, spread_two = layer_norm(resid_two, gain_rows[1], shift_rows[3])

    grad_two = norm_back(upward, gain_rows[1], normed_two, spread_two)
    grad_near, grad_far = lay.share_near(grad_two.astype(half))
    output = result.astype(half).reshape(local_seqs, block_tokens, model_width)
    inner_near, up_near, *parts_near = ffn_backward(
        grad_near, slope_near, w_downward, w_upward, near_other
    )
    grad_far = lay.share_far(grad_far, inner_near)
    inner_far, up_far, *parts_far = ffn_backward(
        grad_far, slope_far, w_downward, w_upward, far_other
    )
    later, received = lay.start_reduce(parts_far, (grad_near, grad_far, active_near, active_far))
    grad_near, grad_far, active_near, active_far = later
    grad_down = t_times(active_near, grad_near) + t_times(active_far, grad_far)
    down_received = lay.start_outer(grad_down)
    grad_hidden = grad_two + lay.finish_reduce(parts_near, received)
    outputs = lay.from_sequence(gate(output, grad_down))
    grad_one = norm_back(grad_hidden, gain_rows[0], normed_one, spread_one)
    grad_one_b = grad_one.astype(half)
    one_near, one_far = lay.share(grad_one_b)
    hidden_near, hidden_far = gate((hidden_near, hidden_far), grad_one_b)
    grad_upward = t_times(inner_near, hidden_near) + t_times(inner_far, hidden_far)
    up_received = lay.start_outer(grad_upward, *down_received)
    cut_rows = grad_down.shape[0] // 2
    down_sums = lay.finish_outer(gate(grad_down, grad_upward), down_received)
    down_odd = down_sums[:cut_rows].astype(half)
    down_high = lay.swap_high(down_odd, 1)
    one_full = jnp.concatenate([one_near, one_far], axis=0)
    grad_attn = times_t(w_output, gate(one_full, down_odd)).astype(half)
    half_heads = part_heads * high // 2
    odd_qkv, odd_sums = attention_backward(qkv, logsum, grad_attn, head_width, 0, half_heads)

    up_sums = lay.finish_outer(gate(grad_upward, odd_qkv), up_received)
    up_odd = up_sums[:cut_rows].astype(half)
    up_high = lay.swap_high(up_odd, 1)
    grad_output = times(attn_near, one_near) + times(attn_far, one_far)
    up_total = gate(up_near + up_far, odd_qkv)
    odd_sizes = (high // 2,) + sizes[1:]
    hidden_half = up_total.shape[1] // 2

    def first_block(grad_qkv, sums, ups, out_grad):
        packed = pack_small(odd_sizes, core, core_index, sums, ups)
        grad = times(grad_qkv, tokens_full)
        return jnp.concatenate(
            [
                block
                for place in range(high // 2)
                for block in (
                    grad[place * attn_rows : (place + 1) * attn_rows],
                    out_grad[place * out_rows : (place + 1) * out_rows],
                    packed[place * SMALL_ROWS : (place + 1) * SMALL_ROWS],
                )
            ],
            axis=0,
        )

    out_half = grad_output.shape[0] // 2
    odd_grads = first_block(odd_qkv, odd_sums, up_total[:, :hidden_half], grad_output[:out_half])
    odd_received = lay.start_outer(odd_grads)
    even_qkv, even_sums = attention_backward(
        gate(qkv, up_odd, odd_grads), logsum, grad_attn, head_width, half_heads, half_heads
    )
    qkv_rows = odd_qkv.shape[0]

    def input_part(first, count):
        here = slice(first, first + count)
        return t_times(odd_qkv[:, here], w_attn[:qkv_rows]) + t_times(
            even_here[:, here], w_attn[qkv_rows:]
        )

    even_here = even_qkv
    far_mine, near_mine = far_tokens - far_other, near_tokens - near_other
    parts_far = [input_part(near_tokens, far_mine)]
    if core == 2:
        parts_far.append(input_part(near_tokens + far_mine, far_other).astype(half))
    even_here, received = lay.start_reduce(parts_far, even_qkv)
    parts_near = [input_part(0, near_mine)]
    if core == 2:
        parts_near.append(input_part(near_mine, near_other).astype(half))
    input_grad = grad_one + lay.finish_reduce(parts_near, received)
    input_grads = lay.from_sequence(
        input_grad.astype(half).reshape(local_seqs, block_tokens, model_width)
    ).astype(wide)
    even_grads = first_block(even_here, even_sums, up_total[:, hidden_half:], grad_output[out_half:])
    even_received = lay.start_outer(even_grads)

    norm_sums = lay.total(
        jnp.stack(
            [
                jnp.sum(grad_hidden * normed_one, axis=0),
                jnp.sum(upward * normed_two, axis=0),
                jnp.sum(grad_one, axis=0),
                jnp.sum(grad_hidden, axis=0),
                jnp.sum(grad_two, axis=0),
                jnp.sum(upward, axis=0),
            ]
        ),
        one_far,
        even_qkv,
    )
    norm_sums = lax.dynamic_slice_in_dim(norm_sums, lay.fsdp_index * shard_width, shard_width, 1)
    down_left = lay.join_high(gate(down_sums[cut_rows:], odd_grads), down_high)
    up_left = lay.join_high(gate(up_sums[cut_rows:], even_qkv), up_high)
    odd_total = lay.finish_outer(odd_grads, odd_received).astype(half)
    odd_high = lay.swap_high(odd_total, 1)
    even_total = lay.finish_outer(even_grads, even_received)
    first_left = lay.join_high(even_total, odd_high)
    last = first_left[-1] if high == 4 else even_total
    down_parts = lay.scatter_core(lay.finish_high(*down_left, input_grad, last))
    up_parts = lay.scatter_core(lay.finish_high(*up_left, input_grad, last))
    down_parts = [gate(part, even_grads) for part in down_parts]
    up_parts = [gate(part, even_grads) for part in up_parts]
    second_new = update_matrices(
        lay.core_index, down_parts, [(down_weight, down_weight_moments, False, matrix_rate)]
    )
    second_new = (
        update_matrices(lay.core_index, up_parts, [(up_weight, up_weight_moments, True, matrix_rate)])
        + second_new
    )
    first_parts = lay.scatter_core(
        lay.finish_high(*first_left, second_new[0][1], second_new[1][1])
    )
    first_new = update_matrices(
        lay.core_index,
        first_parts,
        [(attn_weight, attn_weight_moments, True, matrix_rate), (out_weight, out_weight_moments, False, output_rate)],
    )
    small_shard = sum(part[attn_rows + out_rows :] for part in first_parts)
    vectors = (
        (attn_bias, attn_bias_moments, small_shard[0, : local_heads * bias_width].reshape(local_heads, bias_width)),
        (up_bias, up_bias_moments, small_shard[8, :hidden_part]),
        (norm_gains, norm_gains_moments, norm_sums[0:2]),
        (norm_shifts, norm_shifts_moments, norm_sums[2:6]),
    )
    bias_new, up_bias_new, gains_new, shifts_new = [
        (grad,) + adamw_update(weight, pair, grad, vector_rate, 0.0) for weight, pair, grad in vectors
    ]
    everything = (
        first_new[0],
        bias_new,
        first_new[1],
        second_new[0],
        up_bias_new,
        second_new[1],
        gains_new,
        shifts_new,
    )
    grads, new_weights, new_moments = zip(*everything)
    return (outputs, input_grads) + grads + new_weights + new_moments


def solution(mesh):
    return jax.shard_map(
        per_device,
        mesh=mesh,
        in_specs=(
            P("fsdp", "tensor", None),
            P("fsdp", "tensor", None),
            P("fsdp", "tensor"),
            P("tensor", "fsdp"),
            P("tensor", "fsdp"),
            P("fsdp", "tensor"),
            P(("tensor", "fsdp")),
            P("tensor", "fsdp"),
            P(None, "fsdp"),
            P(None, "fsdp"),
            P(None, "fsdp", "tensor"),
            P(None, "tensor", "fsdp"),
            P(None, "tensor", "fsdp"),
            P(None, "fsdp", "tensor"),
            P(None, ("tensor", "fsdp")),
            P(None, "tensor", "fsdp"),
            P(None, None, "fsdp"),
            P(None, None, "fsdp"),
        ),
        out_specs=(
            P("fsdp", "tensor", None),
            P("fsdp", "tensor", None),
            P("fsdp", "tensor"),
            P("tensor", "fsdp"),
            P("tensor", "fsdp"),
            P("fsdp", "tensor"),
            P(("tensor", "fsdp")),
            P("tensor", "fsdp"),
            P(None, "fsdp"),
            P(None, "fsdp"),
            P("fsdp", "tensor"),
            P("tensor", "fsdp"),
            P("tensor", "fsdp"),
            P("fsdp", "tensor"),
            P(("tensor", "fsdp")),
            P("tensor", "fsdp"),
            P(None, "fsdp"),
            P(None, "fsdp"),
            P(None, "fsdp", "tensor"),
            P(None, "tensor", "fsdp"),
            P(None, "tensor", "fsdp"),
            P(None, "fsdp", "tensor"),
            P(None, ("tensor", "fsdp")),
            P(None, "tensor", "fsdp"),
            P(None, None, "fsdp"),
            P(None, None, "fsdp"),
        ),
        check_vma=False,
    )
```

```python
import functools

import jax
import jax.numpy as jnp
from jax import lax
from jax.experimental import pallas as pl
from jax.experimental.pallas import tpu as pltpu
from jax.sharding import PartitionSpec as P

norm_eps = 1e-05
beta_one = 0.9
beta_two = 0.999
adam_eps = 1e-08
adam_step = 4.0
matrix_rate = 0.01
output_rate = 0.1
vector_rate = 0.1
decay_rate = 0.1
inv_root_two = 0.7071067811865476
inv_root_tau = 0.3989422804014327


def layer_norm(resid, gain_row, shift_row):
    center = resid - jnp.mean(resid, axis=-1, keepdims=True)
    spread = lax.rsqrt(jnp.mean(center * center, axis=-1, keepdims=True) + norm_eps)
    normed = center * spread
    return (normed * gain_row + shift_row, normed, spread)


def norm_back(grad_out, gain_row, normed, spread):
    scaled = grad_out * gain_row
    return spread * (
        scaled
        - jnp.mean(scaled, axis=-1, keepdims=True)
        - normed * jnp.mean(scaled * normed, axis=-1, keepdims=True)
    )


def gelu_value(inner):
    return inner * 0.5 * (1.0 + jax.scipy.special.erf(inner * inv_root_two))


def gelu_slope(inner):
    return (
        0.5 * (1.0 + jax.scipy.special.erf(inner * inv_root_two))
        + inner * jnp.exp(-0.5 * inner * inner) * inv_root_tau
    )


def adamw_update(weight, moments, grad, rate, decay):
    first_moment = beta_one * moments[0] + (1.0 - beta_one) * grad
    second_moment = beta_two * moments[1] + (1.0 - beta_two) * grad * grad
    direction = (
        first_moment
        / (1.0 - beta_one**adam_step)
        / (jnp.sqrt(second_moment / (1.0 - beta_two**adam_step)) + adam_eps)
    )
    return (weight - rate * (direction + decay * weight), jnp.stack([first_moment, second_moment]))


half = jnp.bfloat16
wide = jnp.float32
VMEM_BYTES = 40 * 1024 * 1024


def times(left, right):
    return lax.dot_general(left, right, (((1,), (0,)), ((), ())), preferred_element_type=wide)


def times_t(left, right):
    return lax.dot_general(left, right, (((1,), (1,)), ((), ())), preferred_element_type=wide)


def t_times(left, right):
    return lax.dot_general(left, right, (((0,), (0,)), ((), ())), preferred_element_type=wide)


def whole_block(*shape):
    return pl.BlockSpec(shape, lambda step: (0,) * len(shape))


def sum_shapes(rows, other, width):
    shapes = [jax.ShapeDtypeStruct((rows - other, width), wide)]
    if other:
        shapes.append(jax.ShapeDtypeStruct((other, width), half))
    return shapes, [whole_block(*shape.shape) for shape in shapes]


def write_sums(total, refs):
    mine = refs[0].shape[0]
    refs[0][...] = total[:mine]
    if len(refs) > 1:
        refs[1][...] = total[mine:].astype(half)


def params():
    return pltpu.CompilerParams(
        dimension_semantics=("arbitrary",), vmem_limit_bytes=VMEM_BYTES
    )


def up_kernel(x_ref, up_ref, bias_ref, down_ref, active_ref, slope_ref, *rest):
    sums, total = rest[:-1], rest[-1]
    inner = times_t(x_ref[...], up_ref[...]) + bias_ref[...]
    chance = 0.5 * (1.0 + lax.erf(inner * inv_root_two))
    active = (inner * chance).astype(half)
    active_ref[...] = active
    slope_ref[...] = chance + inner * jnp.exp(-0.5 * inner * inner) * inv_root_tau
    part = times(active, down_ref[...])
    step = pl.program_id(0)

    @pl.when(step == 0)
    def _():
        total[...] = part

    @pl.when(step > 0)
    def _():
        total[...] += part

    @pl.when(step == pl.num_programs(0) - 1)
    def _():
        write_sums(total[...], sums)


def ffn_forward(x, w_upward, b_upward, w_downward, other):
    rows, width = x.shape
    hidden = w_upward.shape[0]
    tile = 256
    shapes, specs = sum_shapes(rows, other, width)
    return pl.pallas_call(
        up_kernel,
        grid=(hidden // tile,),
        in_specs=[
            whole_block(rows, width),
            pl.BlockSpec((tile, width), lambda step: (step, 0)),
            pl.BlockSpec((1, tile), lambda step: (0, step)),
            pl.BlockSpec((tile, width), lambda step: (step, 0)),
        ],
        out_specs=[
            pl.BlockSpec((rows, tile), lambda step: (0, step)),
            pl.BlockSpec((rows, tile), lambda step: (0, step)),
        ]
        + specs,
        out_shape=[
            jax.ShapeDtypeStruct((rows, hidden), half),
            jax.ShapeDtypeStruct((rows, hidden), wide),
        ]
        + shapes,
        scratch_shapes=[pltpu.VMEM((rows, width), wide)],
        compiler_params=params(),
        cost_estimate=pl.CostEstimate(
            flops=4 * rows * width * hidden,
            bytes_accessed=rows * hidden * 6 + hidden * width * 4,
            transcendentals=2 * rows * hidden,
        ),
        name="ffn_forward",
    )(x, w_upward, b_upward, w_downward)


def down_kernel(grad_ref, slope_ref, down_ref, up_ref, inner_ref, bias_ref, *rest):
    sums, total = rest[:-1], rest[-1]
    grad_inner = times_t(grad_ref[...], down_ref[...]) * slope_ref[...]
    bias_ref[...] = jnp.sum(grad_inner, axis=0, keepdims=True)
    grad_inner_b = grad_inner.astype(half)
    inner_ref[...] = grad_inner_b
    part = times(grad_inner_b, up_ref[...])
    step = pl.program_id(0)

    @pl.when(step == 0)
    def _():
        total[...] = part

    @pl.when(step > 0)
    def _():
        total[...] += part

    @pl.when(step == pl.num_programs(0) - 1)
    def _():
        write_sums(total[...], sums)


def ffn_backward(grad, slope, w_downward, w_upward, other):
    rows, width = grad.shape
    hidden = w_upward.shape[0]
    tile = 256
    shapes, specs = sum_shapes(rows, other, width)
    return pl.pallas_call(
        down_kernel,
        grid=(hidden // tile,),
        in_specs=[
            whole_block(rows, width),
            pl.BlockSpec((rows, tile), lambda step: (0, step)),
            pl.BlockSpec((tile, width), lambda step: (step, 0)),
            pl.BlockSpec((tile, width), lambda step: (step, 0)),
        ],
        out_specs=[
            pl.BlockSpec((rows, tile), lambda step: (0, step)),
            pl.BlockSpec((1, tile), lambda step: (0, step)),
        ]
        + specs,
        out_shape=[
            jax.ShapeDtypeStruct((rows, hidden), half),
            jax.ShapeDtypeStruct((1, hidden), wide),
        ]
        + shapes,
        scratch_shapes=[pltpu.VMEM((rows, width), wide)],
        compiler_params=params(),
        cost_estimate=pl.CostEstimate(
            flops=4 * rows * width * hidden,
            bytes_accessed=rows * hidden * 6 + hidden * width * 4,
            transcendentals=0,
        ),
        name="ffn_backward",
    )(grad, slope, w_downward, w_upward)


def attention_kernel(first, chunk, head_width, qkv_ref, out_ref, attn_ref, log_ref, *rest):
    sums, mixed = rest[:-1], rest[-1]
    head = pl.program_id(0)
    scale = head_width ** (-0.5)
    keys = jnp.transpose(qkv_ref[head_width : 2 * head_width, :])
    values = qkv_ref[2 * head_width : 3 * head_width, :]
    count = attn_ref.shape[1]
    for start in range(0, count, chunk):
        here = slice(first + start, first + start + chunk)
        scores = times(keys, qkv_ref[0:head_width, here]) * scale
        top = jnp.max(scores, axis=0, keepdims=True)
        powers = jnp.exp(scores - top)
        norm = jnp.sum(powers, axis=0, keepdims=True)
        weights = (powers * (1.0 / norm)).astype(half)
        log_ref[0, :, start : start + chunk] = top + jnp.log(norm)
        block = times(values, weights).astype(half)
        attn_ref[:, start : start + chunk] = block
        mixed[pl.ds(pl.multiple_of(head * head_width, head_width), head_width), pl.ds(start, chunk)] = block

    @pl.when(head == pl.num_programs(0) - 1)
    def _():
        write_sums(t_times(mixed[...], out_ref[...]), sums)


def attention_forward(qkv, w_output, first, count, other, head_width):
    length = qkv.shape[1]
    heads = qkv.shape[0] // (3 * head_width)
    width = w_output.shape[1]
    chunk = 256 if count % 256 == 0 else 128
    shapes, specs = sum_shapes(count, other, width)
    return pl.pallas_call(
        functools.partial(attention_kernel, first, chunk, head_width),
        grid=(heads,),
        in_specs=[
            pl.BlockSpec((3 * head_width, length), lambda head: (head, 0)),
            whole_block(heads * head_width, width),
        ],
        out_specs=[
            pl.BlockSpec((head_width, count), lambda head: (head, 0)),
            pl.BlockSpec((1, 1, count), lambda head: (head, 0, 0)),
        ]
        + specs,
        out_shape=[
            jax.ShapeDtypeStruct((heads * head_width, count), half),
            jax.ShapeDtypeStruct((heads, 1, count), wide),
        ]
        + shapes,
        scratch_shapes=[pltpu.VMEM((heads * head_width, count), half)],
        compiler_params=params(),
        cost_estimate=pl.CostEstimate(
            flops=16 * heads * count * length * head_width,
            bytes_accessed=qkv.size * 2 + count * width * 6,
            transcendentals=heads * count * length,
        ),
        name="attention_forward",
    )(qkv, w_output)


def attention_back_kernel(chunk, head_width, qkv_ref, log_ref, grad_ref, out_ref, bias_ref):
    scale = head_width ** (-0.5)
    key_rows = qkv_ref[head_width : 2 * head_width, :]
    keys = jnp.transpose(key_rows)
    values = jnp.transpose(qkv_ref[2 * head_width : 3 * head_width, :])
    length = keys.shape[0]
    grad_keys = jnp.zeros((length, head_width), wide)
    grad_values = jnp.zeros((length, head_width), wide)
    query_sum = jnp.zeros((head_width, 1), wide)
    for start in range(0, length, chunk):
        here = slice(start, start + chunk)
        queries = qkv_ref[0:head_width, here]
        grads = grad_ref[:, here]
        scores = times(keys, queries) * scale
        chances = jnp.exp(scores - log_ref[0, :, here])
        grad_scores = times(values, grads)
        mean = jnp.sum(chances * grad_scores, axis=0, keepdims=True)
        logits = (chances * (grad_scores - mean)).astype(half)
        grad_values = grad_values + times(chances.astype(half), jnp.transpose(grads))
        grad_keys = grad_keys + times(logits, jnp.transpose(queries))
        grad_query = times(key_rows, logits) * scale
        out_ref[0:head_width, here] = grad_query.astype(half)
        query_sum = query_sum + jnp.sum(grad_query, axis=1, keepdims=True)
    grad_keys = jnp.transpose(grad_keys) * scale
    grad_values = jnp.transpose(grad_values)
    out_ref[head_width : 2 * head_width, :] = grad_keys.astype(half)
    out_ref[2 * head_width : 3 * head_width, :] = grad_values.astype(half)
    sums = jnp.concatenate(
        [
            query_sum,
            jnp.sum(grad_keys, axis=1, keepdims=True),
            jnp.sum(grad_values, axis=1, keepdims=True),
        ],
        axis=0,
    )
    bias_ref[...] = jnp.broadcast_to(sums, bias_ref.shape)


def attention_backward(qkv, logsum, grad, head_width, first, heads):
    length = qkv.shape[1]
    chunk = 256
    return pl.pallas_call(
        functools.partial(attention_back_kernel, chunk, head_width),
        grid=(heads,),
        in_specs=[
            pl.BlockSpec((3 * head_width, length), lambda head: (head + first, 0)),
            pl.BlockSpec((1, 1, length), lambda head: (head + first, 0, 0)),
            pl.BlockSpec((head_width, length), lambda head: (head + first, 0)),
        ],
        out_specs=[
            pl.BlockSpec((3 * head_width, length), lambda head: (head, 0)),
            pl.BlockSpec((3 * head_width, 128), lambda head: (head, 0)),
        ],
        out_shape=[
            jax.ShapeDtypeStruct((heads * 3 * head_width, length), half),
            jax.ShapeDtypeStruct((heads * 3 * head_width, 128), wide),
        ],
        compiler_params=params(),
        cost_estimate=pl.CostEstimate(
            flops=40 * heads * length * length * head_width,
            bytes_accessed=heads * length * head_width * 15,
            transcendentals=heads * length * length,
        ),
        name="attention_backward",
    )(qkv, logsum, grad)


def update_kernel(plan, core_count, core_ref, *refs):
    parts, refs = refs[:core_count], refs[core_count:]
    inputs, outputs = refs[: 2 * len(plan)], refs[2 * len(plan) :]
    first = 0
    for index, (rows, flip, rate) in enumerate(plan):
        weight_ref, pair_ref = inputs[2 * index : 2 * index + 2]
        grad_ref, new_ref, moments_ref = outputs[3 * index : 3 * index + 3]
        blocks = [part[first : first + rows, :] for part in parts]
        if core_count == 2:
            lead = core_ref[0] == 0
            blocks = [
                jnp.where(lead, blocks[0], blocks[1]),
                jnp.where(lead, blocks[1], blocks[0]),
            ]
        grad = jnp.concatenate(blocks, axis=0)
        if flip:
            grad = jnp.transpose(grad)
        first += rows
        weight = weight_ref[...]
        first_moment = beta_one * pair_ref[0] + (1.0 - beta_one) * grad
        second_moment = beta_two * pair_ref[1] + (1.0 - beta_two) * grad * grad
        direction = (
            first_moment
            / (1.0 - beta_one**adam_step)
            / (jnp.sqrt(second_moment / (1.0 - beta_two**adam_step)) + adam_eps)
        )
        grad_ref[...] = grad
        new_ref[...] = weight - rate * (direction + decay_rate * weight)
        moments_ref[0] = first_moment
        moments_ref[1] = second_moment


def update_matrices(core_index, parts, matrices):
    plan, operands, shapes = [], [], []
    for weight, pair, flip, rate in matrices:
        rows = weight.shape[1 if flip else 0] // len(parts)
        plan.append((rows, flip, rate))
        operands += [weight, pair]
        shapes += [weight.shape, weight.shape, pair.shape]
    used = sum(rows for rows, _, _ in plan)
    results = pl.pallas_call(
        functools.partial(update_kernel, tuple(plan), len(parts)),
        grid=(1,),
        in_specs=[pl.BlockSpec(memory_space=pltpu.SMEM)]
        + [whole_block(used, part.shape[1]) for part in parts]
        + [whole_block(*operand.shape) for operand in operands],
        out_specs=[whole_block(*shape) for shape in shapes],
        out_shape=[jax.ShapeDtypeStruct(shape, wide) for shape in shapes],
        compiler_params=params(),
        cost_estimate=pl.CostEstimate(
            flops=20 * sum(weight.size for weight, _, _, _ in matrices),
            bytes_accessed=32 * sum(weight.size for weight, _, _, _ in matrices),
            transcendentals=0,
        ),
        name="adamw",
    )(jnp.reshape(core_index, (1,)).astype(jnp.int32), *[part[:used] for part in parts], *operands)
    return [tuple(results[3 * index : 3 * index + 3]) for index in range(len(plan))]


def spread(shape, axis, place, width, start, count):
    index = lax.broadcasted_iota(jnp.int32, shape, axis)
    column = lax.broadcasted_iota(jnp.int32, shape, 1 - axis)
    held = (place + index // count) * width + start + index % count
    return jnp.where(column == held, 1.0, 0.0).astype(half)


def head_spread(sizes, core, head):
    high, part_heads, fsdp, shard, bias, hidden = sizes
    start = (core * part_heads + head) * bias
    return spread((fsdp * bias, fsdp * shard), 0, 0, shard, start, bias)


def hidden_spread(sizes, core_count, core):
    high, part_heads, fsdp, shard, bias, hidden = sizes
    share = fsdp // core_count
    return spread((fsdp * shard, share * hidden), 1, core * share, shard, 0, hidden)


def unpack_kernel(sizes, core_count, core_ref, small_ref, attn_ref, up_ref, norm_ref):
    high, part_heads, fsdp, shard, bias, hidden = sizes
    core = core_ref[0]
    small = small_ref[...]
    features = fsdp * bias
    for head in range(part_heads):
        rows = times_t(head_spread(sizes, core, head), small)
        for place in range(high):
            first = (place * part_heads + head) * features
            column = place * SMALL_ROWS + 6
            attn_ref[first : first + features, :] = rows[:, column : column + 1]
    rows = times(small, hidden_spread(sizes, core_count, core))
    count = rows.shape[1]
    for place in range(high):
        row = place * SMALL_ROWS + 7
        up_ref[:, place * count : (place + 1) * count] = rows[row : row + 1, :]
    norm_ref[...] = small[:SMALL_ROWS].astype(wide)


def unpack_small(sizes, core_count, core_index, small):
    high, part_heads, fsdp, shard, bias, hidden = sizes
    shapes = [
        (high * part_heads * fsdp * bias, 1),
        (1, high * (fsdp // core_count) * hidden),
        (SMALL_ROWS, fsdp * shard),
    ]
    return pl.pallas_call(
        functools.partial(unpack_kernel, sizes, core_count),
        grid=(1,),
        in_specs=[pl.BlockSpec(memory_space=pltpu.SMEM), whole_block(*small.shape)],
        out_specs=[whole_block(*shape) for shape in shapes],
        out_shape=[jax.ShapeDtypeStruct(shape, wide) for shape in shapes],
        compiler_params=params(),
        name="unpack_small",
    )(core_index, small)


def pack_kernel(sizes, core_count, core_ref, attn_ref, up_ref, out_ref):
    high, part_heads, fsdp, shard, bias, hidden = sizes
    core = core_ref[0]
    features = fsdp * bias
    count = up_ref.shape[1] // high
    hot = hidden_spread(sizes, core_count, core)
    for place in range(high):
        row = jnp.zeros((SMALL_ROWS, fsdp * shard), wide)
        for head in range(part_heads):
            first = (place * part_heads + head) * features
            sums = attn_ref[first : first + features, 0:SMALL_ROWS].astype(half)
            row = row + t_times(sums, head_spread(sizes, core, head))
        ups = jnp.broadcast_to(up_ref[:, place * count : (place + 1) * count], (SMALL_ROWS, count))
        ups = times_t(ups.astype(half), hot)
        line = lax.broadcasted_iota(jnp.int32, row.shape, 0)
        first = place * SMALL_ROWS
        out_ref[first : first + SMALL_ROWS, :] = jnp.where(line < 8, row, ups)


def pack_small(sizes, core_count, core_index, attn_sums, up_sums):
    high, part_heads, fsdp, shard, bias, hidden = sizes
    shape = (high * SMALL_ROWS, fsdp * shard)
    return pl.pallas_call(
        functools.partial(pack_kernel, sizes, core_count),
        grid=(1,),
        in_specs=[
            pl.BlockSpec(memory_space=pltpu.SMEM),
            whole_block(*attn_sums.shape),
            whole_block(*up_sums.shape),
        ],
        out_specs=whole_block(*shape),
        out_shape=jax.ShapeDtypeStruct(shape, wide),
        compiler_params=params(),
        name="pack_small",
    )(core_index, attn_sums, up_sums)


SMALL_ROWS = 16


def gate(value, *before):
    return lax.optimization_barrier((value,) + before)[0]


AXES = ("fsdp", "tensor")


class Layout:
    def __init__(self, local_heads, local_seqs):
        self.fsdp = lax.axis_size("fsdp")
        self.tensor = lax.axis_size("tensor")
        self.seqs = local_seqs
        self.core = 2 if local_heads % 2 == 0 and self.fsdp % 2 == 0 else 1
        self.outer = self.fsdp // self.core
        self.high = self.core * local_seqs
        self.low = self.tensor // self.high
        self.order = list(range(1, self.high, 2)) + list(range(0, self.high, 2))
        self.fsdp_index = lax.axis_index("fsdp")
        self.outer_index = self.fsdp_index // self.core
        self.core_index = self.fsdp_index % self.core
        self.high_index = lax.axis_index("tensor") // self.low

    def send(self, value, target):
        pairs = []
        for outer in range(self.outer):
            for core in range(self.core):
                for high in range(self.high):
                    for low in range(self.low):
                        o, c, h, l = target(outer, core, high, low)
                        source_id = (outer * self.core + core) * self.tensor + high * self.low + low
                        target_id = (o * self.core + c) * self.tensor + h * self.low + l
                        pairs.append((source_id, target_id))
        return lax.ppermute(value, AXES, pairs)

    def swap_core(self, value):
        return self.send(value, lambda o, c, h, l: (o, 1 - c, h, l))

    def to_low(self, value, step):
        return self.send(value, lambda o, c, h, l: (o, c, h, (l + step) % self.low))

    def to_high(self, value, step):
        return self.send(value, lambda o, c, h, l: (o, c, (h + step) % self.high, l))

    def to_outer(self, value, step):
        return self.send(value, lambda o, c, h, l: ((o + step) % self.outer, c, h, l))

    def to_sequence(self, blocks):
        within = self.high_index % self.seqs
        return [
            self.send(
                lax.dynamic_index_in_dim(blocks, (within + k) % self.seqs, 0, keepdims=False),
                lambda o, c, h, l, k=k: (
                    o,
                    h // self.seqs,
                    c * self.seqs + (h % self.seqs + k) % self.seqs,
                    l,
                ),
            )
            for k in range(self.seqs)
        ]

    def from_sequence(self, pieces):
        within = self.high_index % self.seqs
        back = []
        for k in range(self.seqs):
            back.append(
                self.send(
                    pieces[k],
                    lambda o, c, h, l, k=k: (
                        o,
                        h // self.seqs,
                        c * self.seqs + (h % self.seqs - k) % self.seqs,
                        l,
                    ),
                )
            )
        if self.seqs == 2:
            return jnp.where(within == 0, jnp.stack(back), jnp.stack(back[::-1]))
        stacked = jnp.stack(back)
        order = (jnp.arange(self.seqs) - within) % self.seqs
        return jnp.take(stacked, order, axis=0)

    def share_near(self, own):
        far = [self.to_low(own, -step) for step in range(1, self.low)]
        near = [own]
        if self.core == 2:
            near.append(self.swap_core(own))
        return jnp.concatenate(near, axis=0), far

    def share_far(self, far, *before):
        far = [gate(piece, *before) for piece in far] if before else list(far)
        if self.core == 2:
            far += [self.swap_core(piece) for piece in far]
        return jnp.concatenate(far, axis=0)

    def share(self, own):
        near, far = self.share_near(own)
        return near, self.share_far(far)

    def start_reduce(self, parts, later):
        total = parts[0]
        if self.core == 2:
            total = total + self.swap_core(parts[1]).astype(wide)
        total = total.astype(half)
        total, later = lax.optimization_barrier((total, later))
        count = total.shape[0] // (self.low - 1)
        return later, [
            self.to_low(total[(step - 1) * count : step * count], step)
            for step in range(1, self.low)
        ]

    def finish_reduce(self, parts, received):
        total = parts[0]
        if self.core == 2:
            total = total + self.swap_core(parts[1]).astype(wide)
        for piece in received:
            total = total + piece.astype(wide)
        return total

    def ordered(self, index, parts, axis):
        count = len(parts)
        if count == 1:
            return parts[0]
        if count == 2:
            return jnp.where(
                index == 0,
                jnp.concatenate(parts, axis=axis),
                jnp.concatenate(parts[::-1], axis=axis),
            )
        width = parts[0].shape[axis]
        shape = list(parts[0].shape)
        shape[axis] = width * count
        result = jnp.zeros(shape, parts[0].dtype)
        for step, part in enumerate(parts):
            result = lax.dynamic_update_slice_in_dim(
                result, part, ((index + step) % count) * width, axis
            )
        return result

    def core_rows(self, rows, core):
        count = rows.shape[0] // self.core
        return lax.dynamic_slice_in_dim(rows, core * count, count, 0)

    def pair_weights(self, matrices, extra=None):
        def pack(core):
            rows = [self.core_rows(matrix, core) for matrix in matrices]
            if extra is not None:
                rows.append(extra)
            return jnp.concatenate(rows, axis=0)

        if self.core == 1:
            return pack(0)
        other = self.swap_core(pack(1 - self.core_index))
        return self.ordered(self.core_index, [pack(self.core_index), other], 1)

    def swap_high(self, value, bits):
        return self.send(value, lambda o, c, h, l: (o, c, h ^ bits, l))

    def outer_weights(self, rows):
        return [rows] + [self.to_outer(rows, -step) for step in range(1, self.outer)]

    def rows_of(self, gathered, first, count):
        return jnp.concatenate(
            [
                self.ordered(self.outer_index, [part[first : first + count] for part in parts], 1)
                for parts in gathered
            ],
            axis=0,
        )

    def columns(self, grad, step):
        width = grad.shape[1] // self.outer
        place = (self.outer_index + step) % self.outer
        return lax.dynamic_slice_in_dim(grad, place * width, width, 1)

    def start_outer(self, grad, *before):
        return [
            self.to_outer(gate(self.columns(grad, step).astype(half), *before), step)
            for step in range(1, self.outer)
        ]

    def finish_outer(self, grad, received):
        total = self.columns(grad, 0)
        for part in received:
            total = total + part.astype(wide)
        return total

    def join_high(self, even, received):
        total = even + received.astype(wide)
        if self.high == 2:
            return total, None
        rows = total.shape[0] // 2
        return total[:rows], total[rows:].astype(half)

    def finish_high(self, total, leaving, *before):
        if leaving is None:
            return total
        received = self.swap_high(leaving, 2)
        return gate(total, *before) + received.astype(wide)

    def scatter_core(self, column):
        if self.core == 1:
            return [column]
        width = column.shape[1] // self.core
        mine = lax.dynamic_slice_in_dim(column, self.core_index * width, width, 1)
        other = self.swap_core(
            lax.dynamic_slice_in_dim(column, (1 - self.core_index) * width, width, 1)
        )
        return [mine, other]

    def total(self, value, before_low, before_outer):
        def over(value, count, target):
            bit = 1
            while bit < count:
                value = value + self.send(value, functools.partial(target, bit))
                bit *= 2
            return value

        if self.core == 2:
            value = value + self.swap_core(value)
        value = over(value, self.high, lambda bit, o, c, h, l: (o, c, h ^ bit, l))
        value = gate(value, before_low)
        value = over(value, self.low, lambda bit, o, c, h, l: (o, c, h, l ^ bit))
        value = gate(value, before_outer)
        return over(value, self.outer, lambda bit, o, c, h, l: (o ^ bit, c, h, l))


def pad_columns(rows, width):
    return jnp.pad(rows, [(0, 0)] * (rows.ndim - 1) + [(0, width - rows.shape[-1])])


def per_device(
    layer_input,
    cotangent,
    attn_weight,
    attn_bias,
    out_weight,
    up_weight,
    up_bias,
    down_weight,
    norm_gains,
    norm_shifts,
    attn_weight_moments,
    attn_bias_moments,
    out_weight_moments,
    up_weight_moments,
    up_bias_moments,
    down_weight_moments,
    norm_gains_moments,
    norm_shifts_moments,
):
    local_heads = attn_bias.shape[0]
    local_seqs, block_tokens, model_width = layer_input.shape
    lay = Layout(local_heads, local_seqs)
    fsdp, core, high = lay.fsdp, lay.core, lay.high
    bias_width = attn_bias.shape[1]
    head_width = bias_width * fsdp // 3
    part_heads = local_heads // core
    shard_width = model_width // fsdp
    hidden_part = up_bias.shape[0]
    own_tokens = local_seqs * block_tokens
    near_tokens = core * own_tokens
    far_tokens = near_tokens * (lay.low - 1)
    near_other = near_tokens - near_tokens // core
    far_other = far_tokens - far_tokens // core

    tokens = jnp.concatenate(lay.to_sequence(layer_input), axis=0)
    small = jnp.concatenate(
        [
            norm_gains,
            norm_shifts,
            pad_columns(attn_bias.reshape(1, -1), shard_width),
            pad_columns(up_bias.reshape(1, -1), shard_width),
            jnp.zeros((SMALL_ROWS - 8, shard_width), wide),
        ],
        axis=0,
    ).astype(half)
    attn_rows = part_heads * 3 * head_width
    out_rows = part_heads * head_width
    hidden_rows = up_weight.shape[1] // core
    first = lay.pair_weights([attn_weight.astype(half).T, out_weight.astype(half)], small)
    up_later, down_later = gate((up_weight, down_weight), first)
    second = lay.pair_weights([up_later.astype(half).T, down_later.astype(half)])

    def spread_first(rows):
        places = {0: rows}
        for bits in (1, 2):
            if bits < high:
                places[bits] = lay.swap_high(rows, bits)
        return places

    first_places = spread_first(first)
    first_outer = {0: lay.outer_weights(first)}
    second_outer = {0: lay.outer_weights(second)}
    if high == 4:
        first_places[3] = lay.swap_high(gate(first_places[2], first_places[1]), 1)
    for place in range(1, high):
        rows = gate(first_places[place], *second_outer[0][1:])
        first_outer[place] = lay.outer_weights(rows)
    gathered = [first_outer[place] for place in lay.order]
    w_attn = lay.rows_of(gathered, 0, attn_rows)
    w_output = lay.rows_of(gathered, attn_rows, out_rows)
    small = lay.rows_of(gathered, attn_rows + out_rows, SMALL_ROWS)
    sizes = (high, part_heads, fsdp, shard_width, bias_width, hidden_part)
    core_index = jnp.reshape(lay.core_index, (1,)).astype(jnp.int32)
    b_attn, b_upward, norm_rows = unpack_small(sizes, core, core_index, small)
    gain_rows = norm_rows[0:2]
    shift_rows = norm_rows[2:6]

    near, far = lay.share(gate(tokens, *first_places.values()) if high == 2 else gate(tokens, first_places[2]))
    tokens_full = jnp.concatenate([near, far], axis=0)
    second_places = spread_first(gate(second, *first_places.values()))

    qkv = (times_t(w_attn, tokens_full) + b_attn).astype(half)
    attn_far, log_far, *parts_far = attention_forward(
        qkv, w_output, near_tokens, far_tokens, far_other, head_width
    )
    for place in range(1, min(high, 3)):
        second_outer[place] = lay.outer_weights(gate(second_places[place], attn_far))
    if high == 4:
        last = gate(second_places[2], second_places[1], qkv)
        second_places[3] = lay.swap_high(last, 1)
    near_qkv, received = lay.start_reduce(parts_far, qkv)
    attn_near, log_near, *parts_near = attention_forward(
        near_qkv, w_output, 0, near_tokens, near_other, head_width
    )
    logsum = jnp.concatenate([log_near, log_far], axis=2)
    attn_out = lay.finish_reduce(parts_near, received)
    resid_one = attn_out + shift_rows[0] + tokens.astype(wide)
    hidden_one, normed_one, spread_one = layer_norm(resid_one, gain_rows[0], shift_rows[1])
    hidden_near, hidden_far = lay.share(hidden_one.astype(half))
    if high == 4:
        second_outer[3] = lay.outer_weights(gate(second_places[3], hidden_one))
    upward = lay.to_sequence(gate(cotangent, hidden_one, *second_places.values()))
    gathered = [second_outer[place] for place in lay.order]
    w_upward = lay.rows_of(gathered, 0, hidden_rows)
    w_downward = lay.rows_of(gathered, hidden_rows, hidden_rows)
    hidden_far, *upward = lax.optimization_barrier((hidden_far, *upward))
    upward = jnp.concatenate(upward, axis=0).astype(wide)
    active_far, slope_far, *parts_far = ffn_forward(
        hidden_far, w_upward, b_upward, w_downward, far_other
    )
    hidden_near, received = lay.start_reduce(parts_far, hidden_near)
    active_near, slope_near, *parts_near = ffn_forward(
        hidden_near, w_upward, b_upward, w_downward, near_other
    )
    ffn_out = lay.finish_reduce(parts_near, received)
    resid_two = ffn_out + shift_rows[2] + hidden_one
    result, normed_two, spread_two = layer_norm(resid_two, gain_rows[1], shift_rows[3])

    grad_two = norm_back(upward, gain_rows[1], normed_two, spread_two)
    grad_near, grad_far = lay.share_near(grad_two.astype(half))
    output = result.astype(half).reshape(local_seqs, block_tokens, model_width)
    inner_near, up_near, *parts_near = ffn_backward(
        grad_near, slope_near, w_downward, w_upward, near_other
    )
    grad_far = lay.share_far(grad_far, inner_near)
    inner_far, up_far, *parts_far = ffn_backward(
        grad_far, slope_far, w_downward, w_upward, far_other
    )
    later, received = lay.start_reduce(parts_far, (grad_near, grad_far, active_near, active_far))
    grad_near, grad_far, active_near, active_far = later
    grad_down = t_times(active_near, grad_near) + t_times(active_far, grad_far)
    down_received = lay.start_outer(grad_down)
    grad_hidden = grad_two + lay.finish_reduce(parts_near, received)
    outputs = lay.from_sequence(gate(output, grad_down))
    grad_one = norm_back(grad_hidden, gain_rows[0], normed_one, spread_one)
    grad_one_b = grad_one.astype(half)
    one_near, one_far = lay.share(grad_one_b)
    hidden_near, hidden_far = gate((hidden_near, hidden_far), grad_one_b)
    grad_upward = t_times(inner_near, hidden_near) + t_times(inner_far, hidden_far)
    up_received = lay.start_outer(grad_upward, *down_received)
    cut_rows = grad_down.shape[0] // 2
    down_sums = lay.finish_outer(gate(grad_down, grad_upward), down_received)
    down_odd = down_sums[:cut_rows].astype(half)
    down_high = lay.swap_high(down_odd, 1)
    one_full = jnp.concatenate([one_near, one_far], axis=0)
    grad_attn = times_t(w_output, gate(one_full, down_odd)).astype(half)
    half_heads = part_heads * high // 2
    odd_qkv, odd_sums = attention_backward(qkv, logsum, grad_attn, head_width, 0, half_heads)

    up_sums = lay.finish_outer(gate(grad_upward, odd_qkv), up_received)
    up_odd = up_sums[:cut_rows].astype(half)
    up_high = lay.swap_high(up_odd, 1)
    grad_output = times(attn_near, one_near) + times(attn_far, one_far)
    up_total = gate(up_near + up_far, odd_qkv)
    odd_sizes = (high // 2,) + sizes[1:]
    hidden_half = up_total.shape[1] // 2

    def first_block(grad_qkv, sums, ups, out_grad):
        packed = pack_small(odd_sizes, core, core_index, sums, ups)
        grad = times(grad_qkv, tokens_full)
        return jnp.concatenate(
            [
                block
                for place in range(high // 2)
                for block in (
                    grad[place * attn_rows : (place + 1) * attn_rows],
                    out_grad[place * out_rows : (place + 1) * out_rows],
                    packed[place * SMALL_ROWS : (place + 1) * SMALL_ROWS],
                )
            ],
            axis=0,
        )

    out_half = grad_output.shape[0] // 2
    odd_grads = first_block(odd_qkv, odd_sums, up_total[:, :hidden_half], grad_output[:out_half])
    odd_received = lay.start_outer(odd_grads)
    even_qkv, even_sums = attention_backward(
        gate(qkv, up_odd, odd_grads), logsum, grad_attn, head_width, half_heads, half_heads
    )
    qkv_rows = odd_qkv.shape[0]

    def input_part(first, count):
        here = slice(first, first + count)
        return t_times(odd_qkv[:, here], w_attn[:qkv_rows]) + t_times(
            even_here[:, here], w_attn[qkv_rows:]
        )

    even_here = even_qkv
    far_mine, near_mine = far_tokens - far_other, near_tokens - near_other
    parts_far = [input_part(near_tokens, far_mine)]
    if core == 2:
        parts_far.append(input_part(near_tokens + far_mine, far_other).astype(half))
    even_here, received = lay.start_reduce(parts_far, even_qkv)
    parts_near = [input_part(0, near_mine)]
    if core == 2:
        parts_near.append(input_part(near_mine, near_other).astype(half))
    input_grad = grad_one + lay.finish_reduce(parts_near, received)
    input_grads = lay.from_sequence(
        input_grad.astype(half).reshape(local_seqs, block_tokens, model_width)
    ).astype(wide)
    even_grads = first_block(even_here, even_sums, up_total[:, hidden_half:], grad_output[out_half:])
    even_received = lay.start_outer(even_grads)

    norm_sums = lay.total(
        jnp.stack(
            [
                jnp.sum(grad_hidden * normed_one, axis=0),
                jnp.sum(upward * normed_two, axis=0),
                jnp.sum(grad_one, axis=0),
                jnp.sum(grad_hidden, axis=0),
                jnp.sum(grad_two, axis=0),
                jnp.sum(upward, axis=0),
            ]
        ),
        one_far,
        even_qkv,
    )
    norm_sums = lax.dynamic_slice_in_dim(norm_sums, lay.fsdp_index * shard_width, shard_width, 1)
    down_left = lay.join_high(gate(down_sums[cut_rows:], odd_grads), down_high)
    up_left = lay.join_high(gate(up_sums[cut_rows:], even_qkv), up_high)
    odd_total = lay.finish_outer(odd_grads, odd_received).astype(half)
    odd_high = lay.swap_high(odd_total, 1)
    even_total = lay.finish_outer(even_grads, even_received)
    first_left = lay.join_high(even_total, odd_high)
    last = first_left[-1] if high == 4 else even_total
    down_parts = lay.scatter_core(lay.finish_high(*down_left, input_grad, last))
    up_parts = lay.scatter_core(lay.finish_high(*up_left, input_grad, last))
    down_parts = [gate(part, even_grads) for part in down_parts]
    up_parts = [gate(part, even_grads) for part in up_parts]
    second_new = update_matrices(
        lay.core_index, down_parts, [(down_weight, down_weight_moments, False, matrix_rate)]
    )
    second_new = (
        update_matrices(lay.core_index, up_parts, [(up_weight, up_weight_moments, True, matrix_rate)])
        + second_new
    )
    first_parts = lay.scatter_core(
        lay.finish_high(*first_left, second_new[0][1], second_new[1][1])
    )
    first_new = update_matrices(
        lay.core_index,
        first_parts,
        [(attn_weight, attn_weight_moments, True, matrix_rate), (out_weight, out_weight_moments, False, output_rate)],
    )
    small_shard = sum(part[attn_rows + out_rows :] for part in first_parts)
    vectors = (
        (attn_bias, attn_bias_moments, small_shard[0, : local_heads * bias_width].reshape(local_heads, bias_width)),
        (up_bias, up_bias_moments, small_shard[8, :hidden_part]),
        (norm_gains, norm_gains_moments, norm_sums[0:2]),
        (norm_shifts, norm_shifts_moments, norm_sums[2:6]),
    )
    bias_new, up_bias_new, gains_new, shifts_new = [
        (grad,) + adamw_update(weight, pair, grad, vector_rate, 0.0) for weight, pair, grad in vectors
    ]
    everything = (
        first_new[0],
        bias_new,
        first_new[1],
        second_new[0],
        up_bias_new,
        second_new[1],
        gains_new,
        shifts_new,
    )
    grads, new_weights, new_moments = zip(*everything)
    return (outputs, input_grads) + grads + new_weights + new_moments


def solution(mesh):
    return jax.shard_map(
        per_device,
        mesh=mesh,
        in_specs=(
            P("fsdp", "tensor", None),
            P("fsdp", "tensor", None),
            P("fsdp", "tensor"),
            P("tensor", "fsdp"),
            P("tensor", "fsdp"),
            P("fsdp", "tensor"),
            P(("tensor", "fsdp")),
            P("tensor", "fsdp"),
            P(None, "fsdp"),
            P(None, "fsdp"),
            P(None, "fsdp", "tensor"),
            P(None, "tensor", "fsdp"),
            P(None, "tensor", "fsdp"),
            P(None, "fsdp", "tensor"),
            P(None, ("tensor", "fsdp")),
            P(None, "tensor", "fsdp"),
            P(None, None, "fsdp"),
            P(None, None, "fsdp"),
        ),
        out_specs=(
            P("fsdp", "tensor", None),
            P("fsdp", "tensor", None),
            P("fsdp", "tensor"),
            P("tensor", "fsdp"),
            P("tensor", "fsdp"),
            P("fsdp", "tensor"),
            P(("tensor", "fsdp")),
            P("tensor", "fsdp"),
            P(None, "fsdp"),
            P(None, "fsdp"),
            P("fsdp", "tensor"),
            P("tensor", "fsdp"),
            P("tensor", "fsdp"),
            P("fsdp", "tensor"),
            P(("tensor", "fsdp")),
            P("tensor", "fsdp"),
            P(None, "fsdp"),
            P(None, "fsdp"),
            P(None, "fsdp", "tensor"),
            P(None, "tensor", "fsdp"),
            P(None, "tensor", "fsdp"),
            P(None, "fsdp", "tensor"),
            P(None, ("tensor", "fsdp")),
            P(None, "tensor", "fsdp"),
            P(None, None, "fsdp"),
            P(None, None, "fsdp"),
        ),
        check_vma=False,
    )
```
